32 devices in a mesh: region: 2 (over x), ty: 16 (over z, y, core).
Axes of the slice: x: 2, y: 2, z: 4, core: 2. Of those that a mesh axis runs over, the one named last changes fastest.
Arguments:
- mask_init: float32 [32, 512, 512], P(('region', 'ty')), parts along dimension 0, may hold values from -1.6 to 1.6
- dual_init: float32 [32, 512, 512], P(('region', 'ty')), parts along dimension 0, may hold values from -1.5 to 1.5
- target: bfloat16 [32, 512, 512], P(('region', 'ty')), parts along dimension 0, may hold values from 0 to 1, as said below
- kernels: float32 [8, 2, 1024], replicated, may hold values from -9 to 9
- weights: float32 [8], replicated, may hold values from 0.1 to 1
Outputs:
- mask_final: float32 [32, 512, 512], P(('region', 'ty')), parts along dimension 0
- dual_final: float32 [32, 512, 512], P(('region', 'ty')), parts along dimension 0
The draws below stay inside these ranges and needn't reach their ends.
There are 2 independent parts, one for each index of `region`. The reference program is written for one: setup_inputs(seed, part) draws one part's arguments, and reference() takes and returns one part's arrays. A program takes and returns all parts, laid end to end along the dimension named above; an argument that names none is the same for every part. Nothing has to cross between parts.
Inputs may be any that keep to these rules, and one draw needn't show every extreme that they name: `target`: each entry is 0 or 1; wherever two tiles cover the same canvas position they hold the same value.
All inputs are finite; a program needn't handle non-finite values.
Results may differ from the reference program's by a relative error of at most 0.0045.
Values sent between devices are 32-bit elements; how exact they have to be, the bound alone decides.
A program may use at most 128 MiB of HBM per device.

```python
import math
import jax
import jax.numpy as jnp
from jax import lax

N = 512
INTERSECTION = 128
F = 32
KERNELS = 8
GRID_COLS = 4
ITERS = 2
TILES = 16


def smooth_field(coarse):
    spacing = 2 * N // F
    pixels = jnp.arange(N, dtype=jnp.int32)
    cell_index = pixels // spacing
    fraction = (pixels % spacing).astype(jnp.float32) / spacing
    top_rows = coarse[:, cell_index, :]
    low_rows = coarse[:, cell_index + 1, :]
    rowwise = top_rows * (1.0 - fraction)[None, :, None] + low_rows * fraction[None, :, None]
    west_cols = rowwise[:, :, cell_index]
    east_cols = rowwise[:, :, cell_index + 1]
    return west_cols * (1.0 - fraction)[None, None, :] + east_cols * fraction[None, None, :]


def draw_mask_init(key, part):
    spacing = 2 * N // F
    points = N // spacing + 1
    coarse_key, rough_key = jax.random.split(jax.random.fold_in(key, 11))
    coarse = jnp.clip(0.22 * jax.random.normal(coarse_key, (TILES, points, points), jnp.float32), -0.75, 0.75)
    rough = jax.random.uniform(rough_key, (TILES, N, N), jnp.float32, -0.8, 0.8)
    return smooth_field(coarse) + rough


def draw_kernels(key, part):
    kernel_key = jax.random.fold_in(key, 23)
    return jnp.clip(3.0 * jax.random.normal(kernel_key, (KERNELS, 2, F * F), jnp.float32), -9.0, 9.0)


def draw_target(key, part):
    stride = N - INTERSECTION
    grid_height = TILES // GRID_COLS * stride + INTERSECTION
    grid_width = GRID_COLS * stride + INTERSECTION
    block_side = N // 8
    blocks_high = (grid_height + block_side - 1) // block_side
    blocks_wide = (grid_width + block_side - 1) // block_side
    kind_key, phase_key, bits_key = jax.random.split(jax.random.fold_in(key, 37), 3)
    block_kinds = jax.random.randint(kind_key, (blocks_high, blocks_wide), 0, 4)
    block_phase = jax.random.randint(phase_key, (blocks_high, blocks_wide), 0, 2)
    random_bits = jax.random.randint(bits_key, (grid_height, grid_width), 0, 2)
    canvas_rows = jnp.arange(grid_height, dtype=jnp.int32)
    canvas_cols = jnp.arange(grid_width, dtype=jnp.int32)
    kind_pixels = block_kinds[canvas_rows // block_side][:, canvas_cols // block_side]
    phase_pixels = block_phase[canvas_rows // block_side][:, canvas_cols // block_side]
    vertical = (canvas_cols[None, :] + phase_pixels) % 2
    horizontal = (canvas_rows[:, None] + phase_pixels) % 2
    canvas = jnp.where(kind_pixels == 0, random_bits, jnp.where(kind_pixels == 3, horizontal, vertical))
    tile_ids = jnp.arange(TILES, dtype=jnp.int32)
    row_start = tile_ids // GRID_COLS * stride
    col_start = tile_ids % GRID_COLS * stride
    pixels = jnp.arange(N, dtype=jnp.int32)
    rows_index = row_start[:, None, None] + pixels[None, :, None]
    cols_index = col_start[:, None, None] + pixels[None, None, :]
    return canvas[rows_index, cols_index].astype(jnp.bfloat16)


def shard_levels(stream_key, extent, pieces, least, top_value):
    factor_of = 1.0
    for axis_at, shards_of in pieces:
        heights = jax.random.uniform(jax.random.fold_in(jax.random.fold_in(stream_key, 6), axis_at), (shards_of,), jnp.float32, least / len(pieces), top_value / len(pieces))
        factor_of = factor_of * jnp.repeat(jnp.exp(heights), extent[axis_at] // shards_of).reshape((-1,) + (1,) * (len(extent) - 1 - axis_at))
    return factor_of


def gaussian(rng, extent, deviation, limit, cuts=(), held_as=jnp.bfloat16):
    array = jax.random.normal(rng, extent, jnp.float32) * deviation
    if len(cuts) > 0:
        array = shard_levels(rng, extent, cuts, -0.22, 0.18) * array
    return jnp.clip(array, min=-limit, max=limit).astype(held_as)


def setup_inputs(seed: int = 0, part: int = 0) -> dict:
    splits = jax.random.split(jax.random.key(seed), 6)
    part_keys = jax.random.split(jax.random.fold_in(splits[5], part), 6)
    return {
        "mask_init": draw_mask_init(jax.random.fold_in(jax.random.fold_in(splits[5], part), 71), part),
        "dual_init": gaussian(part_keys[1], (TILES, N, N), 0.3, 1.5, ((0, 16),), jnp.float32),
        "target": draw_target(jax.random.fold_in(jax.random.fold_in(splits[5], part), 71), part),
        "kernels": draw_kernels(jax.random.fold_in(splits[5], 71), part),
        "weights": jnp.clip(jnp.exp(jax.random.uniform(splits[4], (KERNELS,), jnp.float32, math.log(0.1), math.log(1.0))), 0.1, 1.0),
    }


SHARPNESS = 8.0
THRESHOLD = 0.3
STEP_SIZE = 0.25
PENALTY = 1.0
PRECISE = lax.Precision.HIGHEST


def tables():
    pixels = jnp.arange(N, dtype=jnp.int32)
    frequencies = jnp.arange(F, dtype=jnp.int32) - F // 2
    phases = (frequencies[:, None] * pixels[None, :]) % N
    angles = phases.astype(jnp.float32) * (2.0 * math.pi / N)
    return jnp.cos(angles), -jnp.sin(angles)


def exact_dot(left_side, right_side, contract):
    return lax.dot_general(left_side, right_side, (contract, ((), ())), precision=PRECISE, preferred_element_type=jnp.float32)


def plain_dot(left_side, right_side, contract):
    return lax.dot_general(left_side, right_side, (contract, ((), ())), preferred_element_type=jnp.float32)


def kernel_field(kernel, spectrum_real, spectrum_imag, cos_table, sin_table, rows_low):
    kernel_real = kernel[0].reshape(F, F)
    kernel_imag = kernel[1].reshape(F, F)
    gated_real = kernel_real * spectrum_real - kernel_imag * spectrum_imag
    gated_imag = kernel_real * spectrum_imag + kernel_imag * spectrum_real
    band_real = exact_dot(gated_real, cos_table, ((1,), (0,))) + exact_dot(gated_imag, sin_table, ((1,), (0,)))
    band_imag = exact_dot(gated_imag, cos_table, ((1,), (0,))) - exact_dot(gated_real, sin_table, ((1,), (0,)))
    upper = jnp.concatenate([band_real, band_imag], axis=1)
    lower = jnp.concatenate([band_imag, -band_real], axis=1)
    stacked = jnp.concatenate([upper, lower], axis=0).astype(jnp.bfloat16)
    field = plain_dot(rows_low, stacked, ((0,), (0,))) / (N * N)
    return field[:, :N], field[:, N:]


def mask_gradient(mask, target, kernels, weights):
    cos_table, sin_table = tables()
    rows_exact = jnp.concatenate([cos_table, sin_table], axis=0)
    rows_low = rows_exact.astype(jnp.bfloat16)
    cos_low = cos_table.astype(jnp.bfloat16)
    sin_low = sin_table.astype(jnp.bfloat16)
    partial_band = plain_dot(rows_low, mask.astype(jnp.bfloat16), ((1,), (1,)))
    part_real = partial_band[:F]
    part_imag = partial_band[F:]
    spectrum_real = exact_dot(cos_table, part_real, ((1,), (1,))) - exact_dot(sin_table, part_imag, ((1,), (1,)))
    spectrum_imag = exact_dot(cos_table, part_imag, ((1,), (1,))) + exact_dot(sin_table, part_real, ((1,), (1,)))
    weight_total = jnp.sum(weights)

    def forward(summed, item):
        kernel, weight = item
        field_real, field_imag = kernel_field(kernel, spectrum_real, spectrum_imag, cos_table, sin_table, rows_low)
        return summed + weight * (field_real * field_real + field_imag * field_imag), None

    summed, unused = lax.scan(forward, jnp.zeros((N, N), jnp.float32), (kernels, weights))
    intensity = summed / weight_total
    resist = jax.nn.sigmoid(SHARPNESS * (intensity - THRESHOLD))
    slope = 2.0 * (resist - target.astype(jnp.float32)) * SHARPNESS * resist * (1.0 - resist)
    back_table = jnp.concatenate([jnp.concatenate([cos_low, -sin_low], axis=1), jnp.concatenate([sin_low, cos_low], axis=1)], axis=0)

    def backward(carry, item):
        adjoint_real, adjoint_imag = carry
        kernel, weight = item
        field_real, field_imag = kernel_field(kernel, spectrum_real, spectrum_imag, cos_table, sin_table, rows_low)
        weighted = jnp.concatenate([slope * field_real, slope * field_imag], axis=1).astype(jnp.bfloat16)
        turned = plain_dot(back_table, weighted, ((1,), (1,)))
        turned_real = turned[:F]
        turned_imag = turned[F:]
        back_real = exact_dot(cos_table, turned_real, ((1,), (1,))) - exact_dot(sin_table, turned_imag, ((1,), (1,)))
        back_imag = exact_dot(cos_table, turned_imag, ((1,), (1,))) + exact_dot(sin_table, turned_real, ((1,), (1,)))
        kernel_real = kernel[0].reshape(F, F)
        kernel_imag = kernel[1].reshape(F, F)
        portion = weight / weight_total
        new_real = adjoint_real + portion * (kernel_real * back_real + kernel_imag * back_imag)
        new_imag = adjoint_imag + portion * (kernel_real * back_imag - kernel_imag * back_real)
        return (new_real, new_imag), None

    zero_block = jnp.zeros((F, F), jnp.float32)
    adjoints, unused = lax.scan(backward, (zero_block, zero_block), (kernels, weights))
    adjoint_real, adjoint_imag = adjoints
    tail_real = exact_dot(adjoint_real, cos_table, ((1,), (0,))) + exact_dot(adjoint_imag, sin_table, ((1,), (0,)))
    tail_imag = exact_dot(adjoint_imag, cos_table, ((1,), (0,))) - exact_dot(adjoint_real, sin_table, ((1,), (0,)))
    tails = jnp.concatenate([tail_real, tail_imag], axis=0)
    return exact_dot(rows_exact, tails, ((0,), (0,))) * (2.0 / (N * N))


def consensus(shared):
    stride = N - INTERSECTION
    grid_height = (TILES // GRID_COLS) * stride + INTERSECTION
    grid_width = GRID_COLS * stride + INTERSECTION
    canvas = jnp.zeros((grid_height, grid_width), jnp.float32)
    coverage = jnp.zeros((grid_height, grid_width), jnp.float32)
    ones_block = jnp.ones((N, N), jnp.float32)

    def corner_of(tile_index):
        tile_index = tile_index.astype(jnp.int32)
        top_pixel = ((tile_index // GRID_COLS) * stride).astype(jnp.int32)
        left_pixel = ((tile_index % GRID_COLS) * stride).astype(jnp.int32)
        return tile_index, top_pixel, left_pixel

    def place(tile_index, carry):
        canvas, coverage = carry
        tile_index, top_pixel, left_pixel = corner_of(tile_index)
        piece = lax.dynamic_index_in_dim(shared, tile_index, 0, keepdims=False)
        block = lax.dynamic_slice(canvas, (top_pixel, left_pixel), (N, N)) + piece
        canvas = lax.dynamic_update_slice(canvas, block, (top_pixel, left_pixel))
        counted = lax.dynamic_slice(coverage, (top_pixel, left_pixel), (N, N)) + ones_block
        coverage = lax.dynamic_update_slice(coverage, counted, (top_pixel, left_pixel))
        return canvas, coverage

    canvas, coverage = lax.fori_loop(0, TILES, place, (canvas, coverage))

    def take(tile_index):
        tile_index, top_pixel, left_pixel = corner_of(tile_index)
        summed = lax.dynamic_slice(canvas, (top_pixel, left_pixel), (N, N))
        counted = lax.dynamic_slice(coverage, (top_pixel, left_pixel), (N, N))
        return summed / counted

    return lax.map(take, jnp.arange(TILES, dtype=jnp.int32))


def reference(mask_init, dual_init, target, kernels, weights):
    mask = mask_init
    dual = dual_init
    for iteration in range(ITERS):
        agreed = consensus(mask + dual)
        dual = dual + mask - agreed
        gradient = lax.map(lambda item: mask_gradient(item[0], item[1], kernels, weights), (mask, target))
        mask = mask - STEP_SIZE * (gradient + PENALTY * (mask - agreed + dual))
    return mask, dual
```

```python
import functools

import jax
import jax.numpy as jnp
import numpy as np
from jax import lax
from jax.experimental import pallas as pl
from jax.experimental.pallas import tpu as pltpu
from jax.sharding import PartitionSpec as P

GRID_COLS = 4
INTERSECTION = 128
SHARPNESS = 8.0
THRESHOLD = 0.3
STEP_SIZE = 0.25
PENALTY = 1.0
MESH = pl.DeviceIdType.MESH
BF16 = jnp.bfloat16


def split_host(table):
    table = table.astype(np.float32)
    high = table.astype(BF16)
    low = (table - high.astype(np.float32)).astype(BF16)
    return high, low


def host_tables(n, f):
    g = 2 * f
    freq = np.arange(f) - f // 2
    phase = 2.0 * np.pi * ((freq[:, None] * np.arange(n)[None, :]) % n) / n
    cos, sin = np.cos(phase), -np.sin(phase)
    rows = np.concatenate([cos, sin], 0)
    rows_hi, rows_lo = split_host(rows)
    row_side = np.concatenate([rows_hi, rows_lo], 0)
    col_wide = np.concatenate([np.tile(cos.T, (1, 4)), np.tile(sin.T, (1, 4))], 1)
    col_side = split_host(col_wide)[0]
    coarse = 2.0 * np.pi * ((np.arange(g)[:, None] * freq[None, :]) % g) / g
    er, ei = np.cos(coarse), np.sin(coarse)
    pair = np.eye(2)
    to_real = np.kron(pair, np.concatenate([er.T, -ei.T], 0))
    to_imag = np.kron(pair, np.concatenate([ei.T, er.T], 0))
    lane_turn = np.concatenate([to_real, to_imag], 1)
    lane_fwd = np.concatenate(split_host(lane_turn / (n * n)), 1)
    lane_back = np.concatenate(split_host(lane_turn.T), 1)
    row_turn = np.concatenate([np.concatenate([er, -ei], 1), np.concatenate([ei, er], 1)], 0)
    turn_hi, turn_lo = split_host(row_turn)
    row_fwd = np.concatenate([turn_hi, turn_lo, turn_hi, turn_lo], 1)
    row_back = np.concatenate(split_host(row_turn.T), 0)
    half = np.arange(-(f - 1), f)
    angle = np.arange(n)[:, None] * f * 2 - np.arange(g)[None, :] * n
    spread = np.cos(2.0 * np.pi * ((angle[..., None] * half) % (n * g)) / (n * g)).sum(-1) / g
    s_hi, s_lo = split_host(spread)
    up_cols = np.concatenate([s_hi.T, s_lo.T, s_hi.T, s_lo.T], 0)
    down_cols = np.concatenate([s_hi, s_hi, s_lo, s_lo], 1)
    scale = 2.0 / (n * n)
    c_hi, c_lo = split_host(cos * scale)
    t_hi, t_lo = split_host(sin * scale)
    tail_r = np.concatenate([c_hi, c_lo, t_hi, t_lo], 0)
    tail_i = np.concatenate([-t_hi, -t_lo, c_hi, c_lo], 0)
    tail = np.concatenate([tail_r, tail_i], 1)
    tail_tab = np.concatenate([tail, tail], 0)
    grad_rows = np.concatenate([rows_hi.T, rows_lo.T, rows_hi.T, rows_lo.T], 1)
    turn = np.zeros((f, f))
    turn[np.arange(1, f), f - np.arange(1, f)] = 1.0
    row_flip = np.concatenate([turn, turn], 1)
    none = np.zeros((f, f))
    one_flip = np.concatenate(
        [np.concatenate([turn, turn, none, none], 1), np.zeros((f, 4 * f)),
         np.concatenate([none, none, -turn, -turn], 1), np.zeros((f, 4 * f))], 0,
    )
    lane_flip = np.concatenate([one_flip, one_flip], 0)
    tables = (
        row_side, col_side, lane_fwd, row_fwd, up_cols, down_cols, row_back, lane_back,
        row_flip, lane_flip, tail_tab, grad_rows,
    )
    return [np.asarray(t, dtype=BF16) for t in tables]


def dot(a, b):
    return lax.dot_general(a, b, (((1,), (0,)), ((), ())), preferred_element_type=jnp.float32)


def split(x):
    high = x.astype(BF16)
    return high, (x - high.astype(jnp.float32)).astype(BF16)


def stacked(x):
    high, low = split(x)
    return jnp.concatenate([high, high, low, low], axis=0)


INPUTS = 17
ORDER = (1, 0, 5, 6, 4, 3, 7, 8, 9, 2, 10, 11, 12, 13, 14, 15, 16)


def body(n, f, edge, count, *refs):
    ins, refs = refs[:INPUTS], refs[INPUTS:]
    mask_out, dual_out = refs[:2]
    refs = refs[2:]
    held, refs = refs[: INPUTS - 2], refs[INPUTS - 2 :]
    target_ref, k_ref, w_ref = held[:3]
    (
        row_side, col_side, lane_fwd, row_fwd, up_cols, down_cols, row_back, lane_back,
        row_flip, lane_flip, tail_tab, grad_rows,
    ) = held[3:]
    (
        md, h_sc, load_sem, hr, vr, q, c1, c2, c3, c4, c5, mb, xb, yb, slope, spec, spec_in, adj, adj_in,
        send_sem, recv_sem,
    ) = refs
    places = [md.at[0], md.at[1], *held]
    sources = [ins[0].at[0], ins[1].at[0], *ins[2:]]
    loads = [pltpu.make_async_copy(src, dst, load_sem.at[i]) for i, (src, dst) in enumerate(zip(sources, places))]
    far = n - edge
    half = edge // 2
    g = 2 * f
    me = lax.axis_index("ty")
    row, col = me // GRID_COLS, me % GRID_COLS
    grid_rows = count // GRID_COLS
    left, right = col > 0, col < GRID_COLS - 1
    upper, lower = row > 0, row < grid_rows - 1
    both = jnp.logical_and
    near = [
        (-1, left), (1, right), (-GRID_COLS, upper), (GRID_COLS, lower),
        (-GRID_COLS - 1, both(upper, left)), (-GRID_COLS + 1, both(upper, right)),
        (GRID_COLS - 1, both(lower, left)), (GRID_COLS + 1, both(lower, right)),
    ]
    opposite = [1, 0, 3, 2, 7, 6, 5, 4]
    beside, above = (left, right), (upper, lower)
    lone_h, lone_v = [jnp.logical_not(x) for x in beside], [jnp.logical_not(x) for x in above]

    barrier = pltpu.get_barrier_semaphore()
    for shift, there in near:
        @pl.when(there)
        def _(shift=shift):
            pl.semaphore_signal(barrier, inc=1, device_id={"ty": me + shift}, device_id_type=MESH)

    for i in ORDER:
        loads[i].start()

    counter = [0]

    def remote(src, dst, to, send_if, recv_if):
        index = counter[0]
        counter[0] += 1
        copy = pltpu.make_async_remote_copy(
            src_ref=src, dst_ref=dst, send_sem=send_sem.at[index], recv_sem=recv_sem.at[index],
            device_id={"ty": me + near[to][0]}, device_id_type=MESH,
        )
        return copy, send_if, recv_if

    def start(entries):
        for entry in entries:
            pl.when(entry[1])(entry[0].start)

    def arrived(entries):
        for entry in entries:
            pl.when(entry[2])(entry[0].wait_recv)

    def sent(entries):
        for entry in entries:
            pl.when(entry[1])(entry[0].wait_send)

    begin = (0, far)
    bands = (pl.ds(0, edge), pl.ds(far, edge))
    middle = pl.ds(edge, far - edge)
    corners = [(v, h) for v in range(2) for h in range(2)]

    def piece(v, part):
        return pl.ds(begin[v] + part * half, half)

    raw = (ins[0].at[0], ins[1].at[0])
    plan = {}
    for i in range(2):
        plan["v", i] = [
            remote(raw[i].at[bands[v], middle], vr.at[i, 1 - v], 2 + v, above[v], above[1 - v]) for v in range(2)
        ]
        plan["h", i] = [
            remote(raw[i].at[middle, bands[h]], hr.at[i, 1 - h], h, beside[h], beside[1 - h]) for h in range(2)
        ]
    plan["hc"] = [
        remote(
            md.at[:, bands[v], bands[h]], q.at[:, v, 1 - h], h,
            both(beside[h], lone_v[v]), both(beside[1 - h], lone_v[v]),
        )
        for v, h in corners
    ]
    plan["vc"] = [
        remote(
            md.at[:, bands[v], bands[h]], q.at[:, 1 - v, h], 2 + v,
            both(above[v], lone_h[h]), both(above[1 - v], lone_h[h]),
        )
        for v, h in corners
    ]
    plan["c1"] = [
        remote(
            md.at[:, piece(v, h), bands[h]], c1.at[:, v, 1 - h], h,
            both(beside[h], above[v]), both(beside[1 - h], above[v]),
        )
        for v, h in corners
    ]
    plan["c3"] = [
        remote(
            c2.at[:, v, h], c3.at[:, 1 - v, h], 2 + v, both(beside[h], above[v]), both(beside[h], above[1 - v])
        )
        for v, h in corners
    ]
    plan["c5"] = [
        remote(
            c4.at[:, v, h], c5.at[:, v, 1 - h], h, both(beside[h], above[v]), both(beside[1 - h], above[v])
        )
        for v, h in corners
    ]
    plan["spec"] = [
        remote(spec.at[to], spec_in.at[opposite[to]], to, near[to][1], near[opposite[to]][1]) for to in range(8)
    ]
    plan["adj"] = [remote(adj, adj_in.at[opposite[to]], to, near[to][1], near[opposite[to]][1]) for to in range(8)]

    for to in range(8):
        @pl.when(jnp.logical_not(near[to][1]))
        def _(to=to):
            spec_in[to] = jnp.zeros((f, 4 * f), jnp.float32)
            adj_in[to] = jnp.zeros((f, 4 * f), jnp.float32)

    expected = sum(there.astype(jnp.int32) for _, there in near)
    pl.semaphore_wait(barrier, expected)
    start(plan["v", 1] + plan["h", 1])

    waited = set()

    def need(*which):
        for i in which:
            if i not in waited:
                waited.add(i)
                loads[i].wait()

    need(0, 1)
    start(plan["c1"] + plan["vc"] + plan["hc"])

    up_f, down_f = upper.astype(jnp.float32), lower.astype(jnp.float32)
    left_f, right_f = left.astype(jnp.float32), right.astype(jnp.float32)
    at_col = lax.broadcasted_iota(jnp.int32, (1, n), 1)
    share_col = jnp.where(at_col < edge, 1.0 - 0.5 * left_f, jnp.where(at_col >= far, 1.0 - 0.5 * right_f, 1.0))
    share_side = (1.0 - 0.5 * left_f, 1.0 - 0.5 * right_f)
    share_end = (1.0 - 0.5 * up_f, 1.0 - 0.5 * down_f)

    def share_row(r):
        return share_end[0] if r == 0 else share_end[1] if r == far else None

    def scaled(x, by):
        return x if by is None else x * by

    lane = lax.broadcasted_iota(jnp.int32, (1, 4 * f), 1)
    low_half = lane < 2 * f

    for r in range(0, n, edge):
        rows = slice(r, r + edge)
        m, d = md[0, rows, :], md[1, rows, :]
        y = (m + d) * scaled(0.5 * share_col, share_row(r))
        mb[rows, :] = m.astype(BF16)
        yb[rows, :] = y.astype(BF16)
        xb[rows, :] = (0.5 * m - 0.25 * d + y).astype(BF16)

    need(5, 6)
    top_part = dot(row_side[:g, far:], yb[:edge, :]).astype(BF16)
    end_part = dot(row_side[:g, :edge], yb[far:, :]).astype(BF16)
    left_part = dot(row_side[:g, :], yb[:, :edge]).astype(BF16)
    right_part = dot(row_side[:g, :], yb[:, far:]).astype(BF16)

    def to_band(grid):
        real = grid[:f, : 4 * f] - grid[f:, 4 * f :]
        imag = grid[:f, 4 * f :] + grid[f:, : 4 * f]
        return real, imag

    def packed_band(grid):
        real, imag = to_band(grid)
        return jnp.where(low_half, real, imag)

    at_left = dot(
        jnp.concatenate([left_part, top_part[:, :edge], end_part[:, :edge]], axis=0), col_side[far:, :]
    )
    at_right = dot(
        jnp.concatenate([right_part, top_part[:, far:], end_part[:, far:]], axis=0), col_side[:edge, :]
    )
    at_ends = dot(jnp.concatenate([top_part, end_part], axis=0), col_side[...])
    for i, to in enumerate((0, 4, 6)):
        spec[to] = packed_band(at_left[i * g : (i + 1) * g])
    for i, to in enumerate((1, 5, 7)):
        spec[to] = packed_band(at_right[i * g : (i + 1) * g])
    for i, to in enumerate((2, 3)):
        spec[to] = packed_band(at_ends[i * g : (i + 1) * g])
    start(plan["spec"])

    part = dot(row_side[...], jnp.concatenate([mb[...], xb[...]], axis=1))
    part = part[:g] + part[g:]
    first_part, next_part = part[:, :n], part[:, n:]
    grid = dot(jnp.concatenate([*split(first_part), next_part.astype(BF16)], axis=0), col_side[...])
    band_one = to_band(grid[:g] + grid[g : 2 * g])
    band_next = packed_band(grid[2 * g :])

    arrived(plan["c1"])
    for v, h in corners:
        @pl.when(both(beside[h], above[v]))
        def _(v=v, h=h):
            c2[:, v, h] = md[:, piece(v, 1 - h), bands[h]] + c1[:, v, h]
    start(plan["c3"] + plan["v", 0] + plan["h", 0])

    need(4, 3)
    quarters = w_ref.shape[0] // 2
    total = w_ref[0]
    for k in range(1, w_ref.shape[0]):
        total = total + w_ref[k]
    portions = [
        jnp.where(low_half, w_ref[2 * k], w_ref[2 * k + 1]) / jnp.full((1, 4 * f), total, jnp.float32)
        for k in range(quarters)
    ]
    for k in range(quarters):
        rows_of = []
        for j in range(4):
            flat = k_ref.at[2 * k + j // 2]
            rows_of.append(
                jnp.concatenate([flat[j % 2 : j % 2 + 1, 4 * f * a : 4 * f * (a + 1)] for a in range(f // 4)], axis=0)
            )
        for b in range(4):
            value = rows_of[b]
            for j in range(4):
                if j != b:
                    value = jnp.where(lane // f == j, pltpu.roll(rows_of[j], (j - b) % 4 * f, 1), value)
            h_sc[pl.ds(k * f + b, f // 4, stride=4), :] = value
    h_one = h_sc[...]
    is_real = (lane // f) % 2 == 0
    h_two = jnp.where(is_real, -pltpu.roll(h_one, 3 * f, 1), pltpu.roll(h_one, f, 1))

    def fields(real, imag):
        need(7, 8)
        w = 8 * f
        real = jnp.concatenate([real] * quarters, axis=0)
        imag = jnp.concatenate([imag] * quarters, axis=0)
        gated = h_one * real + h_two * imag
        turned = dot(jnp.concatenate(split(gated), axis=0), lane_fwd[...])
        m = quarters * f
        turned = (turned[:m, :w] + turned[:m, w:]) + turned[m:, :w]
        wide = jnp.concatenate(
            [
                jnp.concatenate([turned[k * f : (k + 1) * f, : 4 * f], turned[k * f : (k + 1) * f, 4 * f :]], axis=0)
                for k in range(quarters)
            ],
            axis=1,
        )
        return dot(row_fwd[...], stacked(wide))

    def write_slope(field):
        need(9, 10, 2)
        energy = field[:g] * field[:g] + field[g:] * field[g:]
        summed = energy[:, : 2 * g] * portions[0]
        for k in range(1, quarters):
            summed = summed + energy[:, 2 * g * k : 2 * g * (k + 1)] * portions[k]
        summed = summed + pltpu.roll(summed, g, 1)
        level = dot(jnp.concatenate(split(summed), axis=1), up_cols[...])
        high, rest = split(level)
        level = jnp.concatenate([high, rest, high, rest], axis=0)
        for r in range(0, n, edge):
            intensity = dot(down_cols[r : r + edge, :], level)
            resist = 1.0 / (1.0 + jnp.exp(-SHARPNESS * (intensity - THRESHOLD)))
            goal = target_ref[0, r : r + edge, :].astype(jnp.float32)
            value = (2.0 * SHARPNESS) * (resist - goal) * resist * (1.0 - resist)
            slope[r : r + edge, :] = value.astype(BF16)

    def adjoint(field):
        need(11, 12)
        low = dot(up_cols[: 2 * g, :], slope[...])
        low = low[:g] + low[g:]
        low = dot(jnp.concatenate(split(low), axis=0), down_cols[...])
        low = (low[:g, : 2 * g] + low[:g, 2 * g :]) + low[g:, : 2 * g]
        weighted = field * jnp.concatenate([jnp.concatenate([low] * quarters, axis=1)] * 2, axis=0)
        high, rest = split(weighted)
        back = dot(row_back[...], high)
        back = (back[: 2 * f] + back[2 * f :]) + dot(row_back[: 2 * f, :], rest)
        tall = jnp.concatenate(
            [
                jnp.concatenate([back[:f, 4 * f * k : 4 * f * (k + 1)], back[f:, 4 * f * k : 4 * f * (k + 1)]], axis=1)
                for k in range(quarters)
            ],
            axis=0,
        )
        m = quarters * f
        turned = dot(jnp.concatenate(split(tall), axis=0), lane_back[...])
        turned = (turned[:m, : 4 * f] + turned[:m, 4 * f :]) + turned[m:, : 4 * f]
        first, second = h_one * turned, h_two * turned
        real = jnp.zeros((f, 4 * f), jnp.float32)
        imag = jnp.zeros((f, 4 * f), jnp.float32)
        for k in range(quarters):
            real = real + first[k * f : (k + 1) * f] * portions[k]
            imag = imag + second[k * f : (k + 1) * f] * portions[k]
        real = real + pltpu.roll(real, 2 * f, 1)
        real = real + pltpu.roll(real, f, 1)
        imag = imag + pltpu.roll(imag, 2 * f, 1)
        imag = imag + pltpu.roll(imag, f, 1)
        return jnp.where(low_half, real, imag)

    def tails(packed):
        need(15)
        out = dot(jnp.concatenate(split(packed), axis=1), tail_tab[...])
        return jnp.concatenate([out[:, :n], out[:, n:]], axis=0)

    field = fields(*band_one)
    write_slope(field)
    packed = adjoint(field)
    adj[...] = packed
    start(plan["adj"])

    need(13, 14)
    turned = dot(row_flip[...], jnp.concatenate(split(packed), axis=0))
    mirrored = dot(jnp.concatenate(split(turned), axis=1), lane_flip[...])
    band = band_next - STEP_SIZE * (packed + mirrored)
    arrived(plan["spec"])
    for to in range(8):
        band = band + spec_in[to]
    swapped = pltpu.roll(band, 2 * f, 1)
    field = fields(jnp.where(low_half, band, swapped), jnp.where(low_half, swapped, band))
    write_slope(field)

    arrived(plan["c3"])
    for v, h in corners:
        @pl.when(both(beside[h], above[v]))
        def _(v=v, h=h):
            c4[:, v, h] = c2[:, v, h] + c3[:, v, h]
            q[:, v, h, pl.ds((1 - h) * half, half), :] = c1[:, v, h] + c3[:, v, h]
    start(plan["c5"])

    tail_last = tails(adjoint(field))
    tail_own = tails(packed)
    arrived(plan["adj"])

    def joined(tail, tail_left, tail_right):
        return share_col * jnp.concatenate(
            [tail[:, :edge] + tail_left[:, far:], tail[:, edge:far], tail[:, far:] + tail_right[:, :edge]], axis=1
        )

    around = [tails(adj_in[to]) for to in range(8)]
    sum_own = joined(tail_own, around[0], around[1])
    sum_end = (joined(around[2], around[4], around[5]), joined(around[3], around[6], around[7]))
    need(16)
    base = -0.125 * tail_own - STEP_SIZE * tail_last
    inner_m = stacked(base - 0.125 * sum_own)
    inner_d = stacked(STEP_SIZE * (sum_own - tail_own))
    for r in range(0, n, edge):
        rows = slice(r, r + edge)
        by = share_row(r)
        if by is None:
            grad_m = dot(grad_rows[rows, :], inner_m)
            grad_d = dot(grad_rows[rows, :], inner_d)
        else:
            other = sum_end[0] if r == 0 else sum_end[1]
            across = dot(grad_rows[far:, :] if r == 0 else grad_rows[:edge, :], stacked(by * other))
            grad_m = dot(grad_rows[rows, :], stacked(base - (0.125 * by) * sum_own)) - 0.125 * across
            grad_d = dot(grad_rows[rows, :], stacked(STEP_SIZE * (by * sum_own - tail_own))) + STEP_SIZE * across
        m, d = md[0, rows, :], md[1, rows, :]
        cover = scaled(share_col, by)
        mask_out[0, rows, :] = cover * (m + 0.625 * d) - 0.375 * d + grad_m
        dual_out[0, rows, :] = (1.5 * m + 0.75 * d) * (1.0 - cover) + grad_d

    def settle(rows, cols, by, m, d):
        mask_out[0, rows, cols] = mask_out[0, rows, cols] + by * (m + 0.625 * d)
        dual_out[0, rows, cols] = dual_out[0, rows, cols] - by * (1.5 * m + 0.75 * d)

    arrived(plan["c5"] + plan["hc"] + plan["vc"])
    for v, h in corners:
        @pl.when(both(beside[h], above[v]))
        def _(v=v, h=h):
            q[:, v, h, pl.ds(h * half, half), :] = c5[:, v, h] - md[:, piece(v, h), bands[h]]

        @pl.when(jnp.logical_or(beside[h], above[v]))
        def _(v=v, h=h):
            settle(bands[v], bands[h], share_end[v] * share_side[h], q[0, v, h], q[1, v, h])
    arrived(plan["h", 0] + plan["h", 1])
    for h in range(2):
        @pl.when(beside[h])
        def _(h=h):
            settle(middle, bands[h], share_side[h], hr[0, h], hr[1, h])
    arrived(plan["v", 0] + plan["v", 1])
    for v in range(2):
        @pl.when(above[v])
        def _(v=v):
            settle(bands[v], middle, share_end[v], vr[0, v], vr[1, v])
    for entries in plan.values():
        sent(entries)


def per_device(count, mask_init, dual_init, target, kernels, weights):
    n = mask_init.shape[-1]
    edge = INTERSECTION
    f = int(round(kernels.shape[-1] ** 0.5))
    tables = [jnp.asarray(t) for t in host_tables(n, f)]
    f32 = jnp.float32
    whole = pl.BlockSpec(memory_space=pltpu.VMEM)
    far_memory = pl.BlockSpec(memory_space=pltpu.HBM)
    arrays = (mask_init, dual_init, target, kernels, weights, *tables)
    tile = jax.ShapeDtypeStruct((1, n, n), f32)
    inner = n - 2 * edge
    half = edge // 2
    return pl.pallas_call(
        functools.partial(body, n, f, edge, count),
        out_shape=(tile, tile),
        in_specs=[far_memory] * len(arrays),
        out_specs=(whole, whole),
        scratch_shapes=[
            pltpu.SMEM(a.shape, a.dtype) if i == 4 else pltpu.VMEM(a.shape, a.dtype)
            for i, a in enumerate(arrays) if i >= 2
        ]
        + [
            pltpu.VMEM((2, n, n), f32),
            pltpu.VMEM((kernels.shape[0] // 2 * f, 4 * f), f32),
            pltpu.SemaphoreType.DMA((len(arrays),)),
            pltpu.VMEM((2, 2, inner, edge), f32),
            pltpu.VMEM((2, 2, edge, inner), f32),
            pltpu.VMEM((2, 2, 2, edge, edge), f32),
        ]
        + [pltpu.VMEM((2, 2, 2, half, edge), f32)] * 5
        + [pltpu.VMEM((n, n), BF16)] * 4
        + [
            pltpu.VMEM((8, f, 4 * f), f32),
            pltpu.VMEM((8, f, 4 * f), f32),
            pltpu.VMEM((f, 4 * f), f32),
            pltpu.VMEM((8, f, 4 * f), f32),
            pltpu.SemaphoreType.DMA((44,)),
            pltpu.SemaphoreType.DMA((44,)),
        ],
        compiler_params=pltpu.CompilerParams(
            collective_id=0, has_side_effects=True, vmem_limit_bytes=48 * 1024 * 1024
        ),
    )(*[pltpu.with_memory_space_constraint(a, pltpu.HBM) for a in arrays])


def solution(mesh):
    tile = P(("region", "ty"), None, None)
    return jax.shard_map(
        functools.partial(per_device, mesh.shape["ty"]),
        mesh=mesh,
        in_specs=(tile, tile, tile, P(), P()),
        out_specs=(tile, tile),
        check_vma=False,
    )
```

```python
import functools

import jax
import jax.numpy as jnp
import numpy as np
from jax import lax
from jax.experimental import pallas as pl
from jax.experimental.pallas import tpu as pltpu
from jax.sharding import PartitionSpec as P

GRID_COLS = 4
INTERSECTION = 128
SHARPNESS = 8.0
THRESHOLD = 0.3
STEP_SIZE = 0.25
PENALTY = 1.0
MESH = pl.DeviceIdType.MESH
BF16 = jnp.bfloat16


def split_host(table):
    table = table.astype(np.float32)
    high = table.astype(BF16)
    low = (table - high.astype(np.float32)).astype(BF16)
    return high, low


def host_tables(n, f):
    g = 2 * f
    freq = np.arange(f) - f // 2
    phase = 2.0 * np.pi * ((freq[:, None] * np.arange(n)[None, :]) % n) / n
    cos, sin = np.cos(phase), -np.sin(phase)
    rows = np.concatenate([cos, sin], 0)
    rows_hi, rows_lo = split_host(rows)
    row_side = np.concatenate([rows_hi, rows_lo], 0)
    col_wide = np.concatenate([np.tile(cos.T, (1, 4)), np.tile(sin.T, (1, 4))], 1)
    col_side = split_host(col_wide)[0]
    coarse = 2.0 * np.pi * ((np.arange(g)[:, None] * freq[None, :]) % g) / g
    er, ei = np.cos(coarse), np.sin(coarse)
    pair = np.eye(2)
    to_real = np.kron(pair, np.concatenate([er.T, -ei.T], 0))
    to_imag = np.kron(pair, np.concatenate([ei.T, er.T], 0))
    lane_turn = np.concatenate([to_real, to_imag], 1)
    lane_fwd = np.concatenate(split_host(lane_turn / (n * n)), 1)
    lane_back = np.concatenate(split_host(lane_turn.T), 1)
    row_turn = np.concatenate([np.concatenate([er, -ei], 1), np.concatenate([ei, er], 1)], 0)
    turn_hi, turn_lo = split_host(row_turn)
    row_fwd = np.concatenate([turn_hi, turn_lo, turn_hi, turn_lo], 1)
    row_back = np.concatenate(split_host(row_turn.T), 0)
    half = np.arange(-(f - 1), f)
    angle = np.arange(n)[:, None] * f * 2 - np.arange(g)[None, :] * n
    spread = np.cos(2.0 * np.pi * ((angle[..., None] * half) % (n * g)) / (n * g)).sum(-1) / g
    s_hi, s_lo = split_host(spread)
    up_cols = np.concatenate([s_hi.T, s_lo.T, s_hi.T, s_lo.T], 0)
    down_cols = np.concatenate([s_hi, s_hi, s_lo, s_lo], 1)
    scale = 2.0 / (n * n)
    c_hi, c_lo = split_host(cos * scale)
    t_hi, t_lo = split_host(sin * scale)
    tail_r = np.concatenate([c_hi, t_hi, c_lo, t_lo], 0)
    tail_i = np.concatenate([-t_hi, c_hi, -t_lo, c_lo], 0)
    tail = np.concatenate([tail_r, tail_i], 1)
    tail_tab = np.concatenate([tail, tail], 0)
    grad_rows = np.concatenate([rows_hi.T, rows_lo.T, rows_hi.T, rows_lo.T], 1)
    turn = np.zeros((f, f))
    turn[np.arange(1, f), f - np.arange(1, f)] = 1.0
    row_flip = np.concatenate([turn, turn], 1)
    none = np.zeros((f, f))
    one_flip = np.concatenate(
        [np.concatenate([turn, none, turn, none], 1), np.concatenate([none, -turn, none, -turn], 1),
         np.zeros((2 * f, 4 * f))], 0,
    )
    lane_flip = np.concatenate([one_flip, one_flip], 0)
    tables = (
        row_side, col_side, lane_fwd, row_fwd, up_cols, down_cols, row_back, lane_back,
        row_flip, lane_flip, tail_tab, grad_rows,
    )
    return [np.asarray(t, dtype=BF16) for t in tables]


def dot(a, b):
    return lax.dot_general(a, b, (((1,), (0,)), ((), ())), preferred_element_type=jnp.float32)


def split(x):
    high = x.astype(BF16)
    return high, (x - high.astype(jnp.float32)).astype(BF16)


def stacked(x):
    high, low = split(x)
    return jnp.concatenate([high, high, low, low], axis=0)


INPUTS = 17
ORDER = (1, 0, 5, 6, 4, 3, 7, 8, 9, 2, 10, 11, 12, 13, 14, 15, 16)


def body(n, f, edge, count, *refs):
    ins, refs = refs[:INPUTS], refs[INPUTS:]
    mask_out, dual_out = refs[:2]
    refs = refs[2:]
    held, refs = refs[: INPUTS - 2], refs[INPUTS - 2 :]
    target_ref, k_ref, w_ref = held[:3]
    (
        row_side, col_side, lane_fwd, row_fwd, up_cols, down_cols, row_back, lane_back,
        row_flip, lane_flip, tail_tab, grad_rows,
    ) = held[3:]
    (
        md, h_sc, load_sem, hr, vr, q, q2, c7, c1, c2, c3, c4, c5, mb, xb, yb, slope, spec, spec_in, adj, adj_in,
        ready, send_sem, recv_sem,
    ) = refs
    places = [md.at[0], md.at[1], *held]
    sources = [ins[0].at[0], ins[1].at[0], *ins[2:]]
    loads = [pltpu.make_async_copy(src, dst, load_sem.at[i]) for i, (src, dst) in enumerate(zip(sources, places))]
    far = n - edge
    half = edge // 2
    g = 2 * f
    me = lax.axis_index("ty")
    row, col = me // GRID_COLS, me % GRID_COLS
    grid_rows = count // GRID_COLS
    left, right = col > 0, col < GRID_COLS - 1
    upper, lower = row > 0, row < grid_rows - 1
    both = jnp.logical_and
    near = [
        (-1, left), (1, right), (-GRID_COLS, upper), (GRID_COLS, lower),
        (-GRID_COLS - 1, both(upper, left)), (-GRID_COLS + 1, both(upper, right)),
        (GRID_COLS - 1, both(lower, left)), (GRID_COLS + 1, both(lower, right)),
    ]
    opposite = [1, 0, 3, 2, 7, 6, 5, 4]
    beside, above = (left, right), (upper, lower)
    lone_h, lone_v = [jnp.logical_not(x) for x in beside], [jnp.logical_not(x) for x in above]
    pair = (both(left, col % 2 == 1), both(right, col % 2 == 0))
    cross = [both(beside[h], jnp.logical_not(pair[h])) for h in range(2)]

    barrier = pltpu.get_barrier_semaphore()
    earlier, later = (0, 2, 4, 5), (1, 3, 6, 7)
    for to in later:
        @pl.when(near[to][1])
        def _(shift=near[to][0]):
            pl.semaphore_signal(barrier, inc=1, device_id={"ty": me + shift}, device_id_type=MESH)

    for i in ORDER:
        loads[i].start()

    counter = [0]

    def remote(src, dst, to, send_if, recv_if):
        index = counter[0]
        counter[0] += 1
        copy = pltpu.make_async_remote_copy(
            src_ref=src, dst_ref=dst, send_sem=send_sem.at[index], recv_sem=recv_sem.at[index],
            device_id={"ty": me + near[to][0]}, device_id_type=MESH,
        )
        return copy, send_if, recv_if, to

    def start(entries, which=None):
        for entry in entries:
            if which is None or entry[3] in which:
                pl.when(entry[1])(entry[0].start)

    def arrived(entries):
        for entry in entries:
            pl.when(entry[2])(entry[0].wait_recv)

    def sent(entries):
        for entry in entries:
            pl.when(entry[1])(entry[0].wait_send)

    begin = (0, far)
    bands = (pl.ds(0, edge), pl.ds(far, edge))
    middle = pl.ds(edge, far - edge)
    corners = [(v, h) for v in range(2) for h in range(2)]

    def piece(v, part):
        return pl.ds(begin[v] + part * half, half)

    raw = (ins[0].at[0], ins[1].at[0])
    plan = {}
    for i in range(2):
        for part in range(2):
            cols = pl.ds(edge + part * (far - edge) // 2, (far - edge) // 2)
            into = pl.ds(part * (far - edge) // 2, (far - edge) // 2)
            plan["v", i, part] = [
                remote(raw[i].at[bands[v], cols], vr.at[i, 1 - v, :, into], 2 + v, above[v], above[1 - v])
                for v in range(2)
            ]
        plan["h", i] = [
            remote(raw[i].at[middle, bands[h]], hr.at[i, 1 - h], h, beside[h], beside[1 - h]) for h in range(2)
        ]
    plan["hc"] = [
        remote(
            raw[i].at[bands[v], bands[h]], q.at[i, v, 1 - h], h,
            both(beside[h], lone_v[v]), both(beside[1 - h], lone_v[v]),
        )
        for v, h in corners for i in range(2)
    ]
    for name, side in (("vc", lone_h), ("vx", cross)):
        plan[name] = [
            remote(
                raw[i].at[bands[v], bands[h]], q.at[i, 1 - v, h], 2 + v,
                both(above[v], side[h]), both(above[1 - v], side[h]),
            )
            for v, h in corners for i in range(2)
        ]
    plan["cf"] = [
        remote(c7.at[:, v, h], q2.at[:, v, 1 - h], h, both(cross[h], above[v]), both(cross[1 - h], above[v]))
        for v, h in corners
    ]
    plan["c1"] = [
        remote(
            raw[i].at[piece(v, h), bands[h]], c1.at[i, v, 1 - h], h,
            both(pair[h], above[v]), both(pair[1 - h], above[v]),
        )
        for v, h in corners for i in range(2)
    ]
    plan["c3"] = [
        remote(c2.at[:, v, h], c3.at[:, 1 - v, h], 2 + v, both(pair[h], above[v]), both(pair[h], above[1 - v]))
        for v, h in corners
    ]
    plan["c5"] = [
        remote(c4.at[:, v, h], c5.at[:, v, 1 - h], h, both(pair[h], above[v]), both(pair[1 - h], above[v]))
        for v, h in corners
    ]
    plan["spec"] = [
        remote(spec.at[to], spec_in.at[opposite[to]], to, near[to][1], near[opposite[to]][1]) for to in range(8)
    ]
    plan["adj"] = [remote(adj, adj_in.at[opposite[to]], to, near[to][1], near[opposite[to]][1]) for to in range(8)]

    for to in range(8):
        @pl.when(jnp.logical_not(near[to][1]))
        def _(to=to):
            spec_in[to] = jnp.zeros((f // 2, 4 * f), jnp.float32)
            adj_in[to] = jnp.zeros((f // 2, 4 * f), jnp.float32)

    expected = sum(near[to][1].astype(jnp.int32) for to in earlier)

    @pl.when(expected > 0)
    def _():
        pl.semaphore_wait(barrier, expected)

    for to in earlier:
        @pl.when(near[to][1])
        def _(to=to):
            pl.semaphore_signal(
                ready.at[opposite[to]], inc=1, device_id={"ty": me + near[to][0]}, device_id_type=MESH
            )
    opening = plan["c1"] + plan["vx"] + plan["vc"] + plan["hc"]
    start(opening, earlier)

    waited = set()

    def need(*which):
        for i in which:
            if i not in waited:
                waited.add(i)
                loads[i].wait()

    need(0, 1)
    up_f, down_f = upper.astype(jnp.float32), lower.astype(jnp.float32)
    left_f, right_f = left.astype(jnp.float32), right.astype(jnp.float32)
    at_col = lax.broadcasted_iota(jnp.int32, (1, n), 1)
    share_col = jnp.where(at_col < edge, 1.0 - 0.5 * left_f, jnp.where(at_col >= far, 1.0 - 0.5 * right_f, 1.0))
    share_side = (1.0 - 0.5 * left_f, 1.0 - 0.5 * right_f)
    share_end = (1.0 - 0.5 * up_f, 1.0 - 0.5 * down_f)

    def share_row(r):
        return share_end[0] if r == 0 else share_end[1] if r == far else None

    def scaled(x, by):
        return x if by is None else x * by

    lane = lax.broadcasted_iota(jnp.int32, (1, 4 * f), 1)
    low_half = lane < 2 * f
    is_real = (lane // f) % 2 == 0

    for r in range(0, n, edge):
        rows = slice(r, r + edge)
        m, d = md[0, rows, :], md[1, rows, :]
        y = (m + d) * scaled(0.5 * share_col, share_row(r))
        mb[rows, :] = m.astype(BF16)
        yb[rows, :] = y.astype(BF16)
        xb[rows, :] = (0.5 * m - 0.25 * d + y).astype(BF16)

    def meet(*which):
        for to in which:
            @pl.when(near[to][1])
            def _(to=to):
                pl.semaphore_wait(ready.at[to], 1)

    meet(3)
    start(opening, (3,))
    meet(1)
    start(opening, (1,))

    need(5, 6)
    top_part = dot(row_side[:g, far:], yb[:edge, :]).astype(BF16)
    end_part = dot(row_side[:g, :edge], yb[far:, :]).astype(BF16)
    left_part = dot(row_side[:g, :], yb[:, :edge]).astype(BF16)
    right_part = dot(row_side[:g, :], yb[:, far:]).astype(BF16)

    def to_band(grid):
        real = grid[:f, : 4 * f] - grid[f:, 4 * f :]
        imag = grid[:f, 4 * f :] + grid[f:, : 4 * f]
        return real, imag

    def packed_band(grid):
        real, imag = to_band(grid)
        return jnp.where(is_real, real, imag)

    def folded(x):
        return jnp.where(low_half, x[: f // 2], x[f // 2 :])

    def unfolded(x):
        turned = pltpu.roll(x, 2 * f, 1)
        return jnp.concatenate([jnp.where(low_half, x, turned), jnp.where(low_half, turned, x)], axis=0)

    at_left = dot(
        jnp.concatenate([left_part, top_part[:, :edge], end_part[:, :edge]], axis=0), col_side[far:, :]
    )
    at_right = dot(
        jnp.concatenate([right_part, top_part[:, far:], end_part[:, far:]], axis=0), col_side[:edge, :]
    )
    at_ends = dot(jnp.concatenate([top_part, end_part], axis=0), col_side[...])
    for i, to in enumerate((0, 4, 6)):
        spec[to] = folded(packed_band(at_left[i * g : (i + 1) * g]))
    for i, to in enumerate((1, 5, 7)):
        spec[to] = folded(packed_band(at_right[i * g : (i + 1) * g]))
    for i, to in enumerate((2, 3)):
        spec[to] = folded(packed_band(at_ends[i * g : (i + 1) * g]))
    arrived(plan["c1"])
    for v, h in corners:
        @pl.when(both(pair[h], above[v]))
        def _(v=v, h=h):
            c2[:, v, h] = md[:, piece(v, 1 - h), bands[h]] + c1[:, v, h]
    meet(6, 7)
    start(plan["spec"] + plan["c3"] + plan["v", 1, 0] + plan["h", 1] + plan["h", 0])

    part = dot(row_side[...], jnp.concatenate([mb[...], xb[...]], axis=1))
    part = part[:g] + part[g:]
    first_part, next_part = part[:, :n], part[:, n:]
    grid = dot(jnp.concatenate([*split(first_part), next_part.astype(BF16)], axis=0), col_side[...])
    band_one = to_band(grid[:g] + grid[g : 2 * g])
    band_next = packed_band(grid[2 * g :])

    need(4, 3)
    quarters = w_ref.shape[0] // 2
    total = w_ref[0]
    for k in range(1, w_ref.shape[0]):
        total = total + w_ref[k]
    portions = [
        jnp.where(low_half, w_ref[2 * k], w_ref[2 * k + 1]) / jnp.full((1, 4 * f), total, jnp.float32)
        for k in range(quarters)
    ]
    for k in range(quarters):
        rows_of = []
        for j in range(4):
            flat = k_ref.at[2 * k + j // 2]
            rows_of.append(
                jnp.concatenate([flat[j % 2 : j % 2 + 1, 4 * f * a : 4 * f * (a + 1)] for a in range(f // 4)], axis=0)
            )
        for b in range(4):
            value = rows_of[b]
            for j in range(4):
                if j != b:
                    value = jnp.where(lane // f == j, pltpu.roll(rows_of[j], (j - b) % 4 * f, 1), value)
            h_sc[pl.ds(k * f + b, f // 4, stride=4), :] = value
    h_one = h_sc[...]
    h_two = jnp.where(is_real, -pltpu.roll(h_one, 3 * f, 1), pltpu.roll(h_one, f, 1))

    def fields(real, imag):
        need(7, 8)
        w = 8 * f
        real = jnp.concatenate([real] * quarters, axis=0)
        imag = jnp.concatenate([imag] * quarters, axis=0)
        gated = h_one * real + h_two * imag
        turned = dot(jnp.concatenate(split(gated), axis=0), lane_fwd[...])
        m = quarters * f
        turned = (turned[:m, :w] + turned[:m, w:]) + turned[m:, :w]
        wide = jnp.concatenate(
            [
                jnp.concatenate([turned[k * f : (k + 1) * f, : 4 * f], turned[k * f : (k + 1) * f, 4 * f :]], axis=0)
                for k in range(quarters)
            ],
            axis=1,
        )
        return dot(row_fwd[...], stacked(wide))

    def write_slope(field):
        need(9, 10, 2)
        energy = field[:g] * field[:g] + field[g:] * field[g:]
        summed = energy[:, : 2 * g] * portions[0]
        for k in range(1, quarters):
            summed = summed + energy[:, 2 * g * k : 2 * g * (k + 1)] * portions[k]
        summed = summed + pltpu.roll(summed, g, 1)
        level = dot(jnp.concatenate(split(summed), axis=1), up_cols[...])
        high, rest = split(level)
        level = jnp.concatenate([high, rest, high, rest], axis=0)
        for r in range(0, n, edge):
            intensity = dot(down_cols[r : r + edge, :], level)
            resist = 1.0 / (1.0 + jnp.exp(-SHARPNESS * (intensity - THRESHOLD)))
            goal = target_ref[0, r : r + edge, :].astype(jnp.float32)
            value = (2.0 * SHARPNESS) * (resist - goal) * resist * (1.0 - resist)
            slope[r : r + edge, :] = value.astype(BF16)

    def adjoint(field):
        need(11, 12)
        low = dot(up_cols[: 2 * g, :], slope[...])
        low = low[:g] + low[g:]
        low = dot(jnp.concatenate(split(low), axis=0), down_cols[...])
        low = (low[:g, : 2 * g] + low[:g, 2 * g :]) + low[g:, : 2 * g]
        weighted = field * jnp.concatenate([jnp.concatenate([low] * quarters, axis=1)] * 2, axis=0)
        high, rest = split(weighted)
        back = dot(row_back[...], high)
        back = (back[: 2 * f] + back[2 * f :]) + dot(row_back[: 2 * f, :], rest)
        tall = jnp.concatenate(
            [
                jnp.concatenate([back[:f, 4 * f * k : 4 * f * (k + 1)], back[f:, 4 * f * k : 4 * f * (k + 1)]], axis=1)
                for k in range(quarters)
            ],
            axis=0,
        )
        m = quarters * f
        turned = dot(jnp.concatenate(split(tall), axis=0), lane_back[...])
        turned = (turned[:m, : 4 * f] + turned[:m, 4 * f :]) + turned[m:, : 4 * f]
        first, second = h_one * turned, h_two * turned
        real = jnp.zeros((f, 4 * f), jnp.float32)
        imag = jnp.zeros((f, 4 * f), jnp.float32)
        for k in range(quarters):
            real = real + first[k * f : (k + 1) * f] * portions[k]
            imag = imag + second[k * f : (k + 1) * f] * portions[k]
        real = real + pltpu.roll(real, 2 * f, 1)
        real = real + pltpu.roll(real, f, 1)
        imag = imag + pltpu.roll(imag, 2 * f, 1)
        imag = imag + pltpu.roll(imag, f, 1)
        return jnp.where(is_real, real, imag)

    def tails(packed):
        need(15)
        out = dot(jnp.concatenate(split(packed), axis=1), tail_tab[...])
        return jnp.concatenate([out[:, :n], out[:, n:]], axis=0)

    def band_tails(which, begin):
        packed = jnp.concatenate([unfolded(adj_in[to]) for to in which], axis=0)
        packed = jnp.concatenate(split(packed), axis=1)
        real = dot(packed, tail_tab[:, begin : begin + edge])
        imag = dot(packed, tail_tab[:, n + begin : n + begin + edge])
        return [
            jnp.concatenate([real[i * f : (i + 1) * f], imag[i * f : (i + 1) * f]], axis=0) for i in range(len(which))
        ]

    field = fields(*band_one)
    write_slope(field)
    packed = adjoint(field)
    adj[...] = folded(packed)
    start(plan["adj"] + plan["v", 1, 1] + plan["v", 0, 0] + plan["v", 0, 1])
    arrived(plan["vx"])
    for v, h in corners:
        @pl.when(both(cross[h], above[v]))
        def _(v=v, h=h):
            for i in range(2):
                c7[i, v, h] = md[i, bands[v], bands[h]] + q[i, v, h]
    start(plan["cf"])

    need(13, 14)
    turned = dot(row_flip[...], jnp.concatenate(split(packed), axis=0))
    mirrored = dot(jnp.concatenate(split(turned), axis=1), lane_flip[...])
    band = band_next - STEP_SIZE * (packed + mirrored)
    arrived(plan["spec"])
    incoming = spec_in[0]
    for to in range(1, 8):
        incoming = incoming + spec_in[to]
    band = band + unfolded(incoming)
    field = fields(jnp.where(is_real, band, pltpu.roll(band, f, 1)), jnp.where(is_real, pltpu.roll(band, 3 * f, 1), band))
    write_slope(field)
    arrived(plan["c3"])
    for v, h in corners:
        @pl.when(both(pair[h], above[v]))
        def _(v=v, h=h):
            c4[:, v, h] = c2[:, v, h] + c3[:, v, h]
            q[:, v, h, pl.ds((1 - h) * half, half), :] = c1[:, v, h] + c3[:, v, h]
    start(plan["c5"])


    last = adjoint(field)
    tail_last = tails(last)
    tail_own = tails(packed)
    arrived(plan["adj"])

    def joined(tail, from_left, from_right):
        return share_col * jnp.concatenate(
            [tail[:, :edge] + from_left, tail[:, edge:far], tail[:, far:] + from_right], axis=1
        )

    at_left, at_right = band_tails((0, 4, 6), far), band_tails((1, 5, 7), 0)
    sides = dot(
        jnp.concatenate(split(jnp.concatenate([unfolded(adj_in[2]), unfolded(adj_in[3])], axis=0)), axis=1), tail_tab[...]
    )
    ends = [jnp.concatenate([sides[i * f : (i + 1) * f, :n], sides[i * f : (i + 1) * f, n:]], axis=0) for i in range(2)]
    sum_own = joined(tail_own, at_left[0], at_right[0])
    sum_end = [joined(ends[i], at_left[1 + i], at_right[1 + i]) for i in range(2)]
    need(16)
    base = -0.125 * tail_own - STEP_SIZE * tail_last
    inner_m = stacked(base - 0.125 * sum_own)
    inner_d = stacked(STEP_SIZE * (sum_own - tail_own))
    for r in range(0, n, edge):
        rows = slice(r, r + edge)
        by = share_row(r)
        if by is None:
            grad_m = dot(grad_rows[rows, :], inner_m)
            grad_d = dot(grad_rows[rows, :], inner_d)
        else:
            other = sum_end[0] if r == 0 else sum_end[1]
            across = dot(grad_rows[far:, :] if r == 0 else grad_rows[:edge, :], stacked(by * other))
            grad_m = dot(grad_rows[rows, :], stacked(base - (0.125 * by) * sum_own)) - 0.125 * across
            grad_d = dot(grad_rows[rows, :], stacked(STEP_SIZE * (by * sum_own - tail_own))) + STEP_SIZE * across
        m, d = md[0, rows, :], md[1, rows, :]
        cover = scaled(share_col, by)
        mask_out[0, rows, :] = cover * (m + 0.625 * d) - 0.375 * d + grad_m
        dual_out[0, rows, :] = (1.5 * m + 0.75 * d) * (1.0 - cover) + grad_d

    def settle(rows, cols, by, m, d):
        mask_out[0, rows, cols] = mask_out[0, rows, cols] + by * (m + 0.625 * d)
        dual_out[0, rows, cols] = dual_out[0, rows, cols] - by * (1.5 * m + 0.75 * d)

    arrived(plan["c5"] + plan["hc"] + plan["vc"] + plan["cf"])
    for v, h in corners:
        @pl.when(both(pair[h], above[v]))
        def _(v=v, h=h):
            q[:, v, h, pl.ds(h * half, half), :] = c5[:, v, h] - md[:, piece(v, h), bands[h]]

        @pl.when(both(cross[h], above[v]))
        def _(v=v, h=h):
            q[:, v, h] = q[:, v, h] + q2[:, v, h]

        @pl.when(jnp.logical_or(beside[h], above[v]))
        def _(v=v, h=h):
            settle(bands[v], bands[h], share_end[v] * share_side[h], q[0, v, h], q[1, v, h])
    arrived(plan["h", 0] + plan["h", 1])
    for h in range(2):
        @pl.when(beside[h])
        def _(h=h):
            settle(middle, bands[h], share_side[h], hr[0, h], hr[1, h])
    arrived([entry for i in range(2) for part in range(2) for entry in plan["v", i, part]])
    for v in range(2):
        @pl.when(above[v])
        def _(v=v):
            settle(bands[v], middle, share_end[v], vr[0, v], vr[1, v])
    for entries in plan.values():
        sent(entries)


def per_device(count, mask_init, dual_init, target, kernels, weights):
    n = mask_init.shape[-1]
    edge = INTERSECTION
    f = int(round(kernels.shape[-1] ** 0.5))
    tables = [jnp.asarray(t) for t in host_tables(n, f)]
    f32 = jnp.float32
    whole = pl.BlockSpec(memory_space=pltpu.VMEM)
    far_memory = pl.BlockSpec(memory_space=pltpu.HBM)
    arrays = (mask_init, dual_init, target, kernels, weights, *tables)
    tile = jax.ShapeDtypeStruct((1, n, n), f32)
    inner = n - 2 * edge
    half = edge // 2
    return pl.pallas_call(
        functools.partial(body, n, f, edge, count),
        out_shape=(tile, tile),
        in_specs=[far_memory] * len(arrays),
        out_specs=(whole, whole),
        scratch_shapes=[
            pltpu.SMEM(a.shape, a.dtype) if i == 4 else pltpu.VMEM(a.shape, a.dtype)
            for i, a in enumerate(arrays) if i >= 2
        ]
        + [
            pltpu.VMEM((2, n, n), f32),
            pltpu.VMEM((kernels.shape[0] // 2 * f, 4 * f), f32),
            pltpu.SemaphoreType.DMA((len(arrays),)),
            pltpu.VMEM((2, 2, inner, edge), f32),
            pltpu.VMEM((2, 2, edge, inner), f32),
            pltpu.VMEM((2, 2, 2, edge, edge), f32),
            pltpu.VMEM((2, 2, 2, edge, edge), f32),
            pltpu.VMEM((2, 2, 2, edge, edge), f32),
        ]
        + [pltpu.VMEM((2, 2, 2, half, edge), f32)] * 5
        + [pltpu.VMEM((n, n), BF16)] * 4
        + [
            pltpu.VMEM((8, f // 2, 4 * f), f32),
            pltpu.VMEM((8, f // 2, 4 * f), f32),
            pltpu.VMEM((f // 2, 4 * f), f32),
            pltpu.VMEM((8, f // 2, 4 * f), f32),
            pltpu.SemaphoreType.REGULAR((8,)),
            pltpu.SemaphoreType.DMA((76,)),
            pltpu.SemaphoreType.DMA((76,)),
        ],
        compiler_params=pltpu.CompilerParams(
            collective_id=0, has_side_effects=True, vmem_limit_bytes=48 * 1024 * 1024
        ),
    )(*[pltpu.with_memory_space_constraint(a, pltpu.HBM) for a in arrays])


def solution(mesh):
    tile = P(("region", "ty"), None, None)
    return jax.shard_map(
        functools.partial(per_device, mesh.shape["ty"]),
        mesh=mesh,
        in_specs=(tile, tile, tile, P(), P()),
        out_specs=(tile, tile),
        check_vma=False,
    )
```

```python
import functools

import jax
import jax.numpy as jnp
import numpy as np
from jax import lax
from jax.experimental import pallas as pl
from jax.experimental.pallas import tpu as pltpu
from jax.sharding import PartitionSpec as P

GRID_COLS = 4
INTERSECTION = 128
SHARPNESS = 8.0
THRESHOLD = 0.3
STEP_SIZE = 0.25
PENALTY = 1.0
MESH = pl.DeviceIdType.MESH
BF16 = jnp.bfloat16


def split_host(table):
    table = table.astype(np.float32)
    high = table.astype(BF16)
    low = (table - high.astype(np.float32)).astype(BF16)
    return high, low


def host_tables(n, f):
    g = 2 * f
    freq = np.arange(f) - f // 2
    phase = 2.0 * np.pi * ((freq[:, None] * np.arange(n)[None, :]) % n) / n
    cos, sin = np.cos(phase), -np.sin(phase)
    rows = np.concatenate([cos, sin], 0)
    rows_hi, rows_lo = split_host(rows)
    row_side = np.concatenate([rows_hi, rows_lo], 0)
    col_wide = np.concatenate([np.tile(cos.T, (1, 4)), np.tile(sin.T, (1, 4))], 1)
    col_side = split_host(col_wide)[0]
    coarse = 2.0 * np.pi * ((np.arange(g)[:, None] * freq[None, :]) % g) / g
    er, ei = np.cos(coarse), np.sin(coarse)
    pair = np.eye(2)
    to_real = np.kron(pair, np.concatenate([er.T, -ei.T], 0))
    to_imag = np.kron(pair, np.concatenate([ei.T, er.T], 0))
    lane_turn = np.concatenate([to_real, to_imag], 1)
    lane_fwd = np.concatenate(split_host(lane_turn / (n * n)), 1)
    lane_back = np.concatenate(split_host(lane_turn.T), 1)
    row_turn = np.concatenate([np.concatenate([er, -ei], 1), np.concatenate([ei, er], 1)], 0)
    turn_hi, turn_lo = split_host(row_turn)
    row_fwd = np.concatenate([turn_hi, turn_lo, turn_hi, turn_lo], 1)
    row_back = np.concatenate(split_host(row_turn.T), 0)
    half = np.arange(-(f - 1), f)
    angle = np.arange(n)[:, None] * f * 2 - np.arange(g)[None, :] * n
    spread = np.cos(2.0 * np.pi * ((angle[..., None] * half) % (n * g)) / (n * g)).sum(-1) / g
    s_hi, s_lo = split_host(spread)
    up_cols = np.concatenate([s_hi.T, s_lo.T, s_hi.T, s_lo.T], 0)
    down_cols = np.concatenate([s_hi, s_hi, s_lo, s_lo], 1)
    scale = 2.0 / (n * n)
    c_hi, c_lo = split_host(cos * scale)
    t_hi, t_lo = split_host(sin * scale)
    tail_r = np.concatenate([c_hi, t_hi, c_lo, t_lo], 0)
    tail_i = np.concatenate([-t_hi, c_hi, -t_lo, c_lo], 0)
    tail = np.concatenate([tail_r, tail_i], 1)
    tail_tab = np.concatenate([tail, tail], 0)
    grad_rows = np.concatenate([rows_hi.T, rows_lo.T, rows_hi.T, rows_lo.T], 1)
    turn = np.zeros((f, f))
    turn[np.arange(1, f), f - np.arange(1, f)] = 1.0
    row_flip = np.concatenate([turn, turn], 1)
    none = np.zeros((f, f))
    one_flip = np.concatenate(
        [np.concatenate([turn, none, turn, none], 1), np.concatenate([none, -turn, none, -turn], 1),
         np.zeros((2 * f, 4 * f))], 0,
    )
    lane_flip = np.concatenate([one_flip, one_flip], 0)
    tables = (
        row_side, col_side, lane_fwd, row_fwd, up_cols, down_cols, row_back, lane_back,
        row_flip, lane_flip, tail_tab, grad_rows,
    )
    return [np.asarray(t, dtype=BF16) for t in tables]


def dot(a, b):
    return lax.dot_general(a, b, (((1,), (0,)), ((), ())), preferred_element_type=jnp.float32)


def split(x):
    high = x.astype(BF16)
    return high, (x - high.astype(jnp.float32)).astype(BF16)


def stacked(x):
    high, low = split(x)
    return jnp.concatenate([high, high, low, low], axis=0)


INPUTS = 17
ORDER = (1, 0, 5, 6, 4, 3, 7, 8, 9, 2, 10, 11, 12, 13, 14, 15, 16)


def body(n, f, edge, count, *refs):
    ins, refs = refs[:INPUTS], refs[INPUTS:]
    mask_out, dual_out = refs[:2]
    refs = refs[2:]
    held, refs = refs[: INPUTS - 2], refs[INPUTS - 2 :]
    target_ref, k_ref, w_ref = held[:3]
    (
        row_side, col_side, lane_fwd, row_fwd, up_cols, down_cols, row_back, lane_back,
        row_flip, lane_flip, tail_tab, grad_rows,
    ) = held[3:]
    (
        md, h_sc, load_sem, hr, vr, q, q2, c7, c1, c2, c3, c4, c5, mb, xb, yb, slope, spec, spec_in, adj, adj_in,
        ready, send_sem, recv_sem,
    ) = refs
    places = [md.at[0], md.at[1], *held]
    sources = [ins[0].at[0], ins[1].at[0], *ins[2:]]
    loads = [pltpu.make_async_copy(src, dst, load_sem.at[i]) for i, (src, dst) in enumerate(zip(sources, places))]
    far = n - edge
    half = edge // 2
    g = 2 * f
    me = lax.axis_index("ty")
    row, col = me // GRID_COLS, me % GRID_COLS
    grid_rows = count // GRID_COLS
    left, right = col > 0, col < GRID_COLS - 1
    upper, lower = row > 0, row < grid_rows - 1
    both = jnp.logical_and
    near = [
        (-1, left), (1, right), (-GRID_COLS, upper), (GRID_COLS, lower),
        (-GRID_COLS - 1, both(upper, left)), (-GRID_COLS + 1, both(upper, right)),
        (GRID_COLS - 1, both(lower, left)), (GRID_COLS + 1, both(lower, right)),
    ]
    opposite = [1, 0, 3, 2, 7, 6, 5, 4]
    beside, above = (left, right), (upper, lower)
    lone_h, lone_v = [jnp.logical_not(x) for x in beside], [jnp.logical_not(x) for x in above]
    pair = (both(left, col % 2 == 1), both(right, col % 2 == 0))
    cross = [both(beside[h], jnp.logical_not(pair[h])) for h in range(2)]

    barrier = pltpu.get_barrier_semaphore()
    earlier, later = (0, 2, 4, 5), (1, 3, 6, 7)
    for to in later:
        @pl.when(near[to][1])
        def _(shift=near[to][0]):
            pl.semaphore_signal(barrier, inc=1, device_id={"ty": me + shift}, device_id_type=MESH)

    for i in ORDER:
        loads[i].start()

    counter = [0]

    def remote(src, dst, to, send_if, recv_if):
        index = counter[0]
        counter[0] += 1
        copy = pltpu.make_async_remote_copy(
            src_ref=src, dst_ref=dst, send_sem=send_sem.at[index], recv_sem=recv_sem.at[index],
            device_id={"ty": me + near[to][0]}, device_id_type=MESH,
        )
        return copy, send_if, recv_if, to

    def start(entries, which=None):
        for entry in entries:
            if which is None or entry[3] in which:
                pl.when(entry[1])(entry[0].start)

    def arrived(entries):
        for entry in entries:
            pl.when(entry[2])(entry[0].wait_recv)

    def sent(entries):
        for entry in entries:
            pl.when(entry[1])(entry[0].wait_send)

    begin = (0, far)
    bands = (pl.ds(0, edge), pl.ds(far, edge))
    middle = pl.ds(edge, far - edge)
    corners = [(v, h) for v in range(2) for h in range(2)]

    def piece(v, part):
        return pl.ds(begin[v] + part * half, half)

    raw = (ins[0].at[0], ins[1].at[0])
    plan = {}
    for i in range(2):
        for part in range(2):
            cols = pl.ds(edge + part * (far - edge) // 2, (far - edge) // 2)
            into = pl.ds(part * (far - edge) // 2, (far - edge) // 2)
            plan["v", i, part] = [
                remote(raw[i].at[bands[v], cols], vr.at[i, 1 - v, :, into], 2 + v, above[v], above[1 - v])
                for v in range(2)
            ]
        plan["h", i] = [
            remote(raw[i].at[middle, bands[h]], hr.at[i, 1 - h], h, beside[h], beside[1 - h]) for h in range(2)
        ]
    plan["hc"] = [
        remote(
            raw[i].at[bands[v], bands[h]], q.at[i, v, 1 - h], h,
            both(beside[h], lone_v[v]), both(beside[1 - h], lone_v[v]),
        )
        for v, h in corners for i in range(2)
    ]
    for name, side in (("vc", lone_h), ("vx", cross)):
        plan[name] = [
            remote(
                raw[i].at[bands[v], bands[h]], q.at[i, 1 - v, h], 2 + v,
                both(above[v], side[h]), both(above[1 - v], side[h]),
            )
            for v, h in corners for i in range(2)
        ]
    plan["cf"] = [
        remote(c7.at[:, v, h], q2.at[:, v, 1 - h], h, both(cross[h], above[v]), both(cross[1 - h], above[v]))
        for v, h in corners
    ]
    plan["c1"] = [
        remote(
            raw[i].at[piece(v, h), bands[h]], c1.at[i, v, 1 - h], h,
            both(pair[h], above[v]), both(pair[1 - h], above[v]),
        )
        for v, h in corners for i in range(2)
    ]
    plan["c3"] = [
        remote(c2.at[:, v, h], c3.at[:, 1 - v, h], 2 + v, both(pair[h], above[v]), both(pair[h], above[1 - v]))
        for v, h in corners
    ]
    plan["c5"] = [
        remote(c4.at[:, v, h], c5.at[:, v, 1 - h], h, both(pair[h], above[v]), both(pair[1 - h], above[v]))
        for v, h in corners
    ]
    plan["spec"] = [
        remote(spec.at[to], spec_in.at[opposite[to]], to, near[to][1], near[opposite[to]][1]) for to in range(8)
    ]
    plan["adj"] = [remote(adj, adj_in.at[opposite[to]], to, near[to][1], near[opposite[to]][1]) for to in range(8)]

    for to in range(8):
        @pl.when(jnp.logical_not(near[to][1]))
        def _(to=to):
            spec_in[to] = jnp.zeros((f // 2, 4 * f), jnp.float32)
            adj_in[to] = jnp.zeros((f // 2, 4 * f), jnp.float32)

    expected = sum(near[to][1].astype(jnp.int32) for to in earlier)

    @pl.when(expected > 0)
    def _():
        pl.semaphore_wait(barrier, expected)

    for to in earlier:
        @pl.when(near[to][1])
        def _(to=to):
            pl.semaphore_signal(
                ready.at[opposite[to]], inc=1, device_id={"ty": me + near[to][0]}, device_id_type=MESH
            )
    opening = plan["c1"] + plan["vx"] + plan["vc"] + plan["hc"]
    start(opening, earlier)

    waited = set()

    def need(*which):
        for i in which:
            if i not in waited:
                waited.add(i)
                loads[i].wait()

    need(0, 1)
    up_f, down_f = upper.astype(jnp.float32), lower.astype(jnp.float32)
    left_f, right_f = left.astype(jnp.float32), right.astype(jnp.float32)
    at_col = lax.broadcasted_iota(jnp.int32, (1, n), 1)
    share_col = jnp.where(at_col < edge, 1.0 - 0.5 * left_f, jnp.where(at_col >= far, 1.0 - 0.5 * right_f, 1.0))
    share_side = (1.0 - 0.5 * left_f, 1.0 - 0.5 * right_f)
    share_end = (1.0 - 0.5 * up_f, 1.0 - 0.5 * down_f)

    def share_row(r):
        return share_end[0] if r == 0 else share_end[1] if r == far else None

    def scaled(x, by):
        return x if by is None else x * by

    lane = lax.broadcasted_iota(jnp.int32, (1, 4 * f), 1)
    low_half = lane < 2 * f
    is_real = (lane // f) % 2 == 0

    for r in range(0, n, edge):
        rows = slice(r, r + edge)
        m, d = md[0, rows, :], md[1, rows, :]
        y = (m + d) * scaled(0.5 * share_col, share_row(r))
        mb[rows, :] = m.astype(BF16)
        yb[rows, :] = y.astype(BF16)
        xb[rows, :] = (0.5 * m - 0.25 * d + y).astype(BF16)

    def meet(*which):
        for to in which:
            @pl.when(near[to][1])
            def _(to=to):
                pl.semaphore_wait(ready.at[to], 1)

    meet(3)
    start(opening, (3,))
    meet(1)
    start(opening, (1,))

    need(5, 6)
    top_part = dot(row_side[:g, far:], yb[:edge, :]).astype(BF16)
    end_part = dot(row_side[:g, :edge], yb[far:, :]).astype(BF16)
    left_part = dot(row_side[:g, :], yb[:, :edge]).astype(BF16)
    right_part = dot(row_side[:g, :], yb[:, far:]).astype(BF16)

    def to_band(grid):
        real = grid[:f, : 4 * f] - grid[f:, 4 * f :]
        imag = grid[:f, 4 * f :] + grid[f:, : 4 * f]
        return real, imag

    def packed_band(grid):
        real, imag = to_band(grid)
        return jnp.where(is_real, real, imag)

    def folded(x):
        return jnp.where(low_half, x[: f // 2], x[f // 2 :])

    def unfolded(x):
        turned = pltpu.roll(x, 2 * f, 1)
        return jnp.concatenate([jnp.where(low_half, x, turned), jnp.where(low_half, turned, x)], axis=0)

    at_left = dot(
        jnp.concatenate([left_part, top_part[:, :edge], end_part[:, :edge]], axis=0), col_side[far:, :]
    )
    at_right = dot(
        jnp.concatenate([right_part, top_part[:, far:], end_part[:, far:]], axis=0), col_side[:edge, :]
    )
    at_ends = dot(jnp.concatenate([top_part, end_part], axis=0), col_side[...])
    for i, to in enumerate((0, 4, 6)):
        spec[to] = folded(packed_band(at_left[i * g : (i + 1) * g]))
    for i, to in enumerate((1, 5, 7)):
        spec[to] = folded(packed_band(at_right[i * g : (i + 1) * g]))
    for i, to in enumerate((2, 3)):
        spec[to] = folded(packed_band(at_ends[i * g : (i + 1) * g]))
    arrived(plan["c1"])
    for v, h in corners:
        @pl.when(both(pair[h], above[v]))
        def _(v=v, h=h):
            c2[:, v, h] = md[:, piece(v, 1 - h), bands[h]] + c1[:, v, h]
    meet(6, 7)
    start(plan["spec"] + plan["c3"] + plan["v", 1, 0] + plan["h", 1] + plan["h", 0])

    part = dot(row_side[...], jnp.concatenate([mb[...], xb[...]], axis=1))
    part = part[:g] + part[g:]
    first_part, next_part = part[:, :n], part[:, n:]
    grid = dot(jnp.concatenate([*split(first_part), next_part.astype(BF16)], axis=0), col_side[...])
    band_one = to_band(grid[:g] + grid[g : 2 * g])
    band_next = packed_band(grid[2 * g :])

    need(4, 3)
    quarters = w_ref.shape[0] // 2
    total = w_ref[0]
    for k in range(1, w_ref.shape[0]):
        total = total + w_ref[k]
    portions = [
        jnp.where(low_half, w_ref[2 * k], w_ref[2 * k + 1]) / jnp.full((1, 4 * f), total, jnp.float32)
        for k in range(quarters)
    ]
    for k in range(quarters):
        rows_of = []
        for j in range(4):
            flat = k_ref.at[2 * k + j // 2]
            rows_of.append(
                jnp.concatenate([flat[j % 2 : j % 2 + 1, 4 * f * a : 4 * f * (a + 1)] for a in range(f // 4)], axis=0)
            )
        for b in range(4):
            value = rows_of[b]
            for j in range(4):
                if j != b:
                    value = jnp.where(lane // f == j, pltpu.roll(rows_of[j], (j - b) % 4 * f, 1), value)
            h_sc[pl.ds(k * f + b, f // 4, stride=4), :] = value
    h_one = h_sc[...]
    h_two = jnp.where(is_real, -pltpu.roll(h_one, 3 * f, 1), pltpu.roll(h_one, f, 1))

    def fields(real, imag):
        need(7, 8)
        w = 8 * f
        real = jnp.concatenate([real] * quarters, axis=0)
        imag = jnp.concatenate([imag] * quarters, axis=0)
        gated = h_one * real + h_two * imag
        turned = dot(jnp.concatenate(split(gated), axis=0), lane_fwd[...])
        m = quarters * f
        turned = (turned[:m, :w] + turned[:m, w:]) + turned[m:, :w]
        wide = jnp.concatenate(
            [
                jnp.concatenate([turned[k * f : (k + 1) * f, : 4 * f], turned[k * f : (k + 1) * f, 4 * f :]], axis=0)
                for k in range(quarters)
            ],
            axis=1,
        )
        return dot(row_fwd[...], stacked(wide))

    def write_slope(field):
        need(9, 10, 2)
        energy = field[:g] * field[:g] + field[g:] * field[g:]
        summed = energy[:, : 2 * g] * portions[0]
        for k in range(1, quarters):
            summed = summed + energy[:, 2 * g * k : 2 * g * (k + 1)] * portions[k]
        summed = summed + pltpu.roll(summed, g, 1)
        level = dot(jnp.concatenate(split(summed), axis=1), up_cols[...])
        high, rest = split(level)
        level = jnp.concatenate([high, rest, high, rest], axis=0)
        for r in range(0, n, edge):
            intensity = dot(down_cols[r : r + edge, :], level)
            resist = 1.0 / (1.0 + jnp.exp(-SHARPNESS * (intensity - THRESHOLD)))
            goal = target_ref[0, r : r + edge, :].astype(jnp.float32)
            value = (2.0 * SHARPNESS) * (resist - goal) * resist * (1.0 - resist)
            slope[r : r + edge, :] = value.astype(BF16)

    def adjoint(field):
        need(11, 12)
        low = dot(up_cols[: 2 * g, :], slope[...])
        low = low[:g] + low[g:]
        low = dot(jnp.concatenate(split(low), axis=0), down_cols[...])
        low = (low[:g, : 2 * g] + low[:g, 2 * g :]) + low[g:, : 2 * g]
        weighted = field * jnp.concatenate([jnp.concatenate([low] * quarters, axis=1)] * 2, axis=0)
        high, rest = split(weighted)
        back = dot(row_back[...], high)
        back = (back[: 2 * f] + back[2 * f :]) + dot(row_back[: 2 * f, :], rest)
        tall = jnp.concatenate(
            [
                jnp.concatenate([back[:f, 4 * f * k : 4 * f * (k + 1)], back[f:, 4 * f * k : 4 * f * (k + 1)]], axis=1)
                for k in range(quarters)
            ],
            axis=0,
        )
        m = quarters * f
        turned = dot(jnp.concatenate(split(tall), axis=0), lane_back[...])
        turned = (turned[:m, : 4 * f] + turned[:m, 4 * f :]) + turned[m:, : 4 * f]
        first, second = h_one * turned, h_two * turned
        real = jnp.zeros((f, 4 * f), jnp.float32)
        imag = jnp.zeros((f, 4 * f), jnp.float32)
        for k in range(quarters):
            real = real + first[k * f : (k + 1) * f] * portions[k]
            imag = imag + second[k * f : (k + 1) * f] * portions[k]
        real = real + pltpu.roll(real, 2 * f, 1)
        real = real + pltpu.roll(real, f, 1)
        imag = imag + pltpu.roll(imag, 2 * f, 1)
        imag = imag + pltpu.roll(imag, f, 1)
        return jnp.where(is_real, real, imag)

    def tails(packed):
        need(15)
        out = dot(jnp.concatenate(split(packed), axis=1), tail_tab[...])
        return jnp.concatenate([out[:, :n], out[:, n:]], axis=0)

    def band_tails(which, begin):
        packed = jnp.concatenate([unfolded(adj_in[to]) for to in which], axis=0)
        packed = jnp.concatenate(split(packed), axis=1)
        real = dot(packed, tail_tab[:, begin : begin + edge])
        imag = dot(packed, tail_tab[:, n + begin : n + begin + edge])
        return [
            jnp.concatenate([real[i * f : (i + 1) * f], imag[i * f : (i + 1) * f]], axis=0) for i in range(len(which))
        ]

    field = fields(*band_one)
    write_slope(field)
    packed = adjoint(field)
    adj[...] = folded(packed)
    start(plan["adj"] + plan["v", 1, 1] + plan["v", 0, 0] + plan["v", 0, 1])
    arrived(plan["vx"])
    for v, h in corners:
        @pl.when(both(cross[h], above[v]))
        def _(v=v, h=h):
            for i in range(2):
                c7[i, v, h] = md[i, bands[v], bands[h]] + q[i, v, h]
    start(plan["cf"])

    need(13, 14)
    turned = dot(row_flip[...], jnp.concatenate(split(packed), axis=0))
    mirrored = dot(jnp.concatenate(split(turned), axis=1), lane_flip[...])
    band = band_next - STEP_SIZE * (packed + mirrored)
    arrived(plan["spec"])
    incoming = spec_in[0]
    for to in range(1, 8):
        incoming = incoming + spec_in[to]
    band = band + unfolded(incoming)
    field = fields(jnp.where(is_real, band, pltpu.roll(band, f, 1)), jnp.where(is_real, pltpu.roll(band, 3 * f, 1), band))
    write_slope(field)
    arrived(plan["c3"])
    for v, h in corners:
        @pl.when(both(pair[h], above[v]))
        def _(v=v, h=h):
            c4[:, v, h] = c2[:, v, h] + c3[:, v, h]
            q[:, v, h, pl.ds((1 - h) * half, half), :] = c1[:, v, h] + c3[:, v, h]
    start(plan["c5"])


    last = adjoint(field)
    tail_last = tails(last)
    tail_own = tails(packed)
    arrived(plan["adj"])

    def joined(tail, from_left, from_right):
        return share_col * jnp.concatenate(
            [tail[:, :edge] + from_left, tail[:, edge:far], tail[:, far:] + from_right], axis=1
        )

    at_left, at_right = band_tails((0, 4, 6), far), band_tails((1, 5, 7), 0)
    sides = dot(
        jnp.concatenate(split(jnp.concatenate([unfolded(adj_in[2]), unfolded(adj_in[3])], axis=0)), axis=1), tail_tab[...]
    )
    ends = [jnp.concatenate([sides[i * f : (i + 1) * f, :n], sides[i * f : (i + 1) * f, n:]], axis=0) for i in range(2)]
    sum_own = joined(tail_own, at_left[0], at_right[0])
    sum_end = [joined(ends[i], at_left[1 + i], at_right[1 + i]) for i in range(2)]
    need(16)
    base = -0.125 * tail_own - STEP_SIZE * tail_last
    inner_m = stacked(base - 0.125 * sum_own)
    inner_d = stacked(STEP_SIZE * (sum_own - tail_own))
    for r in range(0, n, edge):
        rows = slice(r, r + edge)
        by = share_row(r)
        if by is None:
            grad_m = dot(grad_rows[rows, :], inner_m)
            grad_d = dot(grad_rows[rows, :], inner_d)
        else:
            other = sum_end[0] if r == 0 else sum_end[1]
            across = dot(grad_rows[far:, :] if r == 0 else grad_rows[:edge, :], stacked(by * other))
            grad_m = dot(grad_rows[rows, :], stacked(base - (0.125 * by) * sum_own)) - 0.125 * across
            grad_d = dot(grad_rows[rows, :], stacked(STEP_SIZE * (by * sum_own - tail_own))) + STEP_SIZE * across
        m, d = md[0, rows, :], md[1, rows, :]
        cover = scaled(share_col, by)
        mask_out[0, rows, :] = cover * (m + 0.625 * d) - 0.375 * d + grad_m
        dual_out[0, rows, :] = (1.5 * m + 0.75 * d) * (1.0 - cover) + grad_d

    def settle(rows, cols, by, m, d):
        mask_out[0, rows, cols] = mask_out[0, rows, cols] + by * (m + 0.625 * d)
        dual_out[0, rows, cols] = dual_out[0, rows, cols] - by * (1.5 * m + 0.75 * d)

    arrived(plan["c5"] + plan["hc"] + plan["vc"] + plan["cf"])
    for v, h in corners:
        @pl.when(both(pair[h], above[v]))
        def _(v=v, h=h):
            q[:, v, h, pl.ds(h * half, half), :] = c5[:, v, h] - md[:, piece(v, h), bands[h]]

        @pl.when(both(cross[h], above[v]))
        def _(v=v, h=h):
            q[:, v, h] = q[:, v, h] + q2[:, v, h]

        @pl.when(jnp.logical_or(beside[h], above[v]))
        def _(v=v, h=h):
            settle(bands[v], bands[h], share_end[v] * share_side[h], q[0, v, h], q[1, v, h])
    arrived(plan["h", 0] + plan["h", 1])
    for h in range(2):
        @pl.when(beside[h])
        def _(h=h):
            settle(middle, bands[h], share_side[h], hr[0, h], hr[1, h])
    arrived([entry for i in range(2) for part in range(2) for entry in plan["v", i, part]])
    for v in range(2):
        @pl.when(above[v])
        def _(v=v):
            settle(bands[v], middle, share_end[v], vr[0, v], vr[1, v])
    for entries in plan.values():
        sent(entries)


def write_out(*refs):
    sources, targets, sem = refs[:2], refs[2:4], refs[4]
    copies = [pltpu.make_async_copy(a, b, sem.at[i]) for i, (a, b) in enumerate(zip(sources, targets))]
    for copy in copies:
        copy.start()
    for copy in copies:
        copy.wait()


def per_device(count, mask_init, dual_init, target, kernels, weights):
    n = mask_init.shape[-1]
    edge = INTERSECTION
    f = int(round(kernels.shape[-1] ** 0.5))
    tables = [jnp.asarray(t) for t in host_tables(n, f)]
    f32 = jnp.float32
    whole = pl.BlockSpec(memory_space=pltpu.VMEM)
    far_memory = pl.BlockSpec(memory_space=pltpu.HBM)
    arrays = (mask_init, dual_init, target, kernels, weights, *tables)
    tile = jax.ShapeDtypeStruct((1, n, n), f32)
    inner = n - 2 * edge
    half = edge // 2
    results = pl.pallas_call(
        functools.partial(body, n, f, edge, count),
        out_shape=(tile, tile),
        in_specs=[far_memory] * len(arrays),
        out_specs=(whole, whole),
        scratch_shapes=[
            pltpu.SMEM(a.shape, a.dtype) if i == 4 else pltpu.VMEM(a.shape, a.dtype)
            for i, a in enumerate(arrays) if i >= 2
        ]
        + [
            pltpu.VMEM((2, n, n), f32),
            pltpu.VMEM((kernels.shape[0] // 2 * f, 4 * f), f32),
            pltpu.SemaphoreType.DMA((len(arrays),)),
            pltpu.VMEM((2, 2, inner, edge), f32),
            pltpu.VMEM((2, 2, edge, inner), f32),
            pltpu.VMEM((2, 2, 2, edge, edge), f32),
            pltpu.VMEM((2, 2, 2, edge, edge), f32),
            pltpu.VMEM((2, 2, 2, edge, edge), f32),
        ]
        + [pltpu.VMEM((2, 2, 2, half, edge), f32)] * 5
        + [pltpu.VMEM((n, n), BF16)] * 4
        + [
            pltpu.VMEM((8, f // 2, 4 * f), f32),
            pltpu.VMEM((8, f // 2, 4 * f), f32),
            pltpu.VMEM((f // 2, 4 * f), f32),
            pltpu.VMEM((8, f // 2, 4 * f), f32),
            pltpu.SemaphoreType.REGULAR((8,)),
            pltpu.SemaphoreType.DMA((76,)),
            pltpu.SemaphoreType.DMA((76,)),
        ],
        compiler_params=pltpu.CompilerParams(
            collective_id=0, has_side_effects=True, vmem_limit_bytes=48 * 1024 * 1024
        ),
    )(*[pltpu.with_memory_space_constraint(a, pltpu.HBM) for a in arrays])
    return pl.pallas_call(
        write_out,
        out_shape=(tile, tile),
        in_specs=[pl.BlockSpec(memory_space=pl.ANY)] * 2,
        out_specs=[far_memory] * 2,
        scratch_shapes=[pltpu.SemaphoreType.DMA((2,))],
        compiler_params=pltpu.CompilerParams(vmem_limit_bytes=1 << 20),
    )(*results)


def solution(mesh):
    tile = P(("region", "ty"), None, None)
    return jax.shard_map(
        functools.partial(per_device, mesh.shape["ty"]),
        mesh=mesh,
        in_specs=(tile, tile, tile, P(), P()),
        out_specs=(tile, tile),
        check_vma=False,
    )
```

```python
import functools

import jax
import jax.numpy as jnp
import numpy as np
from jax import lax
from jax.experimental import pallas as pl
from jax.experimental.pallas import tpu as pltpu
from jax.sharding import PartitionSpec as P

GRID_COLS = 4
INTERSECTION = 128
SHARPNESS = 8.0
THRESHOLD = 0.3
STEP_SIZE = 0.25
PENALTY = 1.0
MESH = pl.DeviceIdType.MESH
BF16 = jnp.bfloat16


def split_host(table):
    table = table.astype(np.float32)
    high = table.astype(BF16)
    low = (table - high.astype(np.float32)).astype(BF16)
    return high, low


def host_tables(n, f):
    g = 2 * f
    freq = np.arange(f) - f // 2
    phase = 2.0 * np.pi * ((freq[:, None] * np.arange(n)[None, :]) % n) / n
    cos, sin = np.cos(phase), -np.sin(phase)
    rows = np.concatenate([cos, sin], 0)
    rows_hi, rows_lo = split_host(rows)
    row_side = np.concatenate([rows_hi, rows_lo], 0)
    col_wide = np.concatenate([np.tile(cos.T, (1, 4)), np.tile(sin.T, (1, 4))], 1)
    col_side = split_host(col_wide)[0]
    coarse = 2.0 * np.pi * ((np.arange(g)[:, None] * freq[None, :]) % g) / g
    er, ei = np.cos(coarse), np.sin(coarse)
    pair = np.eye(2)
    to_real = np.kron(pair, np.concatenate([er.T, -ei.T], 0))
    to_imag = np.kron(pair, np.concatenate([ei.T, er.T], 0))
    lane_turn = np.concatenate([to_real, to_imag], 1)
    lane_fwd = np.concatenate(split_host(lane_turn / (n * n)), 1)
    lane_back = np.concatenate(split_host(lane_turn.T), 1)
    row_turn = np.concatenate([np.concatenate([er, -ei], 1), np.concatenate([ei, er], 1)], 0)
    turn_hi, turn_lo = split_host(row_turn)
    row_fwd = np.concatenate([turn_hi, turn_lo, turn_hi, turn_lo], 1)
    row_back = np.concatenate(split_host(row_turn.T), 0)
    half = np.arange(-(f - 1), f)
    angle = np.arange(n)[:, None] * f * 2 - np.arange(g)[None, :] * n
    spread = np.cos(2.0 * np.pi * ((angle[..., None] * half) % (n * g)) / (n * g)).sum(-1) / g
    s_hi, s_lo = split_host(spread)
    up_cols = np.concatenate([s_hi.T, s_lo.T, s_hi.T, s_lo.T], 0)
    down_cols = np.concatenate([s_hi, s_hi, s_lo, s_lo], 1)
    scale = 2.0 / (n * n)
    c_hi, c_lo = split_host(cos * scale)
    t_hi, t_lo = split_host(sin * scale)
    tail_r = np.concatenate([c_hi, t_hi, c_lo, t_lo], 0)
    tail_i = np.concatenate([-t_hi, c_hi, -t_lo, c_lo], 0)
    tail = np.concatenate([tail_r, tail_i], 1)
    tail_tab = np.concatenate([tail, tail], 0)
    grad_rows = np.concatenate([rows_hi.T, rows_lo.T, rows_hi.T, rows_lo.T], 1)
    turn = np.zeros((f, f))
    turn[np.arange(1, f), f - np.arange(1, f)] = 1.0
    row_flip = np.concatenate([turn, turn], 1)
    none = np.zeros((f, f))
    one_flip = np.concatenate(
        [np.concatenate([turn, none, turn, none], 1), np.concatenate([none, -turn, none, -turn], 1),
         np.zeros((2 * f, 4 * f))], 0,
    )
    lane_flip = np.concatenate([one_flip, one_flip], 0)
    tables = (
        row_side, col_side, lane_fwd, row_fwd, up_cols, down_cols, row_back, lane_back,
        row_flip, lane_flip, tail_tab, grad_rows,
    )
    return [np.asarray(t, dtype=BF16) for t in tables]


def dot(a, b):
    return lax.dot_general(a, b, (((1,), (0,)), ((), ())), preferred_element_type=jnp.float32)


def split(x):
    high = x.astype(BF16)
    return high, (x - high.astype(jnp.float32)).astype(BF16)


def stacked(x):
    high, low = split(x)
    return jnp.concatenate([high, high, low, low], axis=0)


INPUTS = 17
ORDER = (1, 0, 5, 6, 4, 3, 7, 8, 9, 2, 10, 11, 12, 13, 14, 15, 16)


def body(n, f, edge, count, *refs):
    ins, refs = refs[:INPUTS], refs[INPUTS:]
    mask_out, dual_out = refs[:2]
    refs = refs[2:]
    held, refs = refs[: INPUTS - 2], refs[INPUTS - 2 :]
    target_ref, k_ref, w_ref = held[:3]
    (
        row_side, col_side, lane_fwd, row_fwd, up_cols, down_cols, row_back, lane_back,
        row_flip, lane_flip, tail_tab, grad_rows,
    ) = held[3:]
    (
        md, h_sc, load_sem, hr, vr, q, q2, c7, c1, c2, c3, c4, c5, mb, xb, yb, slope, spec, spec_in, adj, adj_in,
        ready, send_sem, recv_sem,
    ) = refs
    places = [md.at[0], md.at[1], *held]
    sources = [ins[0].at[0], ins[1].at[0], *ins[2:]]
    loads = [pltpu.make_async_copy(src, dst, load_sem.at[i]) for i, (src, dst) in enumerate(zip(sources, places))]
    far = n - edge
    half = edge // 2
    g = 2 * f
    me = lax.axis_index("ty")
    row, col = me // GRID_COLS, me % GRID_COLS
    grid_rows = count // GRID_COLS
    left, right = col > 0, col < GRID_COLS - 1
    upper, lower = row > 0, row < grid_rows - 1
    both = jnp.logical_and
    near = [
        (-1, left), (1, right), (-GRID_COLS, upper), (GRID_COLS, lower),
        (-GRID_COLS - 1, both(upper, left)), (-GRID_COLS + 1, both(upper, right)),
        (GRID_COLS - 1, both(lower, left)), (GRID_COLS + 1, both(lower, right)),
    ]
    opposite = [1, 0, 3, 2, 7, 6, 5, 4]
    beside, above = (left, right), (upper, lower)
    lone_h, lone_v = [jnp.logical_not(x) for x in beside], [jnp.logical_not(x) for x in above]
    pair = (both(left, col % 2 == 1), both(right, col % 2 == 0))
    cross = [both(beside[h], jnp.logical_not(pair[h])) for h in range(2)]

    barrier = pltpu.get_barrier_semaphore()
    even = col % 2 == 0
    odd = jnp.logical_not(even)
    sure = [both(near[to][1], even) if to < 2 else near[to][1] for to in range(8)]
    asked = [both(near[to][1], odd) if to < 2 else near[to][1] for to in range(8)]
    earlier, later = (0, 1, 2, 4, 5), (0, 1, 3, 6, 7)
    for to in later:
        @pl.when(asked[to])
        def _(shift=near[to][0]):
            pl.semaphore_signal(barrier, inc=1, device_id={"ty": me + shift}, device_id_type=MESH)

    for i in ORDER[:2]:
        loads[i].start()

    counter = [0]

    def remote(src, dst, to, send_if, recv_if):
        index = counter[0]
        counter[0] += 1
        copy = pltpu.make_async_remote_copy(
            src_ref=src, dst_ref=dst, send_sem=send_sem.at[index], recv_sem=recv_sem.at[index],
            device_id={"ty": me + near[to][0]}, device_id_type=MESH,
        )
        return copy, send_if, recv_if, to

    def start(entries, which=None, known=None):
        for entry in entries:
            if which is None or entry[3] in which:
                pl.when(entry[1] if known is None or entry[3] > 1 else both(entry[1], known))(entry[0].start)

    def arrived(entries):
        for entry in entries:
            pl.when(entry[2])(entry[0].wait_recv)

    def sent(entries):
        for entry in entries:
            pl.when(entry[1])(entry[0].wait_send)

    begin = (0, far)
    bands = (pl.ds(0, edge), pl.ds(far, edge))
    middle = pl.ds(edge, far - edge)
    corners = [(v, h) for v in range(2) for h in range(2)]

    def piece(v, part):
        return pl.ds(begin[v] + part * half, half)

    raw = (ins[0].at[0], ins[1].at[0])
    plan = {}
    for i in range(2):
        for part in range(2):
            cols = pl.ds(edge + part * (far - edge) // 2, (far - edge) // 2)
            into = pl.ds(part * (far - edge) // 2, (far - edge) // 2)
            plan["v", i, part] = [
                remote(raw[i].at[bands[v], cols], vr.at[i, 1 - v, :, into], 2 + v, above[v], above[1 - v])
                for v in range(2)
            ]
        plan["h", i] = [
            remote(raw[i].at[middle, bands[h]], hr.at[i, 1 - h], h, beside[h], beside[1 - h]) for h in range(2)
        ]
    plan["hc"] = [
        remote(
            raw[i].at[bands[v], bands[h]], q.at[i, v, 1 - h], h,
            both(beside[h], lone_v[v]), both(beside[1 - h], lone_v[v]),
        )
        for v, h in corners for i in range(2)
    ]
    for name, side in (("vc", lone_h), ("vx", cross)):
        plan[name] = [
            remote(
                raw[i].at[bands[v], bands[h]], q.at[i, 1 - v, h], 2 + v,
                both(above[v], side[h]), both(above[1 - v], side[h]),
            )
            for v, h in corners for i in range(2)
        ]
    plan["cf"] = [
        remote(c7.at[:, v, h], q2.at[:, v, 1 - h], h, both(cross[h], above[v]), both(cross[1 - h], above[v]))
        for v, h in corners
    ]
    plan["c1"] = [
        remote(
            raw[i].at[piece(v, h), bands[h]], c1.at[i, v, 1 - h], h,
            both(pair[h], above[v]), both(pair[1 - h], above[v]),
        )
        for v, h in corners for i in range(2)
    ]
    plan["c3"] = [
        remote(c2.at[:, v, h], c3.at[:, 1 - v, h], 2 + v, both(pair[h], above[v]), both(pair[h], above[1 - v]))
        for v, h in corners
    ]
    plan["c5"] = [
        remote(c4.at[:, v, h], c5.at[:, v, 1 - h], h, both(pair[h], above[v]), both(pair[1 - h], above[v]))
        for v, h in corners
    ]
    plan["spec"] = [
        remote(spec.at[to], spec_in.at[opposite[to]], to, near[to][1], near[opposite[to]][1]) for to in range(8)
    ]
    plan["adj"] = [remote(adj, adj_in.at[opposite[to]], to, near[to][1], near[opposite[to]][1]) for to in range(8)]

    expected = sum(sure[to].astype(jnp.int32) for to in earlier)

    @pl.when(expected > 0)
    def _():
        pl.semaphore_wait(barrier, expected)

    for to in earlier:
        @pl.when(sure[to])
        def _(to=to):
            pl.semaphore_signal(
                ready.at[opposite[to]], inc=1, device_id={"ty": me + near[to][0]}, device_id_type=MESH
            )
    opening = plan["c1"] + plan["vx"] + plan["vc"] + plan["hc"]
    start(opening, earlier, even)
    for i in ORDER[2:]:
        loads[i].start()

    for to in range(8):
        @pl.when(jnp.logical_not(near[to][1]))
        def _(to=to):
            spec_in[to] = jnp.zeros((f // 2, 4 * f), jnp.float32)
            adj_in[to] = jnp.zeros((f // 2, 4 * f), jnp.float32)


    waited = set()

    def need(*which):
        for i in which:
            if i not in waited:
                waited.add(i)
                loads[i].wait()

    def meet(*which):
        for to in which:
            @pl.when(asked[to])
            def _(to=to):
                pl.semaphore_wait(ready.at[to], 1)

    meet(0)
    start(opening, (0,), odd)
    need(0, 1)
    up_f, down_f = upper.astype(jnp.float32), lower.astype(jnp.float32)
    left_f, right_f = left.astype(jnp.float32), right.astype(jnp.float32)
    at_col = lax.broadcasted_iota(jnp.int32, (1, n), 1)
    share_col = jnp.where(at_col < edge, 1.0 - 0.5 * left_f, jnp.where(at_col >= far, 1.0 - 0.5 * right_f, 1.0))
    share_side = (1.0 - 0.5 * left_f, 1.0 - 0.5 * right_f)
    share_end = (1.0 - 0.5 * up_f, 1.0 - 0.5 * down_f)

    def share_row(r):
        return share_end[0] if r == 0 else share_end[1] if r == far else None

    def scaled(x, by):
        return x if by is None else x * by

    lane = lax.broadcasted_iota(jnp.int32, (1, 4 * f), 1)
    low_half = lane < 2 * f
    is_real = (lane // f) % 2 == 0

    for r in range(0, n, edge):
        rows = slice(r, r + edge)
        m, d = md[0, rows, :], md[1, rows, :]
        y = (m + d) * scaled(0.5 * share_col, share_row(r))
        mb[rows, :] = m.astype(BF16)
        yb[rows, :] = y.astype(BF16)
        xb[rows, :] = (0.5 * m - 0.25 * d + y).astype(BF16)

    meet(3)
    start(opening, (3,))
    meet(1)
    start(opening, (1,), odd)

    need(5, 6)
    top_part = dot(row_side[:g, far:], yb[:edge, :]).astype(BF16)
    end_part = dot(row_side[:g, :edge], yb[far:, :]).astype(BF16)
    left_part = dot(row_side[:g, :], yb[:, :edge]).astype(BF16)
    right_part = dot(row_side[:g, :], yb[:, far:]).astype(BF16)

    def to_band(grid):
        real = grid[:f, : 4 * f] - grid[f:, 4 * f :]
        imag = grid[:f, 4 * f :] + grid[f:, : 4 * f]
        return real, imag

    def packed_band(grid):
        real, imag = to_band(grid)
        return jnp.where(is_real, real, imag)

    def folded(x):
        return jnp.where(low_half, x[: f // 2], x[f // 2 :])

    def unfolded(x):
        turned = pltpu.roll(x, 2 * f, 1)
        return jnp.concatenate([jnp.where(low_half, x, turned), jnp.where(low_half, turned, x)], axis=0)

    at_left = dot(
        jnp.concatenate([left_part, top_part[:, :edge], end_part[:, :edge]], axis=0), col_side[far:, :]
    )
    at_right = dot(
        jnp.concatenate([right_part, top_part[:, far:], end_part[:, far:]], axis=0), col_side[:edge, :]
    )
    at_ends = dot(jnp.concatenate([top_part, end_part], axis=0), col_side[...])
    for i, to in enumerate((0, 4, 6)):
        spec[to] = folded(packed_band(at_left[i * g : (i + 1) * g]))
    for i, to in enumerate((1, 5, 7)):
        spec[to] = folded(packed_band(at_right[i * g : (i + 1) * g]))
    for i, to in enumerate((2, 3)):
        spec[to] = folded(packed_band(at_ends[i * g : (i + 1) * g]))
    arrived(plan["c1"])
    for v, h in corners:
        @pl.when(both(pair[h], above[v]))
        def _(v=v, h=h):
            c2[:, v, h] = md[:, piece(v, 1 - h), bands[h]] + c1[:, v, h]
    meet(6, 7)
    start(plan["spec"] + plan["c3"] + plan["v", 1, 0] + plan["h", 1] + plan["h", 0])

    part = dot(row_side[...], jnp.concatenate([mb[...], xb[...]], axis=1))
    part = part[:g] + part[g:]
    first_part, next_part = part[:, :n], part[:, n:]
    grid = dot(jnp.concatenate([*split(first_part), next_part.astype(BF16)], axis=0), col_side[...])
    band_one = to_band(grid[:g] + grid[g : 2 * g])
    band_next = packed_band(grid[2 * g :])

    need(4, 3)
    quarters = w_ref.shape[0] // 2
    total = w_ref[0]
    for k in range(1, w_ref.shape[0]):
        total = total + w_ref[k]
    portions = [
        jnp.where(low_half, w_ref[2 * k], w_ref[2 * k + 1]) / jnp.full((1, 4 * f), total, jnp.float32)
        for k in range(quarters)
    ]
    for k in range(quarters):
        rows_of = []
        for j in range(4):
            flat = k_ref.at[2 * k + j // 2]
            rows_of.append(
                jnp.concatenate([flat[j % 2 : j % 2 + 1, 4 * f * a : 4 * f * (a + 1)] for a in range(f // 4)], axis=0)
            )
        for b in range(4):
            value = rows_of[b]
            for j in range(4):
                if j != b:
                    value = jnp.where(lane // f == j, pltpu.roll(rows_of[j], (j - b) % 4 * f, 1), value)
            h_sc[pl.ds(k * f + b, f // 4, stride=4), :] = value
    h_one = h_sc[...]
    h_two = jnp.where(is_real, -pltpu.roll(h_one, 3 * f, 1), pltpu.roll(h_one, f, 1))

    def fields(real, imag):
        need(7, 8)
        w = 8 * f
        real = jnp.concatenate([real] * quarters, axis=0)
        imag = jnp.concatenate([imag] * quarters, axis=0)
        gated = h_one * real + h_two * imag
        turned = dot(jnp.concatenate(split(gated), axis=0), lane_fwd[...])
        m = quarters * f
        turned = (turned[:m, :w] + turned[:m, w:]) + turned[m:, :w]
        wide = jnp.concatenate(
            [
                jnp.concatenate([turned[k * f : (k + 1) * f, : 4 * f], turned[k * f : (k + 1) * f, 4 * f :]], axis=0)
                for k in range(quarters)
            ],
            axis=1,
        )
        return dot(row_fwd[...], stacked(wide))

    def write_slope(field):
        need(9, 10, 2)
        energy = field[:g] * field[:g] + field[g:] * field[g:]
        summed = energy[:, : 2 * g] * portions[0]
        for k in range(1, quarters):
            summed = summed + energy[:, 2 * g * k : 2 * g * (k + 1)] * portions[k]
        summed = summed + pltpu.roll(summed, g, 1)
        level = dot(jnp.concatenate(split(summed), axis=1), up_cols[...])
        high, rest = split(level)
        level = jnp.concatenate([high, rest, high, rest], axis=0)
        for r in range(0, n, edge):
            intensity = dot(down_cols[r : r + edge, :], level)
            resist = 1.0 / (1.0 + jnp.exp(-SHARPNESS * (intensity - THRESHOLD)))
            goal = target_ref[0, r : r + edge, :].astype(jnp.float32)
            value = (2.0 * SHARPNESS) * (resist - goal) * resist * (1.0 - resist)
            slope[r : r + edge, :] = value.astype(BF16)

    def adjoint(field):
        need(11, 12)
        low = dot(up_cols[: 2 * g, :], slope[...])
        low = low[:g] + low[g:]
        low = dot(jnp.concatenate(split(low), axis=0), down_cols[...])
        low = (low[:g, : 2 * g] + low[:g, 2 * g :]) + low[g:, : 2 * g]
        weighted = field * jnp.concatenate([jnp.concatenate([low] * quarters, axis=1)] * 2, axis=0)
        high, rest = split(weighted)
        back = dot(row_back[...], high)
        back = (back[: 2 * f] + back[2 * f :]) + dot(row_back[: 2 * f, :], rest)
        tall = jnp.concatenate(
            [
                jnp.concatenate([back[:f, 4 * f * k : 4 * f * (k + 1)], back[f:, 4 * f * k : 4 * f * (k + 1)]], axis=1)
                for k in range(quarters)
            ],
            axis=0,
        )
        m = quarters * f
        turned = dot(jnp.concatenate(split(tall), axis=0), lane_back[...])
        turned = (turned[:m, : 4 * f] + turned[:m, 4 * f :]) + turned[m:, : 4 * f]
        first, second = h_one * turned, h_two * turned
        real = jnp.zeros((f, 4 * f), jnp.float32)
        imag = jnp.zeros((f, 4 * f), jnp.float32)
        for k in range(quarters):
            real = real + first[k * f : (k + 1) * f] * portions[k]
            imag = imag + second[k * f : (k + 1) * f] * portions[k]
        real = real + pltpu.roll(real, 2 * f, 1)
        real = real + pltpu.roll(real, f, 1)
        imag = imag + pltpu.roll(imag, 2 * f, 1)
        imag = imag + pltpu.roll(imag, f, 1)
        return jnp.where(is_real, real, imag)

    def tails(packed):
        need(15)
        out = dot(jnp.concatenate(split(packed), axis=1), tail_tab[...])
        return jnp.concatenate([out[:, :n], out[:, n:]], axis=0)

    def band_tails(which, begin):
        packed = jnp.concatenate([unfolded(adj_in[to]) for to in which], axis=0)
        packed = jnp.concatenate(split(packed), axis=1)
        real = dot(packed, tail_tab[:, begin : begin + edge])
        imag = dot(packed, tail_tab[:, n + begin : n + begin + edge])
        return [
            jnp.concatenate([real[i * f : (i + 1) * f], imag[i * f : (i + 1) * f]], axis=0) for i in range(len(which))
        ]

    field = fields(*band_one)
    write_slope(field)
    packed = adjoint(field)
    adj[...] = folded(packed)
    start(plan["adj"] + plan["v", 1, 1] + plan["v", 0, 0] + plan["v", 0, 1])
    arrived(plan["vx"])
    for v, h in corners:
        @pl.when(both(cross[h], above[v]))
        def _(v=v, h=h):
            for i in range(2):
                c7[i, v, h] = md[i, bands[v], bands[h]] + q[i, v, h]
    start(plan["cf"])

    need(13, 14)
    turned = dot(row_flip[...], jnp.concatenate(split(packed), axis=0))
    mirrored = dot(jnp.concatenate(split(turned), axis=1), lane_flip[...])
    band = band_next - STEP_SIZE * (packed + mirrored)
    arrived(plan["spec"])
    incoming = spec_in[0]
    for to in range(1, 8):
        incoming = incoming + spec_in[to]
    band = band + unfolded(incoming)
    field = fields(jnp.where(is_real, band, pltpu.roll(band, f, 1)), jnp.where(is_real, pltpu.roll(band, 3 * f, 1), band))
    write_slope(field)
    arrived(plan["c3"])
    for v, h in corners:
        @pl.when(both(pair[h], above[v]))
        def _(v=v, h=h):
            c4[:, v, h] = c2[:, v, h] + c3[:, v, h]
            q[:, v, h, pl.ds((1 - h) * half, half), :] = c1[:, v, h] + c3[:, v, h]
    start(plan["c5"])


    last = adjoint(field)
    tail_last = tails(last)
    tail_own = tails(packed)
    arrived(plan["adj"])

    def joined(tail, from_left, from_right):
        return share_col * jnp.concatenate(
            [tail[:, :edge] + from_left, tail[:, edge:far], tail[:, far:] + from_right], axis=1
        )

    at_left, at_right = band_tails((0, 4, 6), far), band_tails((1, 5, 7), 0)
    sides = dot(
        jnp.concatenate(split(jnp.concatenate([unfolded(adj_in[2]), unfolded(adj_in[3])], axis=0)), axis=1), tail_tab[...]
    )
    ends = [jnp.concatenate([sides[i * f : (i + 1) * f, :n], sides[i * f : (i + 1) * f, n:]], axis=0) for i in range(2)]
    sum_own = joined(tail_own, at_left[0], at_right[0])
    sum_end = [joined(ends[i], at_left[1 + i], at_right[1 + i]) for i in range(2)]
    need(16)
    base = -0.125 * tail_own - STEP_SIZE * tail_last
    inner_m = stacked(base - 0.125 * sum_own)
    inner_d = stacked(STEP_SIZE * (sum_own - tail_own))
    for r in range(0, n, edge):
        rows = slice(r, r + edge)
        by = share_row(r)
        if by is None:
            grad_m = dot(grad_rows[rows, :], inner_m)
            grad_d = dot(grad_rows[rows, :], inner_d)
        else:
            other = sum_end[0] if r == 0 else sum_end[1]
            across = dot(grad_rows[far:, :] if r == 0 else grad_rows[:edge, :], stacked(by * other))
            grad_m = dot(grad_rows[rows, :], stacked(base - (0.125 * by) * sum_own)) - 0.125 * across
            grad_d = dot(grad_rows[rows, :], stacked(STEP_SIZE * (by * sum_own - tail_own))) + STEP_SIZE * across
        m, d = md[0, rows, :], md[1, rows, :]
        cover = scaled(share_col, by)
        mask_out[0, rows, :] = cover * (m + 0.625 * d) - 0.375 * d + grad_m
        dual_out[0, rows, :] = (1.5 * m + 0.75 * d) * (1.0 - cover) + grad_d

    def settle(rows, cols, by, m, d):
        mask_out[0, rows, cols] = mask_out[0, rows, cols] + by * (m + 0.625 * d)
        dual_out[0, rows, cols] = dual_out[0, rows, cols] - by * (1.5 * m + 0.75 * d)

    arrived(plan["c5"] + plan["hc"] + plan["vc"] + plan["cf"])
    for v, h in corners:
        @pl.when(both(pair[h], above[v]))
        def _(v=v, h=h):
            q[:, v, h, pl.ds(h * half, half), :] = c5[:, v, h] - md[:, piece(v, h), bands[h]]

        @pl.when(both(cross[h], above[v]))
        def _(v=v, h=h):
            q[:, v, h] = q[:, v, h] + q2[:, v, h]

        @pl.when(jnp.logical_or(beside[h], above[v]))
        def _(v=v, h=h):
            settle(bands[v], bands[h], share_end[v] * share_side[h], q[0, v, h], q[1, v, h])
    arrived(plan["h", 0] + plan["h", 1])
    for h in range(2):
        @pl.when(beside[h])
        def _(h=h):
            settle(middle, bands[h], share_side[h], hr[0, h], hr[1, h])
    arrived(plan["v", 1, 0] + plan["v", 1, 1])
    for v in range(2):
        @pl.when(above[v])
        def _(v=v):
            d = share_end[v] * vr[1, v]
            mask_out[0, bands[v], middle] = mask_out[0, bands[v], middle] + 0.625 * d
            dual_out[0, bands[v], middle] = dual_out[0, bands[v], middle] - 0.75 * d
    final = [("v", 0, 0), ("v", 0, 1)]
    for name, entries in plan.items():
        if name not in final:
            sent(entries)
    width = (far - edge) // 2
    for part, name in enumerate(final):
        arrived(plan[name])
        for v in range(2):
            @pl.when(above[v])
            def _(v=v, part=part):
                cols = pl.ds(edge + part * width, width)
                m = share_end[v] * vr[0, v, :, pl.ds(part * width, width)]
                mask_out[0, bands[v], cols] = mask_out[0, bands[v], cols] + m
                dual_out[0, bands[v], cols] = dual_out[0, bands[v], cols] - 1.5 * m
    for name in final:
        sent(plan[name])


def write_out(*refs):
    sources, targets, sem = refs[:2], refs[2:4], refs[4]
    copies = [pltpu.make_async_copy(a, b, sem.at[i]) for i, (a, b) in enumerate(zip(sources, targets))]
    for copy in copies:
        copy.start()
    for copy in copies:
        copy.wait()


def per_device(count, mask_init, dual_init, target, kernels, weights):
    n = mask_init.shape[-1]
    edge = INTERSECTION
    f = int(round(kernels.shape[-1] ** 0.5))
    tables = [jnp.asarray(t) for t in host_tables(n, f)]
    f32 = jnp.float32
    whole = pl.BlockSpec(memory_space=pltpu.VMEM)
    far_memory = pl.BlockSpec(memory_space=pltpu.HBM)
    arrays = (mask_init, dual_init, target, kernels, weights, *tables)
    tile = jax.ShapeDtypeStruct((1, n, n), f32)
    inner = n - 2 * edge
    half = edge // 2
    results = pl.pallas_call(
        functools.partial(body, n, f, edge, count),
        out_shape=(tile, tile),
        in_specs=[far_memory] * len(arrays),
        out_specs=(whole, whole),
        scratch_shapes=[
            pltpu.SMEM(a.shape, a.dtype) if i == 4 else pltpu.VMEM(a.shape, a.dtype)
            for i, a in enumerate(arrays) if i >= 2
        ]
        + [
            pltpu.VMEM((2, n, n), f32),
            pltpu.VMEM((kernels.shape[0] // 2 * f, 4 * f), f32),
            pltpu.SemaphoreType.DMA((len(arrays),)),
            pltpu.VMEM((2, 2, inner, edge), f32),
            pltpu.VMEM((2, 2, edge, inner), f32),
            pltpu.VMEM((2, 2, 2, edge, edge), f32),
            pltpu.VMEM((2, 2, 2, edge, edge), f32),
            pltpu.VMEM((2, 2, 2, edge, edge), f32),
        ]
        + [pltpu.VMEM((2, 2, 2, half, edge), f32)] * 5
        + [pltpu.VMEM((n, n), BF16)] * 4
        + [
            pltpu.VMEM((8, f // 2, 4 * f), f32),
            pltpu.VMEM((8, f // 2, 4 * f), f32),
            pltpu.VMEM((f // 2, 4 * f), f32),
            pltpu.VMEM((8, f // 2, 4 * f), f32),
            pltpu.SemaphoreType.REGULAR((8,)),
            pltpu.SemaphoreType.DMA((76,)),
            pltpu.SemaphoreType.DMA((76,)),
        ],
        compiler_params=pltpu.CompilerParams(
            collective_id=0, has_side_effects=True, vmem_limit_bytes=48 * 1024 * 1024
        ),
    )(*[pltpu.with_memory_space_constraint(a, pltpu.HBM) for a in arrays])
    return pl.pallas_call(
        write_out,
        out_shape=(tile, tile),
        in_specs=[pl.BlockSpec(memory_space=pl.ANY)] * 2,
        out_specs=[far_memory] * 2,
        scratch_shapes=[pltpu.SemaphoreType.DMA((2,))],
        compiler_params=pltpu.CompilerParams(vmem_limit_bytes=1 << 20),
    )(*results)


def solution(mesh):
    tile = P(("region", "ty"), None, None)
    return jax.shard_map(
        functools.partial(per_device, mesh.shape["ty"]),
        mesh=mesh,
        in_specs=(tile, tile, tile, P(), P()),
        out_specs=(tile, tile),
        check_vma=False,
    )
```

```python
import functools

import jax
import jax.numpy as jnp
import numpy as np
from jax import lax
from jax.experimental import pallas as pl
from jax.experimental.pallas import tpu as pltpu
from jax.sharding import PartitionSpec as P

GRID_COLS = 4
INTERSECTION = 128
SHARPNESS = 8.0
THRESHOLD = 0.3
STEP_SIZE = 0.25
PENALTY = 1.0
MESH = pl.DeviceIdType.MESH
BF16 = jnp.bfloat16


def split_host(table):
    table = table.astype(np.float32)
    high = table.astype(BF16)
    low = (table - high.astype(np.float32)).astype(BF16)
    return high, low


def host_tables(n, f):
    g = 2 * f
    freq = np.arange(f) - f // 2
    phase = 2.0 * np.pi * ((freq[:, None] * np.arange(n)[None, :]) % n) / n
    cos, sin = np.cos(phase), -np.sin(phase)
    rows = np.concatenate([cos, sin], 0)
    rows_hi, rows_lo = split_host(rows)
    row_side = np.concatenate([rows_hi, rows_lo], 0)
    col_wide = np.concatenate([np.tile(cos.T, (1, 4)), np.tile(sin.T, (1, 4))], 1)
    col_side = split_host(col_wide)[0]
    coarse = 2.0 * np.pi * ((np.arange(g)[:, None] * freq[None, :]) % g) / g
    er, ei = np.cos(coarse), np.sin(coarse)
    pair = np.eye(2)
    to_real = np.kron(pair, np.concatenate([er.T, -ei.T], 0))
    to_imag = np.kron(pair, np.concatenate([ei.T, er.T], 0))
    lane_turn = np.concatenate([to_real, to_imag], 1)
    lane_fwd = np.concatenate(split_host(lane_turn / (n * n)), 1)
    lane_back = np.concatenate(split_host(lane_turn.T), 1)
    row_turn = np.concatenate([np.concatenate([er, -ei], 1), np.concatenate([ei, er], 1)], 0)
    turn_hi, turn_lo = split_host(row_turn)
    row_fwd = np.concatenate([turn_hi, turn_lo, turn_hi, turn_lo], 1)
    row_back = np.concatenate(split_host(row_turn.T), 0)
    half = np.arange(-(f - 1), f)
    angle = np.arange(n)[:, None] * f * 2 - np.arange(g)[None, :] * n
    spread = np.cos(2.0 * np.pi * ((angle[..., None] * half) % (n * g)) / (n * g)).sum(-1) / g
    s_hi, s_lo = split_host(spread)
    up_cols = np.concatenate([s_hi.T, s_lo.T, s_hi.T, s_lo.T], 0)
    down_cols = np.concatenate([s_hi, s_hi, s_lo, s_lo], 1)
    scale = 2.0 / (n * n)
    c_hi, c_lo = split_host(cos * scale)
    t_hi, t_lo = split_host(sin * scale)
    tail_r = np.concatenate([c_hi, t_hi, c_lo, t_lo], 0)
    tail_i = np.concatenate([-t_hi, c_hi, -t_lo, c_lo], 0)
    tail = np.concatenate([tail_r, tail_i], 1)
    tail_tab = np.concatenate([tail, tail], 0)
    grad_rows = np.concatenate([rows_hi.T, rows_lo.T, rows_hi.T, rows_lo.T], 1)
    turn = np.zeros((f, f))
    turn[np.arange(1, f), f - np.arange(1, f)] = 1.0
    row_flip = np.concatenate([turn, turn], 1)
    none = np.zeros((f, f))
    one_flip = np.concatenate(
        [np.concatenate([turn, none, turn, none], 1), np.concatenate([none, -turn, none, -turn], 1),
         np.zeros((2 * f, 4 * f))], 0,
    )
    lane_flip = np.concatenate([one_flip, one_flip], 0)
    tables = (
        row_side, col_side, lane_fwd, row_fwd, up_cols, down_cols, row_back, lane_back,
        row_flip, lane_flip, tail_tab, grad_rows,
    )
    return [np.asarray(t, dtype=BF16) for t in tables]


def dot(a, b):
    return lax.dot_general(a, b, (((1,), (0,)), ((), ())), preferred_element_type=jnp.float32)


def split(x):
    high = x.astype(BF16)
    return high, (x - high.astype(jnp.float32)).astype(BF16)


def stacked(x):
    high, low = split(x)
    return jnp.concatenate([high, high, low, low], axis=0)


INPUTS = 17
ORDER = (1, 0, 5, 6, 4, 3, 7, 8, 9, 2, 10, 11, 12, 13, 14, 15, 16)


def body(n, f, edge, count, *refs):
    ins, refs = refs[:INPUTS], refs[INPUTS:]
    mask_out, dual_out = refs[:2]
    refs = refs[2:]
    held, refs = refs[: INPUTS - 2], refs[INPUTS - 2 :]
    target_ref, k_ref, w_ref = held[:3]
    (
        row_side, col_side, lane_fwd, row_fwd, up_cols, down_cols, row_back, lane_back,
        row_flip, lane_flip, tail_tab, grad_rows,
    ) = held[3:]
    (
        md, h_sc, load_sem, hr, vr, q, q2, c7, c1, c2, c3, c4, c5, mb, xb, yb, slope, spec, spec_in, adj, adj_in,
        ready, send_sem, recv_sem,
    ) = refs
    places = [md.at[0], md.at[1], *held]
    sources = [ins[0].at[0], ins[1].at[0], *ins[2:]]
    loads = [pltpu.make_async_copy(src, dst, load_sem.at[i]) for i, (src, dst) in enumerate(zip(sources, places))]
    far = n - edge
    half = edge // 2
    g = 2 * f
    me = lax.axis_index("ty")
    row, col = me // GRID_COLS, me % GRID_COLS
    grid_rows = count // GRID_COLS
    left, right = col > 0, col < GRID_COLS - 1
    upper, lower = row > 0, row < grid_rows - 1
    both = jnp.logical_and
    near = [
        (-1, left), (1, right), (-GRID_COLS, upper), (GRID_COLS, lower),
        (-GRID_COLS - 1, both(upper, left)), (-GRID_COLS + 1, both(upper, right)),
        (GRID_COLS - 1, both(lower, left)), (GRID_COLS + 1, both(lower, right)),
    ]
    opposite = [1, 0, 3, 2, 7, 6, 5, 4]
    beside, above = (left, right), (upper, lower)
    lone_h, lone_v = [jnp.logical_not(x) for x in beside], [jnp.logical_not(x) for x in above]
    pair = (both(left, col % 2 == 1), both(right, col % 2 == 0))
    cross = [both(beside[h], jnp.logical_not(pair[h])) for h in range(2)]

    barrier = pltpu.get_barrier_semaphore()
    even = col % 2 == 0
    odd = jnp.logical_not(even)
    sure = [both(near[to][1], even) if to < 2 else near[to][1] for to in range(8)]
    asked = [both(near[to][1], odd) if to < 2 else near[to][1] for to in range(8)]
    earlier, later = (0, 1, 2, 4, 5), (0, 1, 3, 6, 7)
    for to in later:
        @pl.when(asked[to])
        def _(shift=near[to][0]):
            pl.semaphore_signal(barrier, inc=1, device_id={"ty": me + shift}, device_id_type=MESH)

    for i in ORDER[:2]:
        loads[i].start()

    counter = [0]

    def remote(src, dst, to, send_if, recv_if):
        index = counter[0]
        counter[0] += 1
        copy = pltpu.make_async_remote_copy(
            src_ref=src, dst_ref=dst, send_sem=send_sem.at[index], recv_sem=recv_sem.at[index],
            device_id={"ty": me + near[to][0]}, device_id_type=MESH,
        )
        return copy, send_if, recv_if, to

    def start(entries, which=None, known=None):
        for entry in entries:
            if which is None or entry[3] in which:
                pl.when(entry[1] if known is None or entry[3] > 1 else both(entry[1], known))(entry[0].start)

    def arrived(entries):
        for entry in entries:
            pl.when(entry[2])(entry[0].wait_recv)

    def sent(entries):
        for entry in entries:
            pl.when(entry[1])(entry[0].wait_send)

    begin = (0, far)
    bands = (pl.ds(0, edge), pl.ds(far, edge))
    middle = pl.ds(edge, far - edge)
    corners = [(v, h) for v in range(2) for h in range(2)]

    def piece(v, part):
        return pl.ds(begin[v] + part * half, half)

    raw = (ins[0].at[0], ins[1].at[0])
    plan = {}
    for i in range(2):
        for part in range(2):
            cols = pl.ds(edge + part * (far - edge) // 2, (far - edge) // 2)
            into = pl.ds(part * (far - edge) // 2, (far - edge) // 2)
            plan["v", i, part] = [
                remote(raw[i].at[bands[v], cols], vr.at[i, 1 - v, :, into], 2 + v, above[v], above[1 - v])
                for v in range(2)
            ]
        plan["h", i] = [
            remote(raw[i].at[middle, bands[h]], hr.at[i, 1 - h], h, beside[h], beside[1 - h]) for h in range(2)
        ]
    plan["hc"] = [
        remote(
            raw[i].at[bands[v], bands[h]], q.at[i, v, 1 - h], h,
            both(beside[h], lone_v[v]), both(beside[1 - h], lone_v[v]),
        )
        for v, h in corners for i in range(2)
    ]
    for name, side in (("vc", lone_h), ("vx", cross)):
        plan[name] = [
            remote(
                raw[i].at[bands[v], bands[h]], q.at[i, 1 - v, h], 2 + v,
                both(above[v], side[h]), both(above[1 - v], side[h]),
            )
            for v, h in corners for i in range(2)
        ]
    plan["cf"] = [
        remote(c7.at[:, v, h], q2.at[:, v, 1 - h], h, both(cross[h], above[v]), both(cross[1 - h], above[v]))
        for v, h in corners
    ]
    plan["c1"] = [
        remote(
            raw[i].at[piece(v, h), bands[h]], c1.at[i, v, 1 - h], h,
            both(pair[h], above[v]), both(pair[1 - h], above[v]),
        )
        for v, h in corners for i in range(2)
    ]
    plan["c3"] = [
        remote(c2.at[:, v, h], c3.at[:, 1 - v, h], 2 + v, both(pair[h], above[v]), both(pair[h], above[1 - v]))
        for v, h in corners
    ]
    plan["c5"] = [
        remote(c4.at[:, v, h], c5.at[:, v, 1 - h], h, both(pair[h], above[v]), both(pair[1 - h], above[v]))
        for v, h in corners
    ]
    plan["spec"] = [
        remote(spec.at[to], spec_in.at[opposite[to]], to, near[to][1], near[opposite[to]][1]) for to in range(8)
    ]
    direct = [near[to][1] if to < 4 else both(near[to][1], cross[to % 2]) for to in range(8)]
    plan["adj"] = [remote(adj, adj_in.at[opposite[to]], to, direct[to], direct[opposite[to]]) for to in range(8)]
    plan["pass"] = [
        remote(
            adj_in.at[2 + v], adj_in.at[5 + 2 * v - h], h, both(pair[h], above[v]), both(pair[1 - h], above[v])
        )
        for v, h in corners
    ]

    expected = sum(sure[to].astype(jnp.int32) for to in earlier)

    @pl.when(expected > 0)
    def _():
        pl.semaphore_wait(barrier, expected)

    for to in earlier:
        @pl.when(sure[to])
        def _(to=to):
            pl.semaphore_signal(
                ready.at[opposite[to]], inc=1, device_id={"ty": me + near[to][0]}, device_id_type=MESH
            )
    opening = plan["c1"] + plan["vx"] + plan["vc"] + plan["hc"]
    start(opening, earlier, even)
    for i in ORDER[2:]:
        loads[i].start()

    for to in range(8):
        @pl.when(jnp.logical_not(near[to][1]))
        def _(to=to):
            spec_in[to] = jnp.zeros((f // 2, 4 * f), jnp.float32)
            adj_in[to] = jnp.zeros((f // 2, 4 * f), jnp.float32)


    waited = set()

    def need(*which):
        for i in which:
            if i not in waited:
                waited.add(i)
                loads[i].wait()

    def meet(*which):
        for to in which:
            @pl.when(asked[to])
            def _(to=to):
                pl.semaphore_wait(ready.at[to], 1)

    meet(0)
    start(opening, (0,), odd)
    need(0, 1)
    up_f, down_f = upper.astype(jnp.float32), lower.astype(jnp.float32)
    left_f, right_f = left.astype(jnp.float32), right.astype(jnp.float32)
    at_col = lax.broadcasted_iota(jnp.int32, (1, n), 1)
    share_col = jnp.where(at_col < edge, 1.0 - 0.5 * left_f, jnp.where(at_col >= far, 1.0 - 0.5 * right_f, 1.0))
    share_side = (1.0 - 0.5 * left_f, 1.0 - 0.5 * right_f)
    share_end = (1.0 - 0.5 * up_f, 1.0 - 0.5 * down_f)

    def share_row(r):
        return share_end[0] if r == 0 else share_end[1] if r == far else None

    def scaled(x, by):
        return x if by is None else x * by

    lane = lax.broadcasted_iota(jnp.int32, (1, 4 * f), 1)
    low_half = lane < 2 * f
    is_real = (lane // f) % 2 == 0

    for r in range(0, n, edge):
        rows = slice(r, r + edge)
        m, d = md[0, rows, :], md[1, rows, :]
        y = (m + d) * scaled(0.5 * share_col, share_row(r))
        mb[rows, :] = m.astype(BF16)
        yb[rows, :] = y.astype(BF16)
        xb[rows, :] = (0.5 * m - 0.25 * d + y).astype(BF16)

    meet(3)
    start(opening, (3,))
    meet(1)
    start(opening, (1,), odd)

    need(5, 6)
    top_part = dot(row_side[:g, far:], yb[:edge, :]).astype(BF16)
    end_part = dot(row_side[:g, :edge], yb[far:, :]).astype(BF16)
    left_part = dot(row_side[:g, :], yb[:, :edge]).astype(BF16)
    right_part = dot(row_side[:g, :], yb[:, far:]).astype(BF16)

    def to_band(grid):
        real = grid[:f, : 4 * f] - grid[f:, 4 * f :]
        imag = grid[:f, 4 * f :] + grid[f:, : 4 * f]
        return real, imag

    def packed_band(grid):
        real, imag = to_band(grid)
        return jnp.where(is_real, real, imag)

    def folded(x):
        return jnp.where(low_half, x[: f // 2], x[f // 2 :])

    def unfolded(x):
        turned = pltpu.roll(x, 2 * f, 1)
        return jnp.concatenate([jnp.where(low_half, x, turned), jnp.where(low_half, turned, x)], axis=0)

    at_left = dot(
        jnp.concatenate([left_part, top_part[:, :edge], end_part[:, :edge]], axis=0), col_side[far:, :]
    )
    at_right = dot(
        jnp.concatenate([right_part, top_part[:, far:], end_part[:, far:]], axis=0), col_side[:edge, :]
    )
    at_ends = dot(jnp.concatenate([top_part, end_part], axis=0), col_side[...])
    for i, to in enumerate((0, 4, 6)):
        spec[to] = folded(packed_band(at_left[i * g : (i + 1) * g]))
    for i, to in enumerate((1, 5, 7)):
        spec[to] = folded(packed_band(at_right[i * g : (i + 1) * g]))
    for i, to in enumerate((2, 3)):
        spec[to] = folded(packed_band(at_ends[i * g : (i + 1) * g]))
    meet(6, 7)
    start(plan["spec"])
    arrived(plan["c1"])
    for v, h in corners:
        @pl.when(both(pair[h], above[v]))
        def _(v=v, h=h):
            c2[:, v, h] = md[:, piece(v, 1 - h), bands[h]] + c1[:, v, h]
    start(plan["c3"] + plan["v", 1, 0] + plan["h", 1] + plan["h", 0])

    part = dot(row_side[...], jnp.concatenate([mb[...], xb[...]], axis=1))
    part = part[:g] + part[g:]
    first_part, next_part = part[:, :n], part[:, n:]
    grid = dot(jnp.concatenate([*split(first_part), next_part.astype(BF16)], axis=0), col_side[...])
    band_one = to_band(grid[:g] + grid[g : 2 * g])
    band_next = packed_band(grid[2 * g :])

    need(4, 3)
    quarters = w_ref.shape[0] // 2
    total = w_ref[0]
    for k in range(1, w_ref.shape[0]):
        total = total + w_ref[k]
    portions = [
        jnp.where(low_half, w_ref[2 * k], w_ref[2 * k + 1]) / jnp.full((1, 4 * f), total, jnp.float32)
        for k in range(quarters)
    ]
    for k in range(quarters):
        rows_of = []
        for j in range(4):
            flat = k_ref.at[2 * k + j // 2]
            rows_of.append(
                jnp.concatenate([flat[j % 2 : j % 2 + 1, 4 * f * a : 4 * f * (a + 1)] for a in range(f // 4)], axis=0)
            )
        for b in range(4):
            value = rows_of[b]
            for j in range(4):
                if j != b:
                    value = jnp.where(lane // f == j, pltpu.roll(rows_of[j], (j - b) % 4 * f, 1), value)
            h_sc[pl.ds(k * f + b, f // 4, stride=4), :] = value
    h_one = h_sc[...]
    h_two = jnp.where(is_real, -pltpu.roll(h_one, 3 * f, 1), pltpu.roll(h_one, f, 1))

    def fields(real, imag):
        need(7, 8)
        w = 8 * f
        real = jnp.concatenate([real] * quarters, axis=0)
        imag = jnp.concatenate([imag] * quarters, axis=0)
        gated = h_one * real + h_two * imag
        turned = dot(jnp.concatenate(split(gated), axis=0), lane_fwd[...])
        m = quarters * f
        turned = (turned[:m, :w] + turned[:m, w:]) + turned[m:, :w]
        wide = jnp.concatenate(
            [
                jnp.concatenate([turned[k * f : (k + 1) * f, : 4 * f], turned[k * f : (k + 1) * f, 4 * f :]], axis=0)
                for k in range(quarters)
            ],
            axis=1,
        )
        return dot(row_fwd[...], stacked(wide))

    def write_slope(field):
        need(9, 10, 2)
        energy = field[:g] * field[:g] + field[g:] * field[g:]
        summed = energy[:, : 2 * g] * portions[0]
        for k in range(1, quarters):
            summed = summed + energy[:, 2 * g * k : 2 * g * (k + 1)] * portions[k]
        summed = summed + pltpu.roll(summed, g, 1)
        level = dot(jnp.concatenate(split(summed), axis=1), up_cols[...])
        high, rest = split(level)
        level = jnp.concatenate([high, rest, high, rest], axis=0)
        for r in range(0, n, edge):
            intensity = dot(down_cols[r : r + edge, :], level)
            resist = 1.0 / (1.0 + jnp.exp(-SHARPNESS * (intensity - THRESHOLD)))
            goal = target_ref[0, r : r + edge, :].astype(jnp.float32)
            value = (2.0 * SHARPNESS) * (resist - goal) * resist * (1.0 - resist)
            slope[r : r + edge, :] = value.astype(BF16)

    def adjoint(field):
        need(11, 12)
        low = dot(up_cols[: 2 * g, :], slope[...])
        low = low[:g] + low[g:]
        low = dot(jnp.concatenate(split(low), axis=0), down_cols[...])
        low = (low[:g, : 2 * g] + low[:g, 2 * g :]) + low[g:, : 2 * g]
        weighted = field * jnp.concatenate([jnp.concatenate([low] * quarters, axis=1)] * 2, axis=0)
        high, rest = split(weighted)
        back = dot(row_back[...], high)
        back = (back[: 2 * f] + back[2 * f :]) + dot(row_back[: 2 * f, :], rest)
        tall = jnp.concatenate(
            [
                jnp.concatenate([back[:f, 4 * f * k : 4 * f * (k + 1)], back[f:, 4 * f * k : 4 * f * (k + 1)]], axis=1)
                for k in range(quarters)
            ],
            axis=0,
        )
        m = quarters * f
        turned = dot(jnp.concatenate(split(tall), axis=0), lane_back[...])
        turned = (turned[:m, : 4 * f] + turned[:m, 4 * f :]) + turned[m:, : 4 * f]
        first, second = h_one * turned, h_two * turned
        real = jnp.zeros((f, 4 * f), jnp.float32)
        imag = jnp.zeros((f, 4 * f), jnp.float32)
        for k in range(quarters):
            real = real + first[k * f : (k + 1) * f] * portions[k]
            imag = imag + second[k * f : (k + 1) * f] * portions[k]
        real = real + pltpu.roll(real, 2 * f, 1)
        real = real + pltpu.roll(real, f, 1)
        imag = imag + pltpu.roll(imag, 2 * f, 1)
        imag = imag + pltpu.roll(imag, f, 1)
        return jnp.where(is_real, real, imag)

    def tails(packed):
        need(15)
        out = dot(jnp.concatenate(split(packed), axis=1), tail_tab[...])
        return jnp.concatenate([out[:, :n], out[:, n:]], axis=0)

    def band_tails(which, begin):
        packed = jnp.concatenate([unfolded(adj_in[to]) for to in which], axis=0)
        packed = jnp.concatenate(split(packed), axis=1)
        real = dot(packed, tail_tab[:, begin : begin + edge])
        imag = dot(packed, tail_tab[:, n + begin : n + begin + edge])
        return [
            jnp.concatenate([real[i * f : (i + 1) * f], imag[i * f : (i + 1) * f]], axis=0) for i in range(len(which))
        ]

    field = fields(*band_one)
    write_slope(field)
    packed = adjoint(field)
    adj[...] = folded(packed)
    start(plan["adj"] + plan["v", 1, 1] + plan["v", 0, 0] + plan["v", 0, 1])
    arrived(plan["vx"])
    for v, h in corners:
        @pl.when(both(cross[h], above[v]))
        def _(v=v, h=h):
            for i in range(2):
                c7[i, v, h] = md[i, bands[v], bands[h]] + q[i, v, h]
    start(plan["cf"])

    need(13, 14)
    turned = dot(row_flip[...], jnp.concatenate(split(packed), axis=0))
    mirrored = dot(jnp.concatenate(split(turned), axis=1), lane_flip[...])
    band = band_next - STEP_SIZE * (packed + mirrored)
    arrived(plan["spec"])
    incoming = spec_in[0]
    for to in range(1, 8):
        incoming = incoming + spec_in[to]
    band = band + unfolded(incoming)
    field = fields(jnp.where(is_real, band, pltpu.roll(band, f, 1)), jnp.where(is_real, pltpu.roll(band, 3 * f, 1), band))
    write_slope(field)
    arrived(plan["c3"])
    for v, h in corners:
        @pl.when(both(pair[h], above[v]))
        def _(v=v, h=h):
            c4[:, v, h] = c2[:, v, h] + c3[:, v, h]
            q[:, v, h, pl.ds((1 - h) * half, half), :] = c1[:, v, h] + c3[:, v, h]
    start(plan["c5"])


    last = adjoint(field)
    tail_last = tails(last)
    tail_own = tails(packed)
    arrived(plan["adj"])

    def joined(tail, from_left, from_right):
        return share_col * jnp.concatenate(
            [tail[:, :edge] + from_left, tail[:, edge:far], tail[:, far:] + from_right], axis=1
        )

    start(plan["pass"])
    sides = dot(
        jnp.concatenate(split(jnp.concatenate([unfolded(adj_in[2]), unfolded(adj_in[3])], axis=0)), axis=1), tail_tab[...]
    )
    arrived(plan["pass"])
    at_left, at_right = band_tails((0, 4, 6), far), band_tails((1, 5, 7), 0)
    ends = [jnp.concatenate([sides[i * f : (i + 1) * f, :n], sides[i * f : (i + 1) * f, n:]], axis=0) for i in range(2)]
    sum_own = joined(tail_own, at_left[0], at_right[0])
    sum_end = [joined(ends[i], at_left[1 + i], at_right[1 + i]) for i in range(2)]
    need(16)
    base = -0.125 * tail_own - STEP_SIZE * tail_last
    inner_m = stacked(base - 0.125 * sum_own)
    inner_d = stacked(STEP_SIZE * (sum_own - tail_own))
    for r in range(0, n, edge):
        rows = slice(r, r + edge)
        by = share_row(r)
        if by is None:
            grad_m = dot(grad_rows[rows, :], inner_m)
            grad_d = dot(grad_rows[rows, :], inner_d)
        else:
            other = sum_end[0] if r == 0 else sum_end[1]
            across = dot(grad_rows[far:, :] if r == 0 else grad_rows[:edge, :], stacked(by * other))
            grad_m = dot(grad_rows[rows, :], stacked(base - (0.125 * by) * sum_own)) - 0.125 * across
            grad_d = dot(grad_rows[rows, :], stacked(STEP_SIZE * (by * sum_own - tail_own))) + STEP_SIZE * across
        m, d = md[0, rows, :], md[1, rows, :]
        cover = scaled(share_col, by)
        mask_out[0, rows, :] = cover * (m + 0.625 * d) - 0.375 * d + grad_m
        dual_out[0, rows, :] = (1.5 * m + 0.75 * d) * (1.0 - cover) + grad_d

    def settle(rows, cols, by, m, d):
        mask_out[0, rows, cols] = mask_out[0, rows, cols] + by * (m + 0.625 * d)
        dual_out[0, rows, cols] = dual_out[0, rows, cols] - by * (1.5 * m + 0.75 * d)

    arrived(plan["c5"] + plan["hc"] + plan["vc"] + plan["cf"])
    for v, h in corners:
        @pl.when(both(pair[h], above[v]))
        def _(v=v, h=h):
            q[:, v, h, pl.ds(h * half, half), :] = c5[:, v, h] - md[:, piece(v, h), bands[h]]

        @pl.when(both(cross[h], above[v]))
        def _(v=v, h=h):
            q[:, v, h] = q[:, v, h] + q2[:, v, h]

        @pl.when(jnp.logical_or(beside[h], above[v]))
        def _(v=v, h=h):
            settle(bands[v], bands[h], share_end[v] * share_side[h], q[0, v, h], q[1, v, h])
    arrived(plan["h", 0] + plan["h", 1])
    for h in range(2):
        @pl.when(beside[h])
        def _(h=h):
            settle(middle, bands[h], share_side[h], hr[0, h], hr[1, h])
    arrived(plan["v", 1, 0] + plan["v", 1, 1])
    for v in range(2):
        @pl.when(above[v])
        def _(v=v):
            d = share_end[v] * vr[1, v]
            mask_out[0, bands[v], middle] = mask_out[0, bands[v], middle] + 0.625 * d
            dual_out[0, bands[v], middle] = dual_out[0, bands[v], middle] - 0.75 * d
    final = [("v", 0, 0), ("v", 0, 1)]
    for name, entries in plan.items():
        if name not in final:
            sent(entries)
    width = (far - edge) // 2
    for part, name in enumerate(final):
        arrived(plan[name])
        for v in range(2):
            @pl.when(above[v])
            def _(v=v, part=part):
                cols = pl.ds(edge + part * width, width)
                m = share_end[v] * vr[0, v, :, pl.ds(part * width, width)]
                mask_out[0, bands[v], cols] = mask_out[0, bands[v], cols] + m
                dual_out[0, bands[v], cols] = dual_out[0, bands[v], cols] - 1.5 * m
    for name in final:
        sent(plan[name])


def write_out(*refs):
    sources, targets, sem = refs[:2], refs[2:4], refs[4]
    copies = [pltpu.make_async_copy(a, b, sem.at[i]) for i, (a, b) in enumerate(zip(sources, targets))]
    for copy in copies:
        copy.start()
    for copy in copies:
        copy.wait()


def per_device(count, mask_init, dual_init, target, kernels, weights):
    n = mask_init.shape[-1]
    edge = INTERSECTION
    f = int(round(kernels.shape[-1] ** 0.5))
    tables = [jnp.asarray(t) for t in host_tables(n, f)]
    f32 = jnp.float32
    whole = pl.BlockSpec(memory_space=pltpu.VMEM)
    far_memory = pl.BlockSpec(memory_space=pltpu.HBM)
    arrays = (mask_init, dual_init, target, kernels, weights, *tables)
    tile = jax.ShapeDtypeStruct((1, n, n), f32)
    inner = n - 2 * edge
    half = edge // 2
    results = pl.pallas_call(
        functools.partial(body, n, f, edge, count),
        out_shape=(tile, tile),
        in_specs=[far_memory] * len(arrays),
        out_specs=(whole, whole),
        scratch_shapes=[
            pltpu.SMEM(a.shape, a.dtype) if i == 4 else pltpu.VMEM(a.shape, a.dtype)
            for i, a in enumerate(arrays) if i >= 2
        ]
        + [
            pltpu.VMEM((2, n, n), f32),
            pltpu.VMEM((kernels.shape[0] // 2 * f, 4 * f), f32),
            pltpu.SemaphoreType.DMA((len(arrays),)),
            pltpu.VMEM((2, 2, inner, edge), f32),
            pltpu.VMEM((2, 2, edge, inner), f32),
            pltpu.VMEM((2, 2, 2, edge, edge), f32),
            pltpu.VMEM((2, 2, 2, edge, edge), f32),
            pltpu.VMEM((2, 2, 2, edge, edge), f32),
        ]
        + [pltpu.VMEM((2, 2, 2, half, edge), f32)] * 5
        + [pltpu.VMEM((n, n), BF16)] * 4
        + [
            pltpu.VMEM((8, f // 2, 4 * f), f32),
            pltpu.VMEM((8, f // 2, 4 * f), f32),
            pltpu.VMEM((f // 2, 4 * f), f32),
            pltpu.VMEM((8, f // 2, 4 * f), f32),
            pltpu.SemaphoreType.REGULAR((8,)),
            pltpu.SemaphoreType.DMA((80,)),
            pltpu.SemaphoreType.DMA((80,)),
        ],
        compiler_params=pltpu.CompilerParams(
            collective_id=0, has_side_effects=True, vmem_limit_bytes=48 * 1024 * 1024
        ),
    )(*[pltpu.with_memory_space_constraint(a, pltpu.HBM) for a in arrays])
    return pl.pallas_call(
        write_out,
        out_shape=(tile, tile),
        in_specs=[pl.BlockSpec(memory_space=pl.ANY)] * 2,
        out_specs=[far_memory] * 2,
        scratch_shapes=[pltpu.SemaphoreType.DMA((2,))],
        compiler_params=pltpu.CompilerParams(vmem_limit_bytes=1 << 20),
    )(*results)


def solution(mesh):
    tile = P(("region", "ty"), None, None)
    return jax.shard_map(
        functools.partial(per_device, mesh.shape["ty"]),
        mesh=mesh,
        in_specs=(tile, tile, tile, P(), P()),
        out_specs=(tile, tile),
        check_vma=False,
    )
```

```python
import functools

import jax
import jax.numpy as jnp
import numpy as np
from jax import lax
from jax.experimental import pallas as pl
from jax.experimental.pallas import tpu as pltpu
from jax.sharding import PartitionSpec as P

GRID_COLS = 4
INTERSECTION = 128
SHARPNESS = 8.0
THRESHOLD = 0.3
STEP_SIZE = 0.25
PENALTY = 1.0
MESH = pl.DeviceIdType.MESH
BF16 = jnp.bfloat16


def split_host(table):
    table = table.astype(np.float32)
    high = table.astype(BF16)
    low = (table - high.astype(np.float32)).astype(BF16)
    return high, low


def host_tables(n, f):
    g = 2 * f
    freq = np.arange(f) - f // 2
    phase = 2.0 * np.pi * ((freq[:, None] * np.arange(n)[None, :]) % n) / n
    cos, sin = np.cos(phase), -np.sin(phase)
    rows = np.concatenate([cos, sin], 0)
    rows_hi, rows_lo = split_host(rows)
    row_side = np.concatenate([rows_hi, rows_lo], 0)
    col_wide = np.concatenate([np.tile(cos.T, (1, 4)), np.tile(sin.T, (1, 4))], 1)
    col_side = split_host(col_wide)[0]
    coarse = 2.0 * np.pi * ((np.arange(g)[:, None] * freq[None, :]) % g) / g
    er, ei = np.cos(coarse), np.sin(coarse)
    pair = np.eye(2)
    to_real = np.kron(pair, np.concatenate([er.T, -ei.T], 0))
    to_imag = np.kron(pair, np.concatenate([ei.T, er.T], 0))
    lane_turn = np.concatenate([to_real, to_imag], 1)
    lane_fwd = np.concatenate(split_host(lane_turn / (n * n)), 1)
    lane_back = np.concatenate(split_host(lane_turn.T), 1)
    row_turn = np.concatenate([np.concatenate([er, -ei], 1), np.concatenate([ei, er], 1)], 0)
    turn_hi, turn_lo = split_host(row_turn)
    row_fwd = np.concatenate([turn_hi, turn_lo, turn_hi, turn_lo], 1)
    row_back = np.concatenate(split_host(row_turn.T), 0)
    half = np.arange(-(f - 1), f)
    angle = np.arange(n)[:, None] * f * 2 - np.arange(g)[None, :] * n
    spread = np.cos(2.0 * np.pi * ((angle[..., None] * half) % (n * g)) / (n * g)).sum(-1) / g
    s_hi, s_lo = split_host(spread)
    up_cols = np.concatenate([s_hi.T, s_lo.T, s_hi.T, s_lo.T], 0)
    down_cols = np.concatenate([s_hi, s_hi, s_lo, s_lo], 1)
    scale = 2.0 / (n * n)
    c_hi, c_lo = split_host(cos * scale)
    t_hi, t_lo = split_host(sin * scale)
    tail_r = np.concatenate([c_hi, t_hi, c_lo, t_lo], 0)
    tail_i = np.concatenate([-t_hi, c_hi, -t_lo, c_lo], 0)
    tail = np.concatenate([tail_r, tail_i], 1)
    tail_tab = np.concatenate([tail, tail], 0)
    grad_rows = np.concatenate([rows_hi.T, rows_lo.T, rows_hi.T, rows_lo.T], 1)
    turn = np.zeros((f, f))
    turn[np.arange(1, f), f - np.arange(1, f)] = 1.0
    row_flip = np.concatenate([turn, turn], 1)
    none = np.zeros((f, f))
    one_flip = np.concatenate(
        [np.concatenate([turn, none, turn, none], 1), np.concatenate([none, -turn, none, -turn], 1),
         np.zeros((2 * f, 4 * f))], 0,
    )
    lane_flip = np.concatenate([one_flip, one_flip], 0)
    tables = (
        row_side, col_side, lane_fwd, row_fwd, up_cols, down_cols, row_back, lane_back,
        row_flip, lane_flip, tail_tab, grad_rows,
    )
    return [np.asarray(t, dtype=BF16) for t in tables]


def dot(a, b):
    return lax.dot_general(a, b, (((1,), (0,)), ((), ())), preferred_element_type=jnp.float32)


def split(x):
    high = x.astype(BF16)
    return high, (x - high.astype(jnp.float32)).astype(BF16)


def stacked(x):
    high, low = split(x)
    return jnp.concatenate([high, high, low, low], axis=0)


INPUTS = 17
ORDER = (1, 0, 5, 6, 4, 3, 7, 8, 9, 2, 10, 11, 12, 13, 14, 15, 16)


def body(n, f, edge, count, *refs):
    ins, refs = refs[:INPUTS], refs[INPUTS:]
    mask_out, dual_out = refs[:2]
    refs = refs[2:]
    held, refs = refs[: INPUTS - 2], refs[INPUTS - 2 :]
    target_ref, k_ref, w_ref = held[:3]
    (
        row_side, col_side, lane_fwd, row_fwd, up_cols, down_cols, row_back, lane_back,
        row_flip, lane_flip, tail_tab, grad_rows,
    ) = held[3:]
    (
        md, h_sc, load_sem, hr, vr, q, q2, c7, c1, c2, c3, c4, c5, mb, xb, yb, slope, spec, spec_in, adj, adj_in,
        ready, send_sem, recv_sem,
    ) = refs
    places = [md.at[0], md.at[1], *held]
    sources = [ins[0].at[0], ins[1].at[0], *ins[2:]]
    loads = [pltpu.make_async_copy(src, dst, load_sem.at[i]) for i, (src, dst) in enumerate(zip(sources, places))]
    far = n - edge
    half = edge // 2
    g = 2 * f
    me = lax.axis_index("ty")
    row, col = me // GRID_COLS, me % GRID_COLS
    grid_rows = count // GRID_COLS
    left, right = col > 0, col < GRID_COLS - 1
    upper, lower = row > 0, row < grid_rows - 1
    both = jnp.logical_and
    near = [
        (-1, left), (1, right), (-GRID_COLS, upper), (GRID_COLS, lower),
        (-GRID_COLS - 1, both(upper, left)), (-GRID_COLS + 1, both(upper, right)),
        (GRID_COLS - 1, both(lower, left)), (GRID_COLS + 1, both(lower, right)),
    ]
    opposite = [1, 0, 3, 2, 7, 6, 5, 4]
    beside, above = (left, right), (upper, lower)
    lone_h, lone_v = [jnp.logical_not(x) for x in beside], [jnp.logical_not(x) for x in above]
    pair = (both(left, col % 2 == 1), both(right, col % 2 == 0))
    cross = [both(beside[h], jnp.logical_not(pair[h])) for h in range(2)]

    barrier = pltpu.get_barrier_semaphore()
    even = col % 2 == 0
    odd = jnp.logical_not(even)
    sure = [both(near[to][1], even) if to < 2 else near[to][1] for to in range(8)]
    asked = [both(near[to][1], odd) if to < 2 else near[to][1] for to in range(8)]
    earlier, later = (0, 1, 2, 4, 5), (0, 1, 3, 6, 7)
    for to in later:
        @pl.when(asked[to])
        def _(shift=near[to][0]):
            pl.semaphore_signal(barrier, inc=1, device_id={"ty": me + shift}, device_id_type=MESH)

    for i in ORDER[:2]:
        loads[i].start()

    counter = [0]

    def remote(src, dst, to, send_if, recv_if):
        index = counter[0]
        counter[0] += 1
        copy = pltpu.make_async_remote_copy(
            src_ref=src, dst_ref=dst, send_sem=send_sem.at[index], recv_sem=recv_sem.at[index],
            device_id={"ty": me + near[to][0]}, device_id_type=MESH,
        )
        return copy, send_if, recv_if, to

    def start(entries, which=None, known=None):
        for entry in entries:
            if which is None or entry[3] in which:
                pl.when(entry[1] if known is None or entry[3] > 1 else both(entry[1], known))(entry[0].start)

    def arrived(entries):
        for entry in entries:
            pl.when(entry[2])(entry[0].wait_recv)

    def sent(entries):
        for entry in entries:
            pl.when(entry[1])(entry[0].wait_send)

    begin = (0, far)
    bands = (pl.ds(0, edge), pl.ds(far, edge))
    middle = pl.ds(edge, far - edge)
    corners = [(v, h) for v in range(2) for h in range(2)]

    def piece(v, part):
        return pl.ds(begin[v] + part * half, half)

    raw = (ins[0].at[0], ins[1].at[0])
    plan = {}
    for i in range(2):
        for part in range(2):
            cols = pl.ds(edge + part * (far - edge) // 2, (far - edge) // 2)
            into = pl.ds(part * (far - edge) // 2, (far - edge) // 2)
            plan["v", i, part] = [
                remote(raw[i].at[bands[v], cols], vr.at[i, 1 - v, :, into], 2 + v, above[v], above[1 - v])
                for v in range(2)
            ]
        plan["h", i] = [
            remote(raw[i].at[middle, bands[h]], hr.at[i, 1 - h], h, beside[h], beside[1 - h]) for h in range(2)
        ]
    plan["hc"] = [
        remote(
            raw[i].at[bands[v], bands[h]], q.at[i, v, 1 - h], h,
            both(beside[h], lone_v[v]), both(beside[1 - h], lone_v[v]),
        )
        for v, h in corners for i in range(2)
    ]
    for name, side in (("vc", lone_h), ("vx", cross)):
        plan[name] = [
            remote(
                raw[i].at[bands[v], bands[h]], q.at[i, 1 - v, h], 2 + v,
                both(above[v], side[h]), both(above[1 - v], side[h]),
            )
            for v, h in corners for i in range(2)
        ]
    plan["cf"] = [
        remote(c7.at[:, v, h], q2.at[:, v, 1 - h], h, both(cross[h], above[v]), both(cross[1 - h], above[v]))
        for v, h in corners
    ]
    plan["c1"] = [
        remote(
            raw[i].at[piece(v, h), bands[h]], c1.at[i, v, 1 - h], h,
            both(pair[h], above[v]), both(pair[1 - h], above[v]),
        )
        for v, h in corners for i in range(2)
    ]
    plan["c3"] = [
        remote(c2.at[:, v, h], c3.at[:, 1 - v, h], 2 + v, both(pair[h], above[v]), both(pair[h], above[1 - v]))
        for v, h in corners
    ]
    plan["c5"] = [
        remote(c4.at[:, v, h], c5.at[:, v, 1 - h], h, both(pair[h], above[v]), both(pair[1 - h], above[v]))
        for v, h in corners
    ]
    plan["spec"] = [
        remote(spec.at[to], spec_in.at[opposite[to]], to, near[to][1], near[opposite[to]][1]) for to in range(8)
    ]
    direct = [near[to][1] if to < 4 else both(near[to][1], cross[to % 2]) for to in range(8)]
    plan["adj"] = [remote(adj, adj_in.at[opposite[to]], to, direct[to], direct[opposite[to]]) for to in range(8)]
    plan["pass"] = [
        remote(
            adj_in.at[2 + v], adj_in.at[5 + 2 * v - h], h, both(pair[h], above[v]), both(pair[1 - h], above[v])
        )
        for v, h in corners
    ]

    expected = sum(sure[to].astype(jnp.int32) for to in earlier)

    @pl.when(expected > 0)
    def _():
        pl.semaphore_wait(barrier, expected)

    for to in earlier:
        @pl.when(sure[to])
        def _(to=to):
            pl.semaphore_signal(
                ready.at[opposite[to]], inc=1, device_id={"ty": me + near[to][0]}, device_id_type=MESH
            )
    opening = plan["c1"] + plan["vx"] + plan["vc"] + plan["hc"] + plan["h", 1] + plan["h", 0]
    start(opening, earlier, even)
    for i in ORDER[2:]:
        loads[i].start()

    for to in range(8):
        @pl.when(jnp.logical_not(near[to][1]))
        def _(to=to):
            spec_in[to] = jnp.zeros((f // 2, 4 * f), jnp.float32)
            adj_in[to] = jnp.zeros((f // 2, 4 * f), jnp.float32)


    waited = set()

    def need(*which):
        for i in which:
            if i not in waited:
                waited.add(i)
                loads[i].wait()

    def meet(*which):
        for to in which:
            @pl.when(asked[to])
            def _(to=to):
                pl.semaphore_wait(ready.at[to], 1)

    meet(0)
    start(opening, (0,), odd)
    need(0, 1)
    up_f, down_f = upper.astype(jnp.float32), lower.astype(jnp.float32)
    left_f, right_f = left.astype(jnp.float32), right.astype(jnp.float32)
    at_col = lax.broadcasted_iota(jnp.int32, (1, n), 1)
    share_col = jnp.where(at_col < edge, 1.0 - 0.5 * left_f, jnp.where(at_col >= far, 1.0 - 0.5 * right_f, 1.0))
    share_side = (1.0 - 0.5 * left_f, 1.0 - 0.5 * right_f)
    share_end = (1.0 - 0.5 * up_f, 1.0 - 0.5 * down_f)

    def share_row(r):
        return share_end[0] if r == 0 else share_end[1] if r == far else None

    def scaled(x, by):
        return x if by is None else x * by

    lane = lax.broadcasted_iota(jnp.int32, (1, 4 * f), 1)
    low_half = lane < 2 * f
    is_real = (lane // f) % 2 == 0

    for r in range(0, n, edge):
        rows = slice(r, r + edge)
        m, d = md[0, rows, :], md[1, rows, :]
        y = (m + d) * scaled(0.5 * share_col, share_row(r))
        mb[rows, :] = m.astype(BF16)
        yb[rows, :] = y.astype(BF16)
        xb[rows, :] = (0.5 * m - 0.25 * d + y).astype(BF16)

    meet(3)
    start(opening, (3,))
    meet(1)
    start(opening, (1,), odd)

    need(5, 6)
    top_part = dot(row_side[:g, far:], yb[:edge, :]).astype(BF16)
    end_part = dot(row_side[:g, :edge], yb[far:, :]).astype(BF16)
    left_part = dot(row_side[:g, :], yb[:, :edge]).astype(BF16)
    right_part = dot(row_side[:g, :], yb[:, far:]).astype(BF16)

    def to_band(grid):
        real = grid[:f, : 4 * f] - grid[f:, 4 * f :]
        imag = grid[:f, 4 * f :] + grid[f:, : 4 * f]
        return real, imag

    def packed_band(grid):
        real, imag = to_band(grid)
        return jnp.where(is_real, real, imag)

    def folded(x):
        return jnp.where(low_half, x[: f // 2], x[f // 2 :])

    def unfolded(x):
        turned = pltpu.roll(x, 2 * f, 1)
        return jnp.concatenate([jnp.where(low_half, x, turned), jnp.where(low_half, turned, x)], axis=0)

    at_left = dot(
        jnp.concatenate([left_part, top_part[:, :edge], end_part[:, :edge]], axis=0), col_side[far:, :]
    )
    at_right = dot(
        jnp.concatenate([right_part, top_part[:, far:], end_part[:, far:]], axis=0), col_side[:edge, :]
    )
    at_ends = dot(jnp.concatenate([top_part, end_part], axis=0), col_side[...])
    for i, to in enumerate((0, 4, 6)):
        spec[to] = folded(packed_band(at_left[i * g : (i + 1) * g]))
    for i, to in enumerate((1, 5, 7)):
        spec[to] = folded(packed_band(at_right[i * g : (i + 1) * g]))
    for i, to in enumerate((2, 3)):
        spec[to] = folded(packed_band(at_ends[i * g : (i + 1) * g]))
    meet(6, 7)
    start(plan["spec"])
    arrived(plan["c1"])
    for v, h in corners:
        @pl.when(both(pair[h], above[v]))
        def _(v=v, h=h):
            c2[:, v, h] = md[:, piece(v, 1 - h), bands[h]] + c1[:, v, h]
    start(plan["c3"] + plan["v", 1, 0])

    part = dot(row_side[...], jnp.concatenate([mb[...], xb[...]], axis=1))
    part = part[:g] + part[g:]
    first_part, next_part = part[:, :n], part[:, n:]
    grid = dot(jnp.concatenate([*split(first_part), next_part.astype(BF16)], axis=0), col_side[...])
    band_one = to_band(grid[:g] + grid[g : 2 * g])
    band_next = packed_band(grid[2 * g :])

    need(4, 3)
    quarters = w_ref.shape[0] // 2
    total = w_ref[0]
    for k in range(1, w_ref.shape[0]):
        total = total + w_ref[k]
    portions = [
        jnp.where(low_half, w_ref[2 * k], w_ref[2 * k + 1]) / jnp.full((1, 4 * f), total, jnp.float32)
        for k in range(quarters)
    ]
    for k in range(quarters):
        rows_of = []
        for j in range(4):
            flat = k_ref.at[2 * k + j // 2]
            rows_of.append(
                jnp.concatenate([flat[j % 2 : j % 2 + 1, 4 * f * a : 4 * f * (a + 1)] for a in range(f // 4)], axis=0)
            )
        for b in range(4):
            value = rows_of[b]
            for j in range(4):
                if j != b:
                    value = jnp.where(lane // f == j, pltpu.roll(rows_of[j], (j - b) % 4 * f, 1), value)
            h_sc[pl.ds(k * f + b, f // 4, stride=4), :] = value
    h_one = h_sc[...]
    h_two = jnp.where(is_real, -pltpu.roll(h_one, 3 * f, 1), pltpu.roll(h_one, f, 1))

    def fields(real, imag):
        need(7, 8)
        w = 8 * f
        real = jnp.concatenate([real] * quarters, axis=0)
        imag = jnp.concatenate([imag] * quarters, axis=0)
        gated = h_one * real + h_two * imag
        turned = dot(jnp.concatenate(split(gated), axis=0), lane_fwd[...])
        m = quarters * f
        turned = (turned[:m, :w] + turned[:m, w:]) + turned[m:, :w]
        wide = jnp.concatenate(
            [
                jnp.concatenate([turned[k * f : (k + 1) * f, : 4 * f], turned[k * f : (k + 1) * f, 4 * f :]], axis=0)
                for k in range(quarters)
            ],
            axis=1,
        )
        return dot(row_fwd[...], stacked(wide))

    def write_slope(field):
        need(9, 10, 2)
        energy = field[:g] * field[:g] + field[g:] * field[g:]
        summed = energy[:, : 2 * g] * portions[0]
        for k in range(1, quarters):
            summed = summed + energy[:, 2 * g * k : 2 * g * (k + 1)] * portions[k]
        summed = summed + pltpu.roll(summed, g, 1)
        level = dot(jnp.concatenate(split(summed), axis=1), up_cols[...])
        high, rest = split(level)
        level = jnp.concatenate([high, rest, high, rest], axis=0)
        for r in range(0, n, edge):
            intensity = dot(down_cols[r : r + edge, :], level)
            resist = 1.0 / (1.0 + jnp.exp(-SHARPNESS * (intensity - THRESHOLD)))
            goal = target_ref[0, r : r + edge, :].astype(jnp.float32)
            value = (2.0 * SHARPNESS) * (resist - goal) * resist * (1.0 - resist)
            slope[r : r + edge, :] = value.astype(BF16)

    def adjoint(field):
        need(11, 12)
        low = dot(up_cols[: 2 * g, :], slope[...])
        low = low[:g] + low[g:]
        low = dot(jnp.concatenate(split(low), axis=0), down_cols[...])
        low = (low[:g, : 2 * g] + low[:g, 2 * g :]) + low[g:, : 2 * g]
        weighted = field * jnp.concatenate([jnp.concatenate([low] * quarters, axis=1)] * 2, axis=0)
        high, rest = split(weighted)
        back = dot(row_back[...], high)
        back = (back[: 2 * f] + back[2 * f :]) + dot(row_back[: 2 * f, :], rest)
        tall = jnp.concatenate(
            [
                jnp.concatenate([back[:f, 4 * f * k : 4 * f * (k + 1)], back[f:, 4 * f * k : 4 * f * (k + 1)]], axis=1)
                for k in range(quarters)
            ],
            axis=0,
        )
        m = quarters * f
        turned = dot(jnp.concatenate(split(tall), axis=0), lane_back[...])
        turned = (turned[:m, : 4 * f] + turned[:m, 4 * f :]) + turned[m:, : 4 * f]
        first, second = h_one * turned, h_two * turned
        real = jnp.zeros((f, 4 * f), jnp.float32)
        imag = jnp.zeros((f, 4 * f), jnp.float32)
        for k in range(quarters):
            real = real + first[k * f : (k + 1) * f] * portions[k]
            imag = imag + second[k * f : (k + 1) * f] * portions[k]
        real = real + pltpu.roll(real, 2 * f, 1)
        real = real + pltpu.roll(real, f, 1)
        imag = imag + pltpu.roll(imag, 2 * f, 1)
        imag = imag + pltpu.roll(imag, f, 1)
        return jnp.where(is_real, real, imag)

    def tails(packed):
        need(15)
        out = dot(jnp.concatenate(split(packed), axis=1), tail_tab[...])
        return jnp.concatenate([out[:, :n], out[:, n:]], axis=0)

    def band_tails(which, begin):
        packed = jnp.concatenate([unfolded(adj_in[to]) for to in which], axis=0)
        packed = jnp.concatenate(split(packed), axis=1)
        real = dot(packed, tail_tab[:, begin : begin + edge])
        imag = dot(packed, tail_tab[:, n + begin : n + begin + edge])
        return [
            jnp.concatenate([real[i * f : (i + 1) * f], imag[i * f : (i + 1) * f]], axis=0) for i in range(len(which))
        ]

    field = fields(*band_one)
    write_slope(field)
    packed = adjoint(field)
    adj[...] = folded(packed)
    start(plan["adj"] + plan["v", 1, 1] + plan["v", 0, 0] + plan["v", 0, 1])
    arrived(plan["vx"])
    for v, h in corners:
        @pl.when(both(cross[h], above[v]))
        def _(v=v, h=h):
            for i in range(2):
                c7[i, v, h] = md[i, bands[v], bands[h]] + q[i, v, h]
    start(plan["cf"])

    need(13, 14)
    turned = dot(row_flip[...], jnp.concatenate(split(packed), axis=0))
    mirrored = dot(jnp.concatenate(split(turned), axis=1), lane_flip[...])
    band = band_next - STEP_SIZE * (packed + mirrored)
    arrived(plan["spec"])
    incoming = spec_in[0]
    for to in range(1, 8):
        incoming = incoming + spec_in[to]
    band = band + unfolded(incoming)
    field = fields(jnp.where(is_real, band, pltpu.roll(band, f, 1)), jnp.where(is_real, pltpu.roll(band, 3 * f, 1), band))
    write_slope(field)
    arrived(plan["c3"])
    for v, h in corners:
        @pl.when(both(pair[h], above[v]))
        def _(v=v, h=h):
            c4[:, v, h] = c2[:, v, h] + c3[:, v, h]
            q[:, v, h, pl.ds((1 - h) * half, half), :] = c1[:, v, h] + c3[:, v, h]
    start(plan["c5"])


    last = adjoint(field)
    tail_last = tails(last)
    tail_own = tails(packed)
    arrived(plan["adj"])

    def joined(tail, from_left, from_right):
        return share_col * jnp.concatenate(
            [tail[:, :edge] + from_left, tail[:, edge:far], tail[:, far:] + from_right], axis=1
        )

    start(plan["pass"])
    sides = dot(
        jnp.concatenate(split(jnp.concatenate([unfolded(adj_in[2]), unfolded(adj_in[3])], axis=0)), axis=1), tail_tab[...]
    )
    arrived(plan["pass"])
    at_left, at_right = band_tails((0, 4, 6), far), band_tails((1, 5, 7), 0)
    ends = [jnp.concatenate([sides[i * f : (i + 1) * f, :n], sides[i * f : (i + 1) * f, n:]], axis=0) for i in range(2)]
    sum_own = joined(tail_own, at_left[0], at_right[0])
    sum_end = [joined(ends[i], at_left[1 + i], at_right[1 + i]) for i in range(2)]
    need(16)
    base = -0.125 * tail_own - STEP_SIZE * tail_last
    inner_m = stacked(base - 0.125 * sum_own)
    inner_d = stacked(STEP_SIZE * (sum_own - tail_own))
    for r in range(0, n, edge):
        rows = slice(r, r + edge)
        by = share_row(r)
        if by is None:
            grad_m = dot(grad_rows[rows, :], inner_m)
            grad_d = dot(grad_rows[rows, :], inner_d)
        else:
            other = sum_end[0] if r == 0 else sum_end[1]
            across = dot(grad_rows[far:, :] if r == 0 else grad_rows[:edge, :], stacked(by * other))
            grad_m = dot(grad_rows[rows, :], stacked(base - (0.125 * by) * sum_own)) - 0.125 * across
            grad_d = dot(grad_rows[rows, :], stacked(STEP_SIZE * (by * sum_own - tail_own))) + STEP_SIZE * across
        m, d = md[0, rows, :], md[1, rows, :]
        cover = scaled(share_col, by)
        mask_out[0, rows, :] = cover * (m + 0.625 * d) - 0.375 * d + grad_m
        dual_out[0, rows, :] = (1.5 * m + 0.75 * d) * (1.0 - cover) + grad_d

    def settle(rows, cols, by, m, d):
        mask_out[0, rows, cols] = mask_out[0, rows, cols] + by * (m + 0.625 * d)
        dual_out[0, rows, cols] = dual_out[0, rows, cols] - by * (1.5 * m + 0.75 * d)

    arrived(plan["c5"] + plan["hc"] + plan["vc"] + plan["cf"])
    for v, h in corners:
        @pl.when(both(pair[h], above[v]))
        def _(v=v, h=h):
            q[:, v, h, pl.ds(h * half, half), :] = c5[:, v, h] - md[:, piece(v, h), bands[h]]

        @pl.when(both(cross[h], above[v]))
        def _(v=v, h=h):
            q[:, v, h] = q[:, v, h] + q2[:, v, h]

        @pl.when(jnp.logical_or(beside[h], above[v]))
        def _(v=v, h=h):
            settle(bands[v], bands[h], share_end[v] * share_side[h], q[0, v, h], q[1, v, h])
    arrived(plan["h", 0] + plan["h", 1])
    for h in range(2):
        @pl.when(beside[h])
        def _(h=h):
            settle(middle, bands[h], share_side[h], hr[0, h], hr[1, h])
    arrived(plan["v", 1, 0] + plan["v", 1, 1])
    for v in range(2):
        @pl.when(above[v])
        def _(v=v):
            d = share_end[v] * vr[1, v]
            mask_out[0, bands[v], middle] = mask_out[0, bands[v], middle] + 0.625 * d
            dual_out[0, bands[v], middle] = dual_out[0, bands[v], middle] - 0.75 * d
    final = [("v", 0, 0), ("v", 0, 1)]
    for name, entries in plan.items():
        if name not in final:
            sent(entries)
    width = (far - edge) // 2
    for part, name in enumerate(final):
        arrived(plan[name])
        for v in range(2):
            @pl.when(above[v])
            def _(v=v, part=part):
                cols = pl.ds(edge + part * width, width)
                m = share_end[v] * vr[0, v, :, pl.ds(part * width, width)]
                mask_out[0, bands[v], cols] = mask_out[0, bands[v], cols] + m
                dual_out[0, bands[v], cols] = dual_out[0, bands[v], cols] - 1.5 * m
    for name in final:
        sent(plan[name])


def write_out(*refs):
    sources, targets, sem = refs[:2], refs[2:4], refs[4]
    copies = [pltpu.make_async_copy(a, b, sem.at[i]) for i, (a, b) in enumerate(zip(sources, targets))]
    for copy in copies:
        copy.start()
    for copy in copies:
        copy.wait()


def per_device(count, mask_init, dual_init, target, kernels, weights):
    n = mask_init.shape[-1]
    edge = INTERSECTION
    f = int(round(kernels.shape[-1] ** 0.5))
    tables = [jnp.asarray(t) for t in host_tables(n, f)]
    f32 = jnp.float32
    whole = pl.BlockSpec(memory_space=pltpu.VMEM)
    far_memory = pl.BlockSpec(memory_space=pltpu.HBM)
    arrays = (mask_init, dual_init, target, kernels, weights, *tables)
    tile = jax.ShapeDtypeStruct((1, n, n), f32)
    inner = n - 2 * edge
    half = edge // 2
    results = pl.pallas_call(
        functools.partial(body, n, f, edge, count),
        out_shape=(tile, tile),
        in_specs=[far_memory] * len(arrays),
        out_specs=(whole, whole),
        scratch_shapes=[
            pltpu.SMEM(a.shape, a.dtype) if i == 4 else pltpu.VMEM(a.shape, a.dtype)
            for i, a in enumerate(arrays) if i >= 2
        ]
        + [
            pltpu.VMEM((2, n, n), f32),
            pltpu.VMEM((kernels.shape[0] // 2 * f, 4 * f), f32),
            pltpu.SemaphoreType.DMA((len(arrays),)),
            pltpu.VMEM((2, 2, inner, edge), f32),
            pltpu.VMEM((2, 2, edge, inner), f32),
            pltpu.VMEM((2, 2, 2, edge, edge), f32),
            pltpu.VMEM((2, 2, 2, edge, edge), f32),
            pltpu.VMEM((2, 2, 2, edge, edge), f32),
        ]
        + [pltpu.VMEM((2, 2, 2, half, edge), f32)] * 5
        + [pltpu.VMEM((n, n), BF16)] * 4
        + [
            pltpu.VMEM((8, f // 2, 4 * f), f32),
            pltpu.VMEM((8, f // 2, 4 * f), f32),
            pltpu.VMEM((f // 2, 4 * f), f32),
            pltpu.VMEM((8, f // 2, 4 * f), f32),
            pltpu.SemaphoreType.REGULAR((8,)),
            pltpu.SemaphoreType.DMA((80,)),
            pltpu.SemaphoreType.DMA((80,)),
        ],
        compiler_params=pltpu.CompilerParams(
            collective_id=0, has_side_effects=True, vmem_limit_bytes=48 * 1024 * 1024
        ),
    )(*[pltpu.with_memory_space_constraint(a, pltpu.HBM) for a in arrays])
    return pl.pallas_call(
        write_out,
        out_shape=(tile, tile),
        in_specs=[pl.BlockSpec(memory_space=pl.ANY)] * 2,
        out_specs=[far_memory] * 2,
        scratch_shapes=[pltpu.SemaphoreType.DMA((2,))],
        compiler_params=pltpu.CompilerParams(vmem_limit_bytes=1 << 20),
    )(*results)


def solution(mesh):
    tile = P(("region", "ty"), None, None)
    return jax.shard_map(
        functools.partial(per_device, mesh.shape["ty"]),
        mesh=mesh,
        in_specs=(tile, tile, tile, P(), P()),
        out_specs=(tile, tile),
        check_vma=False,
    )
```

```python
import functools

import jax
import jax.numpy as jnp
import numpy as np
from jax import lax
from jax.experimental import pallas as pl
from jax.experimental.pallas import tpu as pltpu
from jax.sharding import PartitionSpec as P

GRID_COLS = 4
INTERSECTION = 128
SHARPNESS = 8.0
THRESHOLD = 0.3
STEP_SIZE = 0.25
PENALTY = 1.0
MESH = pl.DeviceIdType.MESH
BF16 = jnp.bfloat16


def split_host(table):
    table = table.astype(np.float32)
    high = table.astype(BF16)
    low = (table - high.astype(np.float32)).astype(BF16)
    return high, low


def host_tables(n, f):
    g = 2 * f
    freq = np.arange(f) - f // 2
    phase = 2.0 * np.pi * ((freq[:, None] * np.arange(n)[None, :]) % n) / n
    cos, sin = np.cos(phase), -np.sin(phase)
    rows = np.concatenate([cos, sin], 0)
    rows_hi, rows_lo = split_host(rows)
    row_side = np.concatenate([rows_hi, rows_lo], 0)
    col_wide = np.concatenate([np.tile(cos.T, (1, 4)), np.tile(sin.T, (1, 4))], 1)
    col_side = split_host(col_wide)[0]
    coarse = 2.0 * np.pi * ((np.arange(g)[:, None] * freq[None, :]) % g) / g
    er, ei = np.cos(coarse), np.sin(coarse)
    pair = np.eye(2)
    to_real = np.kron(pair, np.concatenate([er.T, -ei.T], 0))
    to_imag = np.kron(pair, np.concatenate([ei.T, er.T], 0))
    lane_turn = np.concatenate([to_real, to_imag], 1)
    lane_fwd = np.concatenate(split_host(lane_turn / (n * n)), 1)
    lane_back = np.concatenate(split_host(lane_turn.T), 1)
    row_turn = np.concatenate([np.concatenate([er, -ei], 1), np.concatenate([ei, er], 1)], 0)
    turn_hi, turn_lo = split_host(row_turn)
    row_fwd = np.concatenate([turn_hi, turn_lo, turn_hi, turn_lo], 1)
    row_back = np.concatenate(split_host(row_turn.T), 0)
    half = np.arange(-(f - 1), f)
    angle = np.arange(n)[:, None] * f * 2 - np.arange(g)[None, :] * n
    spread = np.cos(2.0 * np.pi * ((angle[..., None] * half) % (n * g)) / (n * g)).sum(-1) / g
    s_hi, s_lo = split_host(spread)
    up_cols = np.concatenate([s_hi.T, s_lo.T, s_hi.T, s_lo.T], 0)
    down_cols = np.concatenate([s_hi, s_hi, s_lo, s_lo], 1)
    scale = 2.0 / (n * n)
    c_hi, c_lo = split_host(cos * scale)
    t_hi, t_lo = split_host(sin * scale)
    tail_r = np.concatenate([c_hi, t_hi, c_lo, t_lo], 0)
    tail_i = np.concatenate([-t_hi, c_hi, -t_lo, c_lo], 0)
    tail = np.concatenate([tail_r, tail_i], 1)
    tail_tab = np.concatenate([tail, tail], 0)
    grad_rows = np.concatenate([rows_hi.T, rows_lo.T, rows_hi.T, rows_lo.T], 1)
    turn = np.zeros((f, f))
    turn[np.arange(1, f), f - np.arange(1, f)] = 1.0
    row_flip = np.concatenate([turn, turn], 1)
    none = np.zeros((f, f))
    one_flip = np.concatenate(
        [np.concatenate([turn, none, turn, none], 1), np.concatenate([none, -turn, none, -turn], 1),
         np.zeros((2 * f, 4 * f))], 0,
    )
    lane_flip = np.concatenate([one_flip, one_flip], 0)
    tables = (
        row_side, col_side, lane_fwd, row_fwd, up_cols, down_cols, row_back, lane_back,
        row_flip, lane_flip, tail_tab, grad_rows,
    )
    return [np.asarray(t, dtype=BF16) for t in tables]


def dot(a, b):
    return lax.dot_general(a, b, (((1,), (0,)), ((), ())), preferred_element_type=jnp.float32)


def split(x):
    high = x.astype(BF16)
    return high, (x - high.astype(jnp.float32)).astype(BF16)


def stacked(x):
    high, low = split(x)
    return jnp.concatenate([high, high, low, low], axis=0)


INPUTS = 17
ORDER = (1, 0, 5, 6, 4, 3, 7, 8, 9, 2, 10, 11, 12, 13, 14, 15, 16)


def body(n, f, edge, count, *refs):
    ins, refs = refs[:INPUTS], refs[INPUTS:]
    mask_out, dual_out = refs[:2]
    refs = refs[2:]
    held, refs = refs[: INPUTS - 2], refs[INPUTS - 2 :]
    target_ref, k_ref, w_ref = held[:3]
    (
        row_side, col_side, lane_fwd, row_fwd, up_cols, down_cols, row_back, lane_back,
        row_flip, lane_flip, tail_tab, grad_rows,
    ) = held[3:]
    (
        md, h_sc, load_sem, hr, vr, q, q2, c7, c1, c2, c3, c4, c5, mb, xb, yb, slope, spec, spec_in, adj, adj_in,
        ready, send_sem, recv_sem,
    ) = refs
    places = [md.at[0], md.at[1], *held]
    sources = [ins[0].at[0], ins[1].at[0], *ins[2:]]
    loads = [pltpu.make_async_copy(src, dst, load_sem.at[i]) for i, (src, dst) in enumerate(zip(sources, places))]
    far = n - edge
    half = edge // 2
    g = 2 * f
    me = lax.axis_index("ty")
    row, col = me // GRID_COLS, me % GRID_COLS
    grid_rows = count // GRID_COLS
    left, right = col > 0, col < GRID_COLS - 1
    upper, lower = row > 0, row < grid_rows - 1
    both = jnp.logical_and
    near = [
        (-1, left), (1, right), (-GRID_COLS, upper), (GRID_COLS, lower),
        (-GRID_COLS - 1, both(upper, left)), (-GRID_COLS + 1, both(upper, right)),
        (GRID_COLS - 1, both(lower, left)), (GRID_COLS + 1, both(lower, right)),
    ]
    opposite = [1, 0, 3, 2, 7, 6, 5, 4]
    beside, above = (left, right), (upper, lower)
    lone_h, lone_v = [jnp.logical_not(x) for x in beside], [jnp.logical_not(x) for x in above]
    pair = (both(left, col % 2 == 1), both(right, col % 2 == 0))
    cross = [both(beside[h], jnp.logical_not(pair[h])) for h in range(2)]

    barrier = pltpu.get_barrier_semaphore()
    even = col % 2 == 0
    odd = jnp.logical_not(even)
    sure = [both(near[to][1], even) if to < 2 else near[to][1] for to in range(8)]
    asked = [both(near[to][1], odd) if to < 2 else near[to][1] for to in range(8)]
    earlier, later = (0, 1, 2, 4, 5), (0, 1, 3, 6, 7)
    for to in later:
        @pl.when(asked[to])
        def _(shift=near[to][0]):
            pl.semaphore_signal(barrier, inc=1, device_id={"ty": me + shift}, device_id_type=MESH)

    for i in ORDER[:2]:
        loads[i].start()

    counter = [0]

    def remote(src, dst, to, send_if, recv_if):
        index = counter[0]
        counter[0] += 1
        copy = pltpu.make_async_remote_copy(
            src_ref=src, dst_ref=dst, send_sem=send_sem.at[index], recv_sem=recv_sem.at[index],
            device_id={"ty": me + near[to][0]}, device_id_type=MESH,
        )
        return copy, send_if, recv_if, to

    def start(entries, which=None, known=None):
        for entry in entries:
            if which is None or entry[3] in which:
                pl.when(entry[1] if known is None or entry[3] > 1 else both(entry[1], known))(entry[0].start)

    def arrived(entries):
        for entry in entries:
            pl.when(entry[2])(entry[0].wait_recv)

    def sent(entries):
        for entry in entries:
            pl.when(entry[1])(entry[0].wait_send)

    begin = (0, far)
    bands = (pl.ds(0, edge), pl.ds(far, edge))
    middle = pl.ds(edge, far - edge)
    corners = [(v, h) for v in range(2) for h in range(2)]

    def piece(v, part):
        return pl.ds(begin[v] + part * half, half)

    raw = (ins[0].at[0], ins[1].at[0])
    plan = {}
    for i in range(2):
        for part in range(2):
            cols = pl.ds(edge + part * (far - edge) // 2, (far - edge) // 2)
            into = pl.ds(part * (far - edge) // 2, (far - edge) // 2)
            plan["v", i, part] = [
                remote(raw[i].at[bands[v], cols], vr.at[i, 1 - v, :, into], 2 + v, above[v], above[1 - v])
                for v in range(2)
            ]
        plan["h", i] = [
            remote(raw[i].at[middle, bands[h]], hr.at[i, 1 - h], h, beside[h], beside[1 - h]) for h in range(2)
        ]
    plan["hc"] = [
        remote(
            raw[i].at[bands[v], bands[h]], q.at[i, v, 1 - h], h,
            both(beside[h], lone_v[v]), both(beside[1 - h], lone_v[v]),
        )
        for v, h in corners for i in range(2)
    ]
    for name, side in (("vc", lone_h), ("vx", cross)):
        plan[name] = [
            remote(
                raw[i].at[bands[v], bands[h]], q.at[i, 1 - v, h], 2 + v,
                both(above[v], side[h]), both(above[1 - v], side[h]),
            )
            for v, h in corners for i in range(2)
        ]
    plan["cf"] = [
        remote(c7.at[:, v, h], q2.at[:, v, 1 - h], h, both(cross[h], above[v]), both(cross[1 - h], above[v]))
        for v, h in corners
    ]
    plan["c1"] = [
        remote(
            raw[i].at[piece(v, h), bands[h]], c1.at[i, v, 1 - h], h,
            both(pair[h], above[v]), both(pair[1 - h], above[v]),
        )
        for v, h in corners for i in range(2)
    ]
    plan["c3"] = [
        remote(c2.at[:, v, h], c3.at[:, 1 - v, h], 2 + v, both(pair[h], above[v]), both(pair[h], above[1 - v]))
        for v, h in corners
    ]
    plan["c5"] = [
        remote(c4.at[:, v, h], c5.at[:, v, 1 - h], h, both(pair[h], above[v]), both(pair[1 - h], above[v]))
        for v, h in corners
    ]
    plan["spec"] = [
        remote(spec.at[to], spec_in.at[opposite[to]], to, near[to][1], near[opposite[to]][1]) for to in range(8)
    ]
    direct = [near[to][1] if to < 4 else both(near[to][1], cross[to % 2]) for to in range(8)]
    plan["adj"] = [remote(adj, adj_in.at[opposite[to]], to, direct[to], direct[opposite[to]]) for to in range(8)]
    plan["pass"] = [
        remote(
            adj_in.at[2 + v], adj_in.at[5 + 2 * v - h], h, both(pair[h], above[v]), both(pair[1 - h], above[v])
        )
        for v, h in corners
    ]

    expected = sum(sure[to].astype(jnp.int32) for to in earlier)

    @pl.when(expected > 0)
    def _():
        pl.semaphore_wait(barrier, expected)

    for to in earlier:
        @pl.when(sure[to])
        def _(to=to):
            pl.semaphore_signal(
                ready.at[opposite[to]], inc=1, device_id={"ty": me + near[to][0]}, device_id_type=MESH
            )
    opening = plan["vx"] + plan["c1"] + plan["vc"] + plan["hc"]
    start(opening, earlier, even)
    for i in ORDER[2:]:
        loads[i].start()

    for to in range(8):
        @pl.when(jnp.logical_not(near[to][1]))
        def _(to=to):
            spec_in[to] = jnp.zeros((f // 2, 4 * f), jnp.float32)
            adj_in[to] = jnp.zeros((f // 2, 4 * f), jnp.float32)


    waited = set()

    def need(*which):
        for i in which:
            if i not in waited:
                waited.add(i)
                loads[i].wait()

    def meet(*which):
        for to in which:
            @pl.when(asked[to])
            def _(to=to):
                pl.semaphore_wait(ready.at[to], 1)

    meet(0)
    start(opening, (0,), odd)
    need(0, 1)
    up_f, down_f = upper.astype(jnp.float32), lower.astype(jnp.float32)
    left_f, right_f = left.astype(jnp.float32), right.astype(jnp.float32)
    at_col = lax.broadcasted_iota(jnp.int32, (1, n), 1)
    share_col = jnp.where(at_col < edge, 1.0 - 0.5 * left_f, jnp.where(at_col >= far, 1.0 - 0.5 * right_f, 1.0))
    share_side = (1.0 - 0.5 * left_f, 1.0 - 0.5 * right_f)
    share_end = (1.0 - 0.5 * up_f, 1.0 - 0.5 * down_f)

    def share_row(r):
        return share_end[0] if r == 0 else share_end[1] if r == far else None

    def scaled(x, by):
        return x if by is None else x * by

    lane = lax.broadcasted_iota(jnp.int32, (1, 4 * f), 1)
    low_half = lane < 2 * f
    is_real = (lane // f) % 2 == 0

    for r in range(0, n, edge):
        rows = slice(r, r + edge)
        m, d = md[0, rows, :], md[1, rows, :]
        y = (m + d) * scaled(0.5 * share_col, share_row(r))
        mb[rows, :] = m.astype(BF16)
        yb[rows, :] = y.astype(BF16)
        xb[rows, :] = (0.5 * m - 0.25 * d + y).astype(BF16)

    meet(3)
    start(opening, (3,))
    meet(1)
    start(opening, (1,), odd)

    need(5, 6)
    top_part = dot(row_side[:g, far:], yb[:edge, :]).astype(BF16)
    end_part = dot(row_side[:g, :edge], yb[far:, :]).astype(BF16)
    left_part = dot(row_side[:g, :], yb[:, :edge]).astype(BF16)
    right_part = dot(row_side[:g, :], yb[:, far:]).astype(BF16)

    def to_band(grid):
        real = grid[:f, : 4 * f] - grid[f:, 4 * f :]
        imag = grid[:f, 4 * f :] + grid[f:, : 4 * f]
        return real, imag

    def packed_band(grid):
        real, imag = to_band(grid)
        return jnp.where(is_real, real, imag)

    def folded(x):
        return jnp.where(low_half, x[: f // 2], x[f // 2 :])

    def unfolded(x):
        turned = pltpu.roll(x, 2 * f, 1)
        return jnp.concatenate([jnp.where(low_half, x, turned), jnp.where(low_half, turned, x)], axis=0)

    at_left = dot(
        jnp.concatenate([left_part, top_part[:, :edge], end_part[:, :edge]], axis=0), col_side[far:, :]
    )
    at_right = dot(
        jnp.concatenate([right_part, top_part[:, far:], end_part[:, far:]], axis=0), col_side[:edge, :]
    )
    at_ends = dot(jnp.concatenate([top_part, end_part], axis=0), col_side[...])
    for i, to in enumerate((0, 4, 6)):
        spec[to] = folded(packed_band(at_left[i * g : (i + 1) * g]))
    for i, to in enumerate((1, 5, 7)):
        spec[to] = folded(packed_band(at_right[i * g : (i + 1) * g]))
    for i, to in enumerate((2, 3)):
        spec[to] = folded(packed_band(at_ends[i * g : (i + 1) * g]))
    meet(6, 7)
    start(plan["spec"])
    arrived(plan["c1"])
    for v, h in corners:
        @pl.when(both(pair[h], above[v]))
        def _(v=v, h=h):
            c2[:, v, h] = md[:, piece(v, 1 - h), bands[h]] + c1[:, v, h]
    start(plan["c3"] + plan["v", 1, 0] + plan["h", 1] + plan["h", 0])

    part = dot(row_side[...], jnp.concatenate([mb[...], xb[...]], axis=1))
    part = part[:g] + part[g:]
    first_part, next_part = part[:, :n], part[:, n:]
    grid = dot(jnp.concatenate([*split(first_part), next_part.astype(BF16)], axis=0), col_side[...])
    band_one = to_band(grid[:g] + grid[g : 2 * g])
    band_next = packed_band(grid[2 * g :])

    need(4, 3)
    quarters = w_ref.shape[0] // 2
    total = w_ref[0]
    for k in range(1, w_ref.shape[0]):
        total = total + w_ref[k]
    portions = [
        jnp.where(low_half, w_ref[2 * k], w_ref[2 * k + 1]) / jnp.full((1, 4 * f), total, jnp.float32)
        for k in range(quarters)
    ]
    for k in range(quarters):
        rows_of = []
        for j in range(4):
            flat = k_ref.at[2 * k + j // 2]
            rows_of.append(
                jnp.concatenate([flat[j % 2 : j % 2 + 1, 4 * f * a : 4 * f * (a + 1)] for a in range(f // 4)], axis=0)
            )
        for b in range(4):
            value = rows_of[b]
            for j in range(4):
                if j != b:
                    value = jnp.where(lane // f == j, pltpu.roll(rows_of[j], (j - b) % 4 * f, 1), value)
            h_sc[pl.ds(k * f + b, f // 4, stride=4), :] = value
    h_one = h_sc[...]
    h_two = jnp.where(is_real, -pltpu.roll(h_one, 3 * f, 1), pltpu.roll(h_one, f, 1))

    def fields(real, imag):
        need(7, 8)
        w = 8 * f
        real = jnp.concatenate([real] * quarters, axis=0)
        imag = jnp.concatenate([imag] * quarters, axis=0)
        gated = h_one * real + h_two * imag
        turned = dot(jnp.concatenate(split(gated), axis=0), lane_fwd[...])
        m = quarters * f
        turned = (turned[:m, :w] + turned[:m, w:]) + turned[m:, :w]
        wide = jnp.concatenate(
            [
                jnp.concatenate([turned[k * f : (k + 1) * f, : 4 * f], turned[k * f : (k + 1) * f, 4 * f :]], axis=0)
                for k in range(quarters)
            ],
            axis=1,
        )
        return dot(row_fwd[...], stacked(wide))

    def write_slope(field):
        need(9, 10, 2)
        energy = field[:g] * field[:g] + field[g:] * field[g:]
        summed = energy[:, : 2 * g] * portions[0]
        for k in range(1, quarters):
            summed = summed + energy[:, 2 * g * k : 2 * g * (k + 1)] * portions[k]
        summed = summed + pltpu.roll(summed, g, 1)
        level = dot(jnp.concatenate(split(summed), axis=1), up_cols[...])
        high, rest = split(level)
        level = jnp.concatenate([high, rest, high, rest], axis=0)
        for r in range(0, n, edge):
            intensity = dot(down_cols[r : r + edge, :], level)
            resist = 1.0 / (1.0 + jnp.exp(-SHARPNESS * (intensity - THRESHOLD)))
            goal = target_ref[0, r : r + edge, :].astype(jnp.float32)
            value = (2.0 * SHARPNESS) * (resist - goal) * resist * (1.0 - resist)
            slope[r : r + edge, :] = value.astype(BF16)

    def adjoint(field):
        need(11, 12)
        low = dot(up_cols[: 2 * g, :], slope[...])
        low = low[:g] + low[g:]
        low = dot(jnp.concatenate(split(low), axis=0), down_cols[...])
        low = (low[:g, : 2 * g] + low[:g, 2 * g :]) + low[g:, : 2 * g]
        weighted = field * jnp.concatenate([jnp.concatenate([low] * quarters, axis=1)] * 2, axis=0)
        high, rest = split(weighted)
        back = dot(row_back[...], high)
        back = (back[: 2 * f] + back[2 * f :]) + dot(row_back[: 2 * f, :], rest)
        tall = jnp.concatenate(
            [
                jnp.concatenate([back[:f, 4 * f * k : 4 * f * (k + 1)], back[f:, 4 * f * k : 4 * f * (k + 1)]], axis=1)
                for k in range(quarters)
            ],
            axis=0,
        )
        m = quarters * f
        turned = dot(jnp.concatenate(split(tall), axis=0), lane_back[...])
        turned = (turned[:m, : 4 * f] + turned[:m, 4 * f :]) + turned[m:, : 4 * f]
        first, second = h_one * turned, h_two * turned
        real = jnp.zeros((f, 4 * f), jnp.float32)
        imag = jnp.zeros((f, 4 * f), jnp.float32)
        for k in range(quarters):
            real = real + first[k * f : (k + 1) * f] * portions[k]
            imag = imag + second[k * f : (k + 1) * f] * portions[k]
        real = real + pltpu.roll(real, 2 * f, 1)
        real = real + pltpu.roll(real, f, 1)
        imag = imag + pltpu.roll(imag, 2 * f, 1)
        imag = imag + pltpu.roll(imag, f, 1)
        return jnp.where(is_real, real, imag)

    def tails(packed):
        need(15)
        out = dot(jnp.concatenate(split(packed), axis=1), tail_tab[...])
        return jnp.concatenate([out[:, :n], out[:, n:]], axis=0)

    def band_tails(which, begin):
        packed = jnp.concatenate([unfolded(adj_in[to]) for to in which], axis=0)
        packed = jnp.concatenate(split(packed), axis=1)
        real = dot(packed, tail_tab[:, begin : begin + edge])
        imag = dot(packed, tail_tab[:, n + begin : n + begin + edge])
        return [
            jnp.concatenate([real[i * f : (i + 1) * f], imag[i * f : (i + 1) * f]], axis=0) for i in range(len(which))
        ]

    field = fields(*band_one)
    write_slope(field)
    packed = adjoint(field)
    adj[...] = folded(packed)
    start(plan["adj"] + plan["v", 1, 1] + plan["v", 0, 0] + plan["v", 0, 1])
    arrived(plan["vx"])
    for v, h in corners:
        @pl.when(both(cross[h], above[v]))
        def _(v=v, h=h):
            for i in range(2):
                c7[i, v, h] = md[i, bands[v], bands[h]] + q[i, v, h]
    start(plan["cf"])

    need(13, 14)
    turned = dot(row_flip[...], jnp.concatenate(split(packed), axis=0))
    mirrored = dot(jnp.concatenate(split(turned), axis=1), lane_flip[...])
    band = band_next - STEP_SIZE * (packed + mirrored)
    arrived(plan["spec"])
    incoming = spec_in[0]
    for to in range(1, 8):
        incoming = incoming + spec_in[to]
    band = band + unfolded(incoming)
    field = fields(jnp.where(is_real, band, pltpu.roll(band, f, 1)), jnp.where(is_real, pltpu.roll(band, 3 * f, 1), band))
    write_slope(field)
    arrived(plan["c3"])
    for v, h in corners:
        @pl.when(both(pair[h], above[v]))
        def _(v=v, h=h):
            c4[:, v, h] = c2[:, v, h] + c3[:, v, h]
            q[:, v, h, pl.ds((1 - h) * half, half), :] = c1[:, v, h] + c3[:, v, h]
    start(plan["c5"])


    last = adjoint(field)
    tail_last = tails(last)
    tail_own = tails(packed)
    arrived(plan["adj"])

    def joined(tail, from_left, from_right):
        return share_col * jnp.concatenate(
            [tail[:, :edge] + from_left, tail[:, edge:far], tail[:, far:] + from_right], axis=1
        )

    start(plan["pass"])
    sides = dot(
        jnp.concatenate(split(jnp.concatenate([unfolded(adj_in[2]), unfolded(adj_in[3])], axis=0)), axis=1), tail_tab[...]
    )
    arrived(plan["pass"])
    at_left, at_right = band_tails((0, 4, 6), far), band_tails((1, 5, 7), 0)
    ends = [jnp.concatenate([sides[i * f : (i + 1) * f, :n], sides[i * f : (i + 1) * f, n:]], axis=0) for i in range(2)]
    sum_own = joined(tail_own, at_left[0], at_right[0])
    sum_end = [joined(ends[i], at_left[1 + i], at_right[1 + i]) for i in range(2)]
    need(16)
    base = -0.125 * tail_own - STEP_SIZE * tail_last
    inner_m = stacked(base - 0.125 * sum_own)
    inner_d = stacked(STEP_SIZE * (sum_own - tail_own))
    for r in range(0, n, edge):
        rows = slice(r, r + edge)
        by = share_row(r)
        if by is None:
            grad_m = dot(grad_rows[rows, :], inner_m)
            grad_d = dot(grad_rows[rows, :], inner_d)
        else:
            other = sum_end[0] if r == 0 else sum_end[1]
            across = dot(grad_rows[far:, :] if r == 0 else grad_rows[:edge, :], stacked(by * other))
            grad_m = dot(grad_rows[rows, :], stacked(base - (0.125 * by) * sum_own)) - 0.125 * across
            grad_d = dot(grad_rows[rows, :], stacked(STEP_SIZE * (by * sum_own - tail_own))) + STEP_SIZE * across
        m, d = md[0, rows, :], md[1, rows, :]
        cover = scaled(share_col, by)
        mask_out[0, rows, :] = cover * (m + 0.625 * d) - 0.375 * d + grad_m
        dual_out[0, rows, :] = (1.5 * m + 0.75 * d) * (1.0 - cover) + grad_d

    def settle(rows, cols, by, m, d):
        mask_out[0, rows, cols] = mask_out[0, rows, cols] + by * (m + 0.625 * d)
        dual_out[0, rows, cols] = dual_out[0, rows, cols] - by * (1.5 * m + 0.75 * d)

    arrived(plan["c5"] + plan["hc"] + plan["vc"] + plan["cf"])
    for v, h in corners:
        @pl.when(both(pair[h], above[v]))
        def _(v=v, h=h):
            q[:, v, h, pl.ds(h * half, half), :] = c5[:, v, h] - md[:, piece(v, h), bands[h]]

        @pl.when(both(cross[h], above[v]))
        def _(v=v, h=h):
            q[:, v, h] = q[:, v, h] + q2[:, v, h]

        @pl.when(jnp.logical_or(beside[h], above[v]))
        def _(v=v, h=h):
            settle(bands[v], bands[h], share_end[v] * share_side[h], q[0, v, h], q[1, v, h])
    arrived(plan["h", 0] + plan["h", 1])
    for h in range(2):
        @pl.when(beside[h])
        def _(h=h):
            settle(middle, bands[h], share_side[h], hr[0, h], hr[1, h])
    arrived(plan["v", 1, 0] + plan["v", 1, 1])
    for v in range(2):
        @pl.when(above[v])
        def _(v=v):
            d = share_end[v] * vr[1, v]
            mask_out[0, bands[v], middle] = mask_out[0, bands[v], middle] + 0.625 * d
            dual_out[0, bands[v], middle] = dual_out[0, bands[v], middle] - 0.75 * d
    final = [("v", 0, 0), ("v", 0, 1)]
    for name, entries in plan.items():
        if name not in final:
            sent(entries)
    width = (far - edge) // 2
    for part, name in enumerate(final):
        arrived(plan[name])
        for v in range(2):
            @pl.when(above[v])
            def _(v=v, part=part):
                cols = pl.ds(edge + part * width, width)
                m = share_end[v] * vr[0, v, :, pl.ds(part * width, width)]
                mask_out[0, bands[v], cols] = mask_out[0, bands[v], cols] + m
                dual_out[0, bands[v], cols] = dual_out[0, bands[v], cols] - 1.5 * m
    for name in final:
        sent(plan[name])


def write_out(*refs):
    sources, targets, sem = refs[:2], refs[2:4], refs[4]
    copies = [pltpu.make_async_copy(a, b, sem.at[i]) for i, (a, b) in enumerate(zip(sources, targets))]
    for copy in copies:
        copy.start()
    for copy in copies:
        copy.wait()


def per_device(count, mask_init, dual_init, target, kernels, weights):
    n = mask_init.shape[-1]
    edge = INTERSECTION
    f = int(round(kernels.shape[-1] ** 0.5))
    tables = [jnp.asarray(t) for t in host_tables(n, f)]
    f32 = jnp.float32
    whole = pl.BlockSpec(memory_space=pltpu.VMEM)
    far_memory = pl.BlockSpec(memory_space=pltpu.HBM)
    arrays = (mask_init, dual_init, target, kernels, weights, *tables)
    tile = jax.ShapeDtypeStruct((1, n, n), f32)
    inner = n - 2 * edge
    half = edge // 2
    results = pl.pallas_call(
        functools.partial(body, n, f, edge, count),
        out_shape=(tile, tile),
        in_specs=[far_memory] * len(arrays),
        out_specs=(whole, whole),
        scratch_shapes=[
            pltpu.SMEM(a.shape, a.dtype) if i == 4 else pltpu.VMEM(a.shape, a.dtype)
            for i, a in enumerate(arrays) if i >= 2
        ]
        + [
            pltpu.VMEM((2, n, n), f32),
            pltpu.VMEM((kernels.shape[0] // 2 * f, 4 * f), f32),
            pltpu.SemaphoreType.DMA((len(arrays),)),
            pltpu.VMEM((2, 2, inner, edge), f32),
            pltpu.VMEM((2, 2, edge, inner), f32),
            pltpu.VMEM((2, 2, 2, edge, edge), f32),
            pltpu.VMEM((2, 2, 2, edge, edge), f32),
            pltpu.VMEM((2, 2, 2, edge, edge), f32),
        ]
        + [pltpu.VMEM((2, 2, 2, half, edge), f32)] * 5
        + [pltpu.VMEM((n, n), BF16)] * 4
        + [
            pltpu.VMEM((8, f // 2, 4 * f), f32),
            pltpu.VMEM((8, f // 2, 4 * f), f32),
            pltpu.VMEM((f // 2, 4 * f), f32),
            pltpu.VMEM((8, f // 2, 4 * f), f32),
            pltpu.SemaphoreType.REGULAR((8,)),
            pltpu.SemaphoreType.DMA((80,)),
            pltpu.SemaphoreType.DMA((80,)),
        ],
        compiler_params=pltpu.CompilerParams(
            collective_id=0, has_side_effects=True, vmem_limit_bytes=48 * 1024 * 1024
        ),
    )(*[pltpu.with_memory_space_constraint(a, pltpu.HBM) for a in arrays])
    return pl.pallas_call(
        write_out,
        out_shape=(tile, tile),
        in_specs=[pl.BlockSpec(memory_space=pl.ANY)] * 2,
        out_specs=[far_memory] * 2,
        scratch_shapes=[pltpu.SemaphoreType.DMA((2,))],
        compiler_params=pltpu.CompilerParams(vmem_limit_bytes=1 << 20),
    )(*results)


def solution(mesh):
    tile = P(("region", "ty"), None, None)
    return jax.shard_map(
        functools.partial(per_device, mesh.shape["ty"]),
        mesh=mesh,
        in_specs=(tile, tile, tile, P(), P()),
        out_specs=(tile, tile),
        check_vma=False,
    )
```
